128 devices in a mesh: head: 8 (over y_lo, z), key: 16 (over x, y_hi, core).
Axes of the slice: x: 4, y: 4 (y_hi: 2, y_lo: 2; y = y_hi * 2 + y_lo), z: 4, core: 2. Of those that a mesh axis runs over, the one named last changes fastest.
Arguments:
- q_latent: bfloat16 [128, 512, 576], P('head'), may hold values from -48 to 48
- k_latent: bfloat16 [16384, 576], P('key'), may hold values from -6 to 6
- q_index: bfloat16 [512, 8192], P('head'), may hold values from -8 to 8
- k_index: bfloat16 [16384, 128], P('key'), may hold values from -6 to 6
- head_weight: float32 [512, 64], P('head'), may hold values from -4 to 4, as said below
- loss_weight: float32 [512], P('head'), may hold values from 4096 to 32768
- query_pos: int32 [512], replicated, may hold values from 0 to 16383, as said below
- key_start: int32 [512], replicated, may hold values from 0 to 16383, as said below
Outputs:
- grad_query: float32 [512, 8192], P('head', 'key')
- grad_key: float32 [16384, 128], P('key')
- grad_weight: float32 [512, 64], P('head', 'key')
The draws below stay inside these ranges and needn't reach their ends.
Inputs may be any that keep to these rules, and one draw needn't show every extreme that they name: `head_weight`: indexer head weights, of either sign. Query t sees the keys key_start[t] to query_pos[t]; some query sits at position 16383 and some at 0. key_start[t] <= query_pos[t] for every query t; some query starts at 0 and some at 16383.
All inputs are finite; a program needn't handle non-finite values.
Results may differ from the reference program's by a relative error of at most 0.0028.
Values sent between devices are 32-bit elements; how exact they have to be, the bound alone decides.
No kernel may reach another device: no remote copies, remote signals or barrier semaphores. Data moves between devices by JAX's collectives and lax.ppermute only.
A program may use at most 128 MiB of HBM per device.

```python
import math
import jax
import jax.numpy as jnp
from jax import lax

H = 128
LAT = 576
QK_DIM = 192
IH = 64
ID = 128
Q_DEV = 64
QUERIES = 512
KEYS = 16384
N_HEAD = 8


def drawn_draw(subkey, out_shape, spread, limit):
    values = jax.random.normal(subkey, out_shape, jnp.float32) * spread
    return jnp.clip(values, -limit, limit)


def draw_everything(key):
    base_key = jax.random.fold_in(key, 7341)
    subkeys = jax.random.split(base_key, 9)
    shuffled = jax.random.permutation(subkeys[0], QUERIES)
    aligned = shuffled[:3]
    lowest_row = shuffled[3]
    last_row = shuffled[4]
    query_pos = jax.random.randint(subkeys[1], (QUERIES,), 0, KEYS).astype(jnp.int32)
    query_pos = query_pos.at[aligned].set(KEYS - 1)
    query_pos = query_pos.at[lowest_row].set(0)
    query_pos = query_pos.at[last_row].set(KEYS - 1)
    key_start = jax.random.randint(subkeys[2], (QUERIES,), 0, query_pos + 1).astype(jnp.int32)
    key_start = key_start.at[aligned].set(0)
    key_start = key_start.at[last_row].set(KEYS - 1)
    k_latent = drawn_draw(subkeys[4], (KEYS, LAT), 1.0, 6.0)
    q_latent = drawn_draw(subkeys[5], (H, QUERIES, LAT), 2.0, 12.0)
    k_index = drawn_draw(subkeys[6], (KEYS, ID), 1.0, 6.0)
    q_index = drawn_draw(subkeys[7], (QUERIES, IH, ID), 1.0, 6.0)
    head_weight = drawn_draw(subkeys[8], (QUERIES, IH), 0.7, 4.0)
    return (q_latent, k_latent, q_index.reshape(QUERIES, IH * ID), k_index, head_weight, query_pos, key_start)


def draw_q_latent(key, part):
    return draw_everything(key)[0].astype(jnp.bfloat16)


def draw_k_latent(key, part):
    return draw_everything(key)[1].astype(jnp.bfloat16)


def draw_q_index(key, part):
    return draw_everything(key)[2].astype(jnp.bfloat16)


def draw_k_index(key, part):
    return draw_everything(key)[3].astype(jnp.bfloat16)


def draw_head_weight(key, part):
    return draw_everything(key)[4]


def draw_query_pos(key, part):
    return draw_everything(key)[5]


def draw_key_start(key, part):
    return draw_everything(key)[6]


def level_of(own_key, extent, pieces, least, largest):
    loudness, own = 1.0, jax.random.fold_in(own_key, 6)
    for dim, blocks in pieces:
        heights = jnp.exp(jax.random.uniform(jax.random.fold_in(own, dim), (blocks,), jnp.float32, least / len(pieces), largest / len(pieces)))
        loudness = loudness * jnp.repeat(heights, extent[dim] // blocks).reshape([-1 if axis == dim else 1 for axis in range(len(extent))])
    return loudness


def setup_inputs(seed: int = 0) -> dict:
    key_of = jax.random.split(jax.random.key(seed), 9)
    q_latent = draw_q_latent(jax.random.fold_in(key_of[8], 71), 0)
    k_latent = draw_k_latent(jax.random.fold_in(key_of[8], 71), 0)
    q_index = draw_q_index(jax.random.fold_in(key_of[8], 71), 0)
    k_index = draw_k_index(jax.random.fold_in(key_of[8], 71), 0)
    head_weight = draw_head_weight(jax.random.fold_in(key_of[8], 71), 0)
    loss_weight = jnp.clip(jnp.exp(math.log(32768.0) - 2.0794415 * jax.random.uniform(key_of[5], (QUERIES,), jnp.float32) ** level_of(key_of[5], (QUERIES,), ((0, 8),), -0.2, 0.2)), 4096.0, 32768.0)
    query_pos = draw_query_pos(jax.random.fold_in(key_of[8], 71), 0)
    key_start = draw_key_start(jax.random.fold_in(key_of[8], 71), 0)
    return dict(q_latent=q_latent, k_latent=k_latent, q_index=q_index, k_index=k_index, head_weight=head_weight, loss_weight=loss_weight, query_pos=query_pos, key_start=key_start)


def reference(q_latent, k_latent, q_index, k_index, head_weight, loss_weight, query_pos, key_start):
    positions = jnp.arange(KEYS, dtype=jnp.int32)
    visible = (positions[None, :] >= key_start[:, None]) & (positions[None, :] <= query_pos[:, None])
    score_scale = 1.0 / math.sqrt(QK_DIM)

    def add_head(running, q_head):
        scores = jnp.dot(q_head, k_latent.T, preferred_element_type=jnp.float32) * score_scale
        masked = jnp.where(visible, scores, -jnp.inf)
        highest = lax.optimization_barrier(jnp.max(masked, axis=1, keepdims=True))
        exponents = jnp.where(visible, jnp.exp(scores - highest), 0.0)
        probabilities = exponents / lax.optimization_barrier(jnp.sum(exponents, axis=1, keepdims=True))
        return (running + probabilities, None)
    summed, _ = lax.scan(add_head, jnp.zeros((QUERIES, KEYS), jnp.float32), q_latent)
    target = summed / H
    index_scale = 1.0 / math.sqrt(ID)
    key_float = k_index.astype(jnp.float32)
    q_blocks = q_index.reshape(N_HEAD, Q_DEV, IH, ID)
    w_blocks = head_weight.reshape(N_HEAD, Q_DEV, IH)
    c_blocks = loss_weight.reshape(N_HEAD, Q_DEV)
    v_blocks = visible.reshape(N_HEAD, Q_DEV, KEYS)
    t_blocks = target.reshape(N_HEAD, Q_DEV, KEYS)

    def block_step(key_total, entries):
        q_block, w_block, c_block, seen_mask, t_block = entries
        q_float = q_block.astype(jnp.float32)
        head_dots = jnp.einsum('qjd,sd->qjs', q_float, key_float)
        rectified = jnp.maximum(head_dots, 0.0)
        index_scores = lax.optimization_barrier(jnp.sum(w_block[:, :, None] * rectified, axis=1)) * index_scale
        masked = jnp.where(seen_mask, index_scores, -jnp.inf)
        highest = lax.optimization_barrier(jnp.max(masked, axis=1, keepdims=True))
        exponents = jnp.where(seen_mask, jnp.exp(index_scores - highest), 0.0)
        index_probs = exponents / lax.optimization_barrier(jnp.sum(exponents, axis=1, keepdims=True))
        grad_scores = jnp.where(seen_mask, c_block[:, None] * (index_probs - t_block), 0.0)
        head_coef = w_block * index_scale
        head_grad = jnp.where(head_dots > 0.0, grad_scores[:, None, :] * head_coef[:, :, None], 0.0).astype(jnp.bfloat16)
        grad_float = head_grad.astype(jnp.float32)
        query_part = jnp.einsum('qjs,sd->qjd', grad_float, key_float)
        key_part = jnp.einsum('qjs,qjd->sd', grad_float, q_float)
        weight_part = lax.optimization_barrier(jnp.sum(grad_scores[:, None, :] * rectified, axis=2)) * index_scale
        return (key_total + key_part, (query_part, weight_part))
    grad_key, (query_parts, weight_parts) = lax.scan(block_step, jnp.zeros((KEYS, ID), jnp.float32), (q_blocks, w_blocks, c_blocks, v_blocks, t_blocks))
    grad_query = query_parts.reshape(QUERIES, IH * ID)
    grad_weight = weight_parts.reshape(QUERIES, IH)
    return (grad_query, grad_key, grad_weight)
```

```python
import functools
import math

import jax
import jax.numpy as jnp
from jax import lax
from jax.experimental import pallas as pl
from jax.experimental.pallas import tpu as pltpu
from jax.sharding import PartitionSpec as P

H = 128
QK_DIM = 192
LOG2E = 1.4426950408889634
LOW = -1e30
FLOOR = -1e29
CHUNK = 256
GROUP = 4


def eye_of(n):
    rows = lax.broadcasted_iota(jnp.int32, (n, n), 0)
    return rows == lax.broadcasted_iota(jnp.int32, (n, n), 1)


def as_column(row):
    n = row.shape[1]
    return jnp.sum(jnp.where(eye_of(n), row, jnp.zeros_like(row)), axis=1, keepdims=True)


def as_row(column):
    n = column.shape[0]
    return jnp.sum(jnp.where(eye_of(n), column, jnp.zeros_like(column)), axis=0, keepdims=True)


def joined_lse(a, b):
    high = jnp.maximum(a, b)
    return high + jnp.log2(jnp.exp2(a - high) + jnp.exp2(b - high))


def main_kernel(base_ref, kt_ref, qt_ref, start_ref, pos_ref, e_ref, m_ref, lse_ref, k_ref, bias_ref):
    h = pl.program_id(0)
    keys, queries = bias_ref.shape
    chunks = keys // CHUNK
    scale = LOG2E / math.sqrt(QK_DIM)

    @pl.when(h == 0)
    def _():
        k_ref[...] = kt_ref[...].T
        s = base_ref[0] + lax.broadcasted_iota(jnp.int32, (keys, queries), 0)
        seen = (s >= start_ref[...]) & (s <= pos_ref[...])
        bias_ref[...] = jnp.where(seen, 0.0, LOW)

    qt = qt_ref[0]
    highs, sums = [], []
    for c in range(chunks):
        here = pl.ds(c * CHUNK, CHUNK)
        s = jnp.dot(k_ref[here, :], qt, preferred_element_type=jnp.float32)
        s = s * scale + bias_ref[here, :]
        high = jnp.maximum(jnp.max(s, axis=0, keepdims=True), FLOOR)
        e = jnp.exp2(s - high).astype(jnp.bfloat16)
        e_ref[0, here, :] = e
        highs.append(high)
        sums.append(jnp.sum(e.astype(jnp.float32), axis=0, keepdims=True))
        m_ref[pl.ds(h * chunks + c, 1), :] = high
    top = functools.reduce(jnp.maximum, highs)
    total = sum(l * jnp.exp2(m - top) for l, m in zip(sums, highs))
    lse_ref[pl.ds(h, 1), :] = jnp.where(total > 0.0, top + jnp.log2(total), FLOOR)


def main_forward(base, kt, qt, start, pos):
    heads, lat, queries = qt.shape
    keys = kt.shape[1]
    chunks = keys // CHUNK
    return pl.pallas_call(
        main_kernel,
        grid=(heads,),
        in_specs=[
            pl.BlockSpec(memory_space=pltpu.SMEM),
            pl.BlockSpec((lat, keys), lambda h: (0, 0)),
            pl.BlockSpec((1, lat, queries), lambda h: (h, 0, 0)),
            pl.BlockSpec((1, queries), lambda h: (0, 0)),
            pl.BlockSpec((1, queries), lambda h: (0, 0)),
        ],
        out_specs=[
            pl.BlockSpec((1, keys, queries), lambda h: (h, 0, 0)),
            pl.BlockSpec((heads * chunks, queries), lambda h: (0, 0)),
            pl.BlockSpec((heads, queries), lambda h: (0, 0)),
        ],
        out_shape=[
            jax.ShapeDtypeStruct((heads, keys, queries), jnp.bfloat16),
            jax.ShapeDtypeStruct((heads * chunks, queries), jnp.float32),
            jax.ShapeDtypeStruct((heads, queries), jnp.float32),
        ],
        scratch_shapes=[
            pltpu.VMEM((keys, lat), jnp.bfloat16),
            pltpu.VMEM((keys, queries), jnp.float32),
        ],
        cost_estimate=pl.CostEstimate(
            flops=2 * heads * keys * queries * lat, bytes_accessed=26 << 20, transcendentals=heads * keys * queries
        ),
        name="main_forward",
    )(base, kt, qt, start, pos)


def index_kernel(base_ref, q_ref, kt_ref, w_ref, start_ref, pos_ref, s_ref, lse_ref):
    c = pl.program_id(0)
    rows, width = s_ref.shape[0], CHUNK
    heads = w_ref.shape[1]
    dim = kt_ref.shape[0]
    here = pl.ds(pl.multiple_of(c * width, width), width)
    kt = kt_ref[:, here]
    total = jnp.zeros((rows, width), jnp.float32)
    for j in range(heads):
        d = jnp.dot(q_ref[:, j * dim : (j + 1) * dim], kt, preferred_element_type=jnp.float32)
        total = total + w_ref[:, j : j + 1] * jnp.maximum(d, 0.0)
    s = base_ref[0] + c * width + lax.broadcasted_iota(jnp.int32, (rows, width), 1)
    seen = (s >= as_column(start_ref[...])) & (s <= as_column(pos_ref[...]))
    s_ref[:, here] = jnp.where(seen, total * (LOG2E / math.sqrt(dim)), LOW)

    @pl.when(c == pl.num_programs(0) - 1)
    def _():
        scores = s_ref[...]
        high = jnp.maximum(jnp.max(scores, axis=1, keepdims=True), FLOOR)
        total = jnp.sum(jnp.exp2(scores - high), axis=1, keepdims=True)
        lse_ref[...] = as_row(jnp.where(total > 0.0, high + jnp.log2(total), FLOOR))


def index_forward(base, q, kt, w, start, pos):
    rows, width = q.shape
    dim, keys = kt.shape
    heads = w.shape[1]
    whole = lambda *shape: pl.BlockSpec(shape, lambda c: (0,) * len(shape))
    return pl.pallas_call(
        index_kernel,
        grid=(keys // CHUNK,),
        in_specs=[
            pl.BlockSpec(memory_space=pltpu.SMEM),
            whole(rows, width),
            whole(dim, keys),
            whole(rows, heads),
            whole(1, rows),
            whole(1, rows),
        ],
        out_specs=[whole(rows, keys), whole(1, rows)],
        out_shape=[
            jax.ShapeDtypeStruct((rows, keys), jnp.float32),
            jax.ShapeDtypeStruct((1, rows), jnp.float32),
        ],
        cost_estimate=pl.CostEstimate(flops=2 * rows * width * keys, bytes_accessed=2 << 20, transcendentals=rows * keys),
        name="index_forward",
    )(base, q, kt, w, start, pos)


def sum_kernel(e_ref, m_ref, lse_ref, t_ref):
    c = pl.program_id(0)
    heads, width, queries = e_ref.shape
    chunks = pl.num_programs(0)
    owners, rows, _ = t_ref.shape
    lanes = 128
    weights = [jnp.exp2(m_ref[pl.ds(h * chunks + c, 1), :] - lse_ref[h : h + 1, :]) for h in range(heads)]
    for b in range(queries // lanes):
        cols = slice(b * lanes, (b + 1) * lanes)
        for r in range(width // 128):
            at = pl.ds(r * 128, 128)
            total = e_ref[0, at, cols].astype(jnp.float32) * weights[0][:, cols]
            for h in range(1, heads):
                total = total + e_ref[h, at, cols].astype(jnp.float32) * weights[h][:, cols]
            flipped = total.T
            for o in range(lanes // rows):
                t_ref[b * (lanes // rows) + o, :, at] = flipped[o * rows : (o + 1) * rows]


def weighted_sum(e, m, lse, owners):
    heads, keys, queries = e.shape
    chunks = keys // CHUNK
    rows = queries // owners
    return pl.pallas_call(
        sum_kernel,
        grid=(chunks,),
        in_specs=[
            pl.BlockSpec((heads, CHUNK, queries), lambda c: (0, c, 0)),
            pl.BlockSpec((heads * chunks, queries), lambda c: (0, 0)),
            pl.BlockSpec((heads, queries), lambda c: (0, 0)),
        ],
        out_specs=pl.BlockSpec((owners, rows, CHUNK), lambda c: (0, 0, c)),
        out_shape=jax.ShapeDtypeStruct((owners, rows, keys), jnp.float32),
        cost_estimate=pl.CostEstimate(
            flops=2 * heads * keys * queries, bytes_accessed=18 << 20, transcendentals=heads * chunks * queries
        ),
        name="weighted_sum",
    )(e, m, lse)


def back_kernel(t_ref, s_ref, lse_ref, c_ref, q_ref, k_ref, kt_ref, w_ref, gq_ref, gk_ref, g_ref, gkt_ref):
    i = pl.program_id(0)
    rows, keys = g_ref.shape
    dim = kt_ref.shape[0]
    index_scale = 1.0 / math.sqrt(dim)

    @pl.when(i == 0)
    def _():
        target = jnp.sum(t_ref[...], axis=0) * (1.0 / H)
        scores = s_ref[...]
        probs = jnp.exp2(scores - as_column(lse_ref[...]))
        g_ref[...] = jnp.where(scores > FLOOR, as_column(c_ref[...]) * (probs - target), 0.0)
        gkt_ref[...] = jnp.zeros_like(gkt_ref)

    q = jnp.concatenate([q_ref[:, j * dim : (j + 1) * dim] for j in range(GROUP)], axis=0)
    d = jnp.dot(q, kt_ref[...], preferred_element_type=jnp.float32)
    g = g_ref[...]
    parts, sums = [], []
    for j in range(GROUP):
        dots = d[j * rows : (j + 1) * rows]
        kept = jnp.where(dots > 0.0, g, 0.0)
        coef = w_ref[0][:, j : j + 1] * index_scale
        parts.append((kept * coef).astype(jnp.bfloat16))
        sums.append(as_row(jnp.sum(kept * dots, axis=1, keepdims=True)))
    head_grad = jnp.concatenate(parts, axis=0)
    gq = jnp.dot(head_grad, k_ref[...], preferred_element_type=jnp.float32)
    for j in range(GROUP):
        gq_ref[0, :rows, j * dim : (j + 1) * dim] = gq[j * rows : (j + 1) * rows]
        gq_ref[0, rows + j : rows + j + 1, :rows] = sums[j] * index_scale
    gkt_ref[...] += lax.dot_general(q, head_grad, (((0,), (0,)), ((), ())), preferred_element_type=jnp.float32)

    @pl.when(i == pl.num_programs(0) - 1)
    def _():
        gk_ref[...] = gkt_ref[...].T


def backward(t, s, lse, c, q, k, kt, w):
    rows, width = q.shape
    keys, dim = k.shape
    steps = width // (dim * GROUP)
    whole = lambda *shape: pl.BlockSpec(shape, lambda i: (0,) * len(shape))
    w = jnp.moveaxis(w.reshape(rows, steps, GROUP), 1, 0)
    return pl.pallas_call(
        back_kernel,
        grid=(steps,),
        in_specs=[
            whole(*t.shape),
            whole(rows, keys),
            whole(1, rows),
            whole(1, rows),
            pl.BlockSpec((rows, dim * GROUP), lambda i: (0, i)),
            whole(keys, dim),
            whole(dim, keys),
            pl.BlockSpec((1, rows, GROUP), lambda i: (i, 0, 0)),
        ],
        out_specs=[
            pl.BlockSpec((1, rows + 8, dim * GROUP), lambda i: (i, 0, 0)),
            whole(keys, dim),
        ],
        out_shape=[
            jax.ShapeDtypeStruct((steps, rows + 8, dim * GROUP), jnp.float32),
            jax.ShapeDtypeStruct((keys, dim), jnp.float32),
        ],
        scratch_shapes=[pltpu.VMEM((rows, keys), jnp.float32), pltpu.VMEM((dim, keys), jnp.float32)],
        cost_estimate=pl.CostEstimate(flops=6 * rows * width * keys, bytes_accessed=8 << 20, transcendentals=rows * keys),
        name="backward",
    )(t, s, lse, c, q, k, kt, w)


def joined_over_key(x):
    n = lax.axis_size("key")
    for mask in (1, 2):
        x = joined_lse(x, lax.ppermute(x, "key", [(i, i ^ mask) for i in range(n)]))
    others = [lax.ppermute(x, "key", [(i, (i + 4 * k) % n) for i in range(n)]) for k in (1, 2, 3)]
    high = functools.reduce(jnp.maximum, others, x)
    return high + jnp.log2(sum(jnp.exp2(y - high) for y in [x, *others]))


def shards(q_latent, k_latent, q_index, k_index, head_weight, loss_weight, query_pos, key_start):
    keys = k_latent.shape[0]
    rows = q_index.shape[0]
    owners = lax.axis_size("head")
    base = (lax.axis_index("key") * keys).astype(jnp.int32).reshape(1)
    own = lax.axis_index("head") * rows
    start, pos = key_start.reshape(1, -1), query_pos.reshape(1, -1)
    own_start = lax.dynamic_slice_in_dim(start, own, rows, axis=1)
    own_pos = lax.dynamic_slice_in_dim(pos, own, rows, axis=1)
    kt_index = k_index.T
    e, high, lse = main_forward(base, k_latent.T, jnp.swapaxes(q_latent, 1, 2), start, pos)
    scores, index_lse = index_forward(base, q_index, kt_index, head_weight, own_start, own_pos)
    lse = joined_over_key(lse)
    index_lse = joined_over_key(index_lse)
    partial = weighted_sum(e, high, lse, owners)
    blocks = lax.all_to_all(partial, "head", 0, 0, tiled=True)
    gq, gk = backward(blocks, scores, index_lse, loss_weight.reshape(1, -1), q_index, k_index, kt_index, head_weight)
    gq = jnp.sum(lax.all_to_all(gq, "key", 0, 0, tiled=True), axis=0)
    gk = gk.reshape(owners, -1, gk.shape[1])
    gk = jnp.sum(lax.all_to_all(gk, "head", 0, 0, tiled=True), axis=0)
    gk = lax.all_to_all(jnp.broadcast_to(gk, (owners, *gk.shape)), "head", 0, 0, tiled=True)
    return (gq[:rows], gk.reshape(keys, -1), gq[rows : rows + GROUP, :rows].T)


def solution(mesh):
    return jax.shard_map(
        shards,
        mesh=mesh,
        in_specs=(
            P("head", None, None),
            P("key", None),
            P("head", None),
            P("key", None),
            P("head", None),
            P("head"),
            P(),
            P(),
        ),
        out_specs=(P("head", "key"), P("key", None), P("head", "key")),
        check_vma=False,
    )
```

```python
import functools
import math

import jax
import jax.numpy as jnp
from jax import lax
from jax.experimental import pallas as pl
from jax.experimental.pallas import tpu as pltpu
from jax.sharding import PartitionSpec as P


H = 128
QK_DIM = 192
LOG2E = 1.4426950408889634
LOW = -1e30
FLOOR = -1e29
CHUNK = 256
GROUP = 4
PARTS = 2
MASKS = (1, 3, 4)
MASKS_OF = [(r >> 2) * MASKS[0] ^ (r >> 1 & 1) * MASKS[1] ^ (r & 1) * MASKS[2] for r in range(8)]


def eye_of(n):
    rows = lax.broadcasted_iota(jnp.int32, (n, n), 0)
    return rows == lax.broadcasted_iota(jnp.int32, (n, n), 1)


def as_column(row):
    n = row.shape[1]
    return jnp.sum(jnp.where(eye_of(n), row, jnp.zeros_like(row)), axis=1, keepdims=True)


def as_row(column):
    n = column.shape[0]
    return jnp.sum(jnp.where(eye_of(n), column, jnp.zeros_like(column)), axis=0, keepdims=True)


def main_kernel(base_ref, kt_ref, qt_ref, start_ref, pos_ref, e_ref, m_ref, lse_ref, k_ref, bias_ref, part_ref):
    h = pl.program_id(0)
    keys, queries = bias_ref.shape
    chunks = keys // CHUNK
    scale = LOG2E / math.sqrt(QK_DIM)

    @pl.when(h == 0)
    def _():
        k_ref[...] = kt_ref[...].T
        s = base_ref[0] + lax.broadcasted_iota(jnp.int32, (keys, queries), 0)
        seen = (s >= start_ref[...]) & (s <= pos_ref[...])
        bias_ref[...] = jnp.where(seen, 0.0, LOW)

    qt = qt_ref[0]
    highs, sums = [], []
    for c in range(chunks):
        here = pl.ds(c * CHUNK, CHUNK)
        s = jnp.dot(k_ref[here, :], qt, preferred_element_type=jnp.float32)
        s = s * scale + bias_ref[here, :]
        high = jnp.maximum(jnp.max(s, axis=0, keepdims=True), FLOOR)
        e = jnp.exp2(s - high)
        e_ref[0, here, :] = e.astype(jnp.bfloat16)
        highs.append(high)
        sums.append(jnp.sum(e, axis=0, keepdims=True))
        m_ref[pl.ds(h * chunks + c, 1), :] = high
    top = functools.reduce(jnp.maximum, highs)
    total = sum(l * jnp.exp2(m - top) for l, m in zip(sums, highs))
    part_ref[pl.ds(h, 1), :] = jnp.where(total > 0.0, top + jnp.log2(total), FLOOR)

    @pl.when(h == pl.num_programs(0) - 1)
    def _():
        for i in range(lse_ref.shape[0]):
            lse_ref[i] = part_ref[...]


def main_forward(base, kt, qt, start, pos, peers):
    heads, lat, queries = qt.shape
    keys = kt.shape[1]
    chunks = keys // CHUNK
    return pl.pallas_call(
        main_kernel,
        grid=(heads,),
        in_specs=[
            pl.BlockSpec(memory_space=pltpu.SMEM),
            pl.BlockSpec((lat, keys), lambda h: (0, 0)),
            pl.BlockSpec((1, lat, queries), lambda h: (h, 0, 0)),
            pl.BlockSpec((1, queries), lambda h: (0, 0)),
            pl.BlockSpec((1, queries), lambda h: (0, 0)),
        ],
        out_specs=[
            pl.BlockSpec((1, keys, queries), lambda h: (h, 0, 0)),
            pl.BlockSpec((heads * chunks, queries), lambda h: (0, 0)),
            pl.BlockSpec((peers, heads, queries), lambda h: (0, 0, 0)),
        ],
        out_shape=[
            jax.ShapeDtypeStruct((heads, keys, queries), jnp.bfloat16),
            jax.ShapeDtypeStruct((heads * chunks, queries), jnp.float32),
            jax.ShapeDtypeStruct((peers, heads, queries), jnp.float32),
        ],
        scratch_shapes=[
            pltpu.VMEM((keys, lat), jnp.bfloat16),
            pltpu.VMEM((keys, queries), jnp.float32),
            pltpu.VMEM((heads, queries), jnp.float32),
        ],
        cost_estimate=pl.CostEstimate(
            flops=2 * heads * keys * queries * lat, bytes_accessed=26 << 20, transcendentals=heads * keys * queries
        ),
        name="main_forward",
    )(base, kt, qt, start, pos)


def index_kernel(base_ref, q_ref, kt_ref, w_ref, start_ref, pos_ref, s_ref, lse_ref):
    c = pl.program_id(0)
    rows, width = s_ref.shape[0], CHUNK
    heads = w_ref.shape[1]
    dim = kt_ref.shape[0]
    here = pl.ds(pl.multiple_of(c * width, width), width)
    kt = kt_ref[:, here]
    total = jnp.zeros((rows, width), jnp.float32)
    for j in range(heads):
        d = jnp.dot(q_ref[:, j * dim : (j + 1) * dim], kt, preferred_element_type=jnp.float32)
        total = total + w_ref[:, j : j + 1] * jnp.maximum(d, 0.0)
    s = base_ref[0] + c * width + lax.broadcasted_iota(jnp.int32, (rows, width), 1)
    seen = (s >= as_column(start_ref[...])) & (s <= as_column(pos_ref[...]))
    s_ref[:, here] = jnp.where(seen, total * (LOG2E / math.sqrt(dim)), LOW)

    @pl.when(c == pl.num_programs(0) - 1)
    def _():
        scores = s_ref[...]
        high = jnp.maximum(jnp.max(scores, axis=1, keepdims=True), FLOOR)
        total = jnp.sum(jnp.exp2(scores - high), axis=1, keepdims=True)
        lse_ref[...] = as_row(jnp.where(total > 0.0, high + jnp.log2(total), FLOOR))


def index_forward(base, q, kt, w, start, pos):
    rows, width = q.shape
    dim, keys = kt.shape
    heads = w.shape[1]
    whole = lambda *shape: pl.BlockSpec(shape, lambda c: (0,) * len(shape))
    return pl.pallas_call(
        index_kernel,
        grid=(keys // CHUNK,),
        in_specs=[
            pl.BlockSpec(memory_space=pltpu.SMEM),
            whole(rows, width),
            whole(dim, keys),
            whole(rows, heads),
            whole(1, rows),
            whole(1, rows),
        ],
        out_specs=[whole(rows, keys), whole(1, rows)],
        out_shape=[
            jax.ShapeDtypeStruct((rows, keys), jnp.float32),
            jax.ShapeDtypeStruct((1, rows), jnp.float32),
        ],
        cost_estimate=pl.CostEstimate(flops=2 * rows * width * keys, bytes_accessed=2 << 20, transcendentals=rows * keys),
        name="index_forward",
    )(base, q, kt, w, start, pos)


def sum_kernel(first, e_ref, m_ref, stats_ref, t_ref, lse_ref):
    c = pl.program_id(0)
    heads, width, queries = e_ref.shape
    rows = t_ref.shape[1]
    chunks = m_ref.shape[0] // heads
    lanes = 128

    @pl.when(c == 0)
    def _():
        stats = [stats_ref[i] for i in range(stats_ref.shape[0])]
        high = functools.reduce(jnp.maximum, stats)
        lse_ref[...] = high + jnp.log2(sum(jnp.exp2(x - high) for x in stats))

    chunk = (first + c) * width // CHUNK
    weights = [jnp.exp2(m_ref[pl.ds(h * chunks + chunk, 1), :] - lse_ref[h : h + 1, :]) for h in range(heads)]
    for b in range(queries // lanes):
        cols = slice(b * lanes, (b + 1) * lanes)
        total = e_ref[0, :, cols].astype(jnp.float32) * weights[0][:, cols]
        for h in range(1, heads):
            total = total + e_ref[h, :, cols].astype(jnp.float32) * weights[h][:, cols]
        flipped = total.T
        for o in range(lanes // rows):
            t_ref[b * (lanes // rows) + o] = flipped[o * rows : (o + 1) * rows]


def weighted_sum(e, m, stats, owners, part):
    heads, keys, queries = e.shape
    rows = queries // owners
    width = 128
    steps = keys // PARTS // width
    first = part * steps
    return pl.pallas_call(
        functools.partial(sum_kernel, first),
        grid=(steps,),
        in_specs=[
            pl.BlockSpec((heads, width, queries), lambda c: (0, first + c, 0)),
            pl.BlockSpec(m.shape, lambda c: (0, 0)),
            pl.BlockSpec(stats.shape, lambda c: (0, 0, 0)),
        ],
        out_specs=pl.BlockSpec((owners, rows, width), lambda c: (0, 0, c)),
        out_shape=jax.ShapeDtypeStruct((owners, rows, keys // PARTS), jnp.float32),
        scratch_shapes=[pltpu.VMEM((heads, queries), jnp.float32)],
        cost_estimate=pl.CostEstimate(
            flops=2 * heads * keys * queries // PARTS, bytes_accessed=18 << 19, transcendentals=heads * queries
        ),
    )(e, m, stats)


def back_kernel(has_former, has_keys, splits, *refs):
    place_ref, t_ref, s_ref, stats_ref, c_ref, q_ref, k_ref, kt_ref, w_ref, *refs = refs
    if has_former:
        former_ref, *refs = refs
    if has_keys:
        fk_ref, *refs = refs
    gq_ref, gk_ref, g_ref, gkt_ref, turned_ref = refs
    i = pl.program_id(0)
    rows, _ = g_ref.shape
    dim = kt_ref.shape[0]
    index_scale = 1.0 / math.sqrt(dim)

    @pl.when(i == 0)
    def _():
        target = jnp.sum(t_ref[...], axis=0) * (1.0 / H)
        scores = s_ref[...]
        probs = jnp.exp2(scores - as_column(stats_ref[...]))
        g_ref[...] = jnp.where(scores > FLOOR, as_column(c_ref[...]) * (probs - target), 0.0)
        gkt_ref[...] = jnp.zeros_like(gkt_ref)

    q = jnp.concatenate([q_ref[:, j * dim : (j + 1) * dim] for j in range(GROUP)], axis=0)
    d = jnp.dot(q, kt_ref[...], preferred_element_type=jnp.float32)
    g = g_ref[...]
    parts, sums = [], []
    for j in range(GROUP):
        dots = d[j * rows : (j + 1) * rows]
        kept = jnp.where(dots > 0.0, g, 0.0)
        coef = w_ref[0][:, j : j + 1] * index_scale
        parts.append((kept * coef).astype(jnp.bfloat16))
        sums.append(as_row(jnp.sum(kept * dots, axis=1, keepdims=True)))
    head_grad = jnp.concatenate(parts, axis=0)
    gq = jnp.dot(head_grad, k_ref[...], preferred_element_type=jnp.float32)
    pad = jnp.zeros((1, dim * GROUP - rows), jnp.float32)
    low = jnp.concatenate([jnp.concatenate([x * index_scale, pad], axis=1) for x in sums], axis=0)
    low = jnp.concatenate([low, jnp.zeros((8 - GROUP, dim * GROUP), jnp.float32)], axis=0)
    gq = jnp.concatenate([gq[j * rows : (j + 1) * rows] for j in range(GROUP)], axis=1)
    if has_former:
        gq, low = gq + former_ref[0, :rows], low + former_ref[0, rows:]
    gq_ref[0, :rows] = gq
    gq_ref[0, rows:] = low
    gkt_ref[...] += lax.dot_general(q, head_grad, (((0,), (0,)), ((), ())), preferred_element_type=jnp.float32)

    @pl.when(i == pl.num_programs(0) - 1)
    def _():
        gk = gkt_ref[...].T.reshape(turned_ref.shape)
        if has_keys:
            gk = gk + fk_ref[...]
        if splits:
            turned_ref[...] = gk
            for r in range(len(MASKS_OF)):
                gk_ref[r] = turned_ref[place_ref[1] ^ MASKS_OF[r]]
        else:
            gk_ref[...] = gk


def backward(place, t, s, stats, c, q, k, kt, w, part, dests, owners, former=None, gk=None):
    rows, width = q.shape
    keys, dim = k.shape
    keys = keys // PARTS
    steps = width // (dim * GROUP)
    count = steps if dests is None else steps // 2
    if dests is None:
        dest = lambda i, place: i
    elif dests == "far":
        dest = lambda i, place: 2 * i + 1 - place[0]
    else:
        dest = lambda i, place: 2 * i + place[0]
    whole = lambda *shape: pl.BlockSpec(shape, lambda i, place: (0,) * len(shape))
    w = jnp.moveaxis(w.reshape(rows, steps, GROUP), 1, 0)
    block = (1, rows + 8, dim * GROUP)
    in_specs = [
        whole(*t.shape),
        pl.BlockSpec((rows, keys), lambda i, place: (0, part)),
        whole(*stats.shape),
        whole(1, rows),
        pl.BlockSpec((rows, dim * GROUP), lambda i, place: (0, dest(i, place))),
        pl.BlockSpec((keys, dim), lambda i, place: (part, 0)),
        pl.BlockSpec((dim, keys), lambda i, place: (0, part)),
        pl.BlockSpec((1, rows, GROUP), lambda i, place: (dest(i, place), 0, 0)),
    ]
    args = [t, s, stats, c, q, k, kt, w]
    if former is not None:
        in_specs.append(pl.BlockSpec(block, lambda i, place: (dest(i, place), 0, 0)))
        args.append(former)
    shape = (owners, keys // owners, dim)
    if gk is not None:
        in_specs.append(whole(*shape))
        args.append(gk)
    return pl.pallas_call(
        functools.partial(back_kernel, former is not None, gk is not None, dests != "far"),
        grid_spec=pltpu.PrefetchScalarGridSpec(
            num_scalar_prefetch=1,
            grid=(count,),
            in_specs=in_specs,
            out_specs=[pl.BlockSpec(block, lambda i, place: (i, 0, 0)), whole(*shape)],
            scratch_shapes=[
                pltpu.VMEM((rows, keys), jnp.float32),
                pltpu.VMEM((dim, keys), jnp.float32),
                pltpu.VMEM(shape, jnp.float32),
            ],
        ),
        out_shape=[
            jax.ShapeDtypeStruct((count, rows + 8, dim * GROUP), jnp.float32),
            jax.ShapeDtypeStruct(shape, jnp.float32),
        ],
        cost_estimate=pl.CostEstimate(
            flops=6 * rows * width * keys * count // steps, bytes_accessed=4 << 20, transcendentals=rows * keys
        ),
    )(place, *args)


def end_kernel(x_ref, gq_ref, gw_ref):
    rows = gq_ref.shape[0]
    total = jnp.sum(x_ref[...], axis=0)
    gq_ref[...] = total[:rows]
    gw_ref[...] = total[rows : rows + GROUP, :rows]


def ended(x):
    _, rows, width = x.shape
    rows -= 8
    return pl.pallas_call(
        end_kernel,
        out_shape=[
            jax.ShapeDtypeStruct((rows, width), jnp.float32),
            jax.ShapeDtypeStruct((GROUP, rows), jnp.float32),
        ],
        name="end",
    )(x)


def join_kernel(place_ref, near_ref, far_ref, out_ref):
    half = near_ref.shape[0]
    parts, _, rows, _ = out_ref.shape
    for n, ref in enumerate((near_ref, far_ref)):
        for r in range(half):
            for p in range(parts):
                out_ref[p, place_ref[1] ^ MASKS_OF[n * half + r]] = ref[r, p * rows : (p + 1) * rows]


def joined(place, near, far):
    half, rows, dim = near.shape
    vmem = pl.BlockSpec(memory_space=pltpu.VMEM)
    return pl.pallas_call(
        join_kernel,
        in_specs=[pl.BlockSpec(memory_space=pltpu.SMEM), vmem, vmem],
        out_specs=vmem,
        out_shape=jax.ShapeDtypeStruct((PARTS, 2 * half, rows // PARTS, dim), jnp.float32),
        name="join",
    )(place, near, far)


def exchanged(x, axis, groups=None):
    return lax.all_to_all(x, axis, 0, 0, axis_index_groups=groups, tiled=True)


def flipped(x, axis, mask):
    return lax.ppermute(x, axis, [(i, i ^ mask) for i in range(lax.axis_size(axis))])


def summed(x):
    for mask in MASKS:
        half = x.shape[0] // 2
        x = x[:half] + flipped(x[half:], "head", mask)
    return x


def gathered(x):
    for mask in MASKS[:0:-1]:
        x = jnp.concatenate([x, flipped(x, "head", mask)], axis=0)
    return x, flipped(x, "head", MASKS[0])


def joined_lse(a, b):
    high = jnp.maximum(a, b)
    return high + jnp.log2(jnp.exp2(a - high) + jnp.exp2(b - high))


def joined_over_key(x):
    n = lax.axis_size("key")
    for mask in (1, 2):
        x = joined_lse(x, flipped(x, "key", mask))
    others = [lax.ppermute(x, "key", [(i, (i + 4 * k) % n) for i in range(n)]) for k in (1, 2, 3)]
    high = functools.reduce(jnp.maximum, others, x)
    return high + jnp.log2(sum(jnp.exp2(y - high) for y in [x, *others]))


def shards(q_latent, k_latent, q_index, k_index, head_weight, loss_weight, query_pos, key_start):
    keys = k_latent.shape[0]
    rows = q_index.shape[0]
    owners, peers = lax.axis_size("head"), lax.axis_size("key")
    at_key, at_head = (lax.axis_index(name).astype(jnp.int32) for name in ("key", "head"))
    base, place = (at_key * keys).reshape(1), jnp.stack([at_key % 2, at_head])
    own = at_head * rows
    start, pos = key_start.reshape(1, -1), query_pos.reshape(1, -1)
    own_start = lax.dynamic_slice_in_dim(start, own, rows, axis=1)
    own_pos = lax.dynamic_slice_in_dim(pos, own, rows, axis=1)
    kt_index = k_index.T
    e, high, lse = main_forward(base, k_latent.T, jnp.swapaxes(q_latent, 1, 2), start, pos, peers)
    stats = exchanged(lse, "key")
    scores, index_lse = index_forward(base, q_index, kt_index, head_weight, own_start, own_pos)
    targets = []
    for part in range(PARTS):
        partial = weighted_sum(e, high, stats, owners, part)
        targets.append(exchanged(partial, "head"))
    index_stats = joined_over_key(index_lse)

    def back(part, dests, *former):
        fixed = (scores, index_stats, loss_weight.reshape(1, -1), q_index, k_index, kt_index, head_weight)
        return backward(place, targets[part], *fixed, part, dests, owners, *former)

    gq_0, gk_0 = back(0, None)
    gk_0 = summed(gk_0)
    targets[1], gk_0 = lax.optimization_barrier((targets[1], gk_0))
    far, gk_1 = back(1, "far", gq_0)
    moved = flipped(far, "key", 1)
    near, gk_1 = back(1, "near", gq_0, gk_1)
    groups = [list(range(c, peers, 2)) for c in (0, 1)]
    gq = exchanged(near + moved, "key", groups)
    gk_1 = summed(gk_1)
    gk = joined(place, *gathered(jnp.concatenate([gk_0, gk_1], axis=1))).reshape(keys, -1)
    gq, gw = ended(gq)
    return (gq, gk, gw.T)


def solution(mesh):
    return jax.shard_map(
        shards,
        mesh=mesh,
        in_specs=(
            P("head", None, None),
            P("key", None),
            P("head", None),
            P("key", None),
            P("head", None),
            P("head"),
            P(),
            P(),
        ),
        out_specs=(P("head", "key"), P("key", None), P("head", "key")),
        check_vma=False,
    )
```

```python
import functools
import math

import jax
import jax.numpy as jnp
from jax import lax
from jax.experimental import pallas as pl
from jax.experimental.pallas import tpu as pltpu
from jax.sharding import PartitionSpec as P


H = 128
QK_DIM = 192
LOG2E = 1.4426950408889634
LOW = -1e30
FLOOR = -1e29
CHUNK = 256
GROUP = 4
PARTS = 2
ROUNDS = 4
VMEM = 48 << 20


def eye_of(n):
    rows = lax.broadcasted_iota(jnp.int32, (n, n), 0)
    return rows == lax.broadcasted_iota(jnp.int32, (n, n), 1)


def as_column(row):
    n = row.shape[1]
    return jnp.sum(jnp.where(eye_of(n), row, jnp.zeros_like(row)), axis=1, keepdims=True)


def as_row(column):
    n = column.shape[0]
    return jnp.sum(jnp.where(eye_of(n), column, jnp.zeros_like(column)), axis=0, keepdims=True)


def main_kernel(base_ref, kt_ref, qt_ref, start_ref, pos_ref, e_ref, m_ref, lse_ref, k_ref, bias_ref, part_ref):
    h = pl.program_id(0)
    keys, queries = bias_ref.shape
    chunks = keys // CHUNK
    scale = LOG2E / math.sqrt(QK_DIM)

    @pl.when(h == 0)
    def _():
        k_ref[...] = kt_ref[...].T
        s = base_ref[0] + lax.broadcasted_iota(jnp.int32, (keys, queries), 0)
        seen = (s >= start_ref[...]) & (s <= pos_ref[...])
        bias_ref[...] = jnp.where(seen, 0.0, LOW)

    qt = qt_ref[0]
    highs, sums = [], []
    for c in range(chunks):
        here = pl.ds(c * CHUNK, CHUNK)
        s = jnp.dot(k_ref[here, :], qt, preferred_element_type=jnp.float32)
        s = s * scale + bias_ref[here, :]
        high = jnp.maximum(jnp.max(s, axis=0, keepdims=True), FLOOR)
        e = jnp.exp2(s - high)
        e_ref[0, here, :] = e.astype(jnp.bfloat16)
        highs.append(high)
        sums.append(jnp.sum(e, axis=0, keepdims=True))
        m_ref[pl.ds(h * chunks + c, 1), :] = high
    top = functools.reduce(jnp.maximum, highs)
    total = sum(l * jnp.exp2(m - top) for l, m in zip(sums, highs))
    part_ref[pl.ds(h, 1), :] = jnp.where(total > 0.0, top + jnp.log2(total), FLOOR)

    @pl.when(h == pl.num_programs(0) - 1)
    def _():
        for i in range(lse_ref.shape[0]):
            lse_ref[i] = part_ref[...]


def main_forward(base, kt, qt, start, pos, peers):
    heads, lat, queries = qt.shape
    keys = kt.shape[1]
    chunks = keys // CHUNK
    return pl.pallas_call(
        main_kernel,
        grid=(heads,),
        in_specs=[
            pl.BlockSpec(memory_space=pltpu.SMEM),
            pl.BlockSpec((lat, keys), lambda h: (0, 0)),
            pl.BlockSpec((1, lat, queries), lambda h: (h, 0, 0)),
            pl.BlockSpec((1, queries), lambda h: (0, 0)),
            pl.BlockSpec((1, queries), lambda h: (0, 0)),
        ],
        out_specs=[
            pl.BlockSpec((1, keys, queries), lambda h: (h, 0, 0)),
            pl.BlockSpec((heads * chunks, queries), lambda h: (0, 0)),
            pl.BlockSpec((peers, heads, queries), lambda h: (0, 0, 0)),
        ],
        out_shape=[
            jax.ShapeDtypeStruct((heads, keys, queries), jnp.bfloat16),
            jax.ShapeDtypeStruct((heads * chunks, queries), jnp.float32),
            jax.ShapeDtypeStruct((peers, heads, queries), jnp.float32),
        ],
        scratch_shapes=[
            pltpu.VMEM((keys, lat), jnp.bfloat16),
            pltpu.VMEM((keys, queries), jnp.float32),
            pltpu.VMEM((heads, queries), jnp.float32),
        ],
        cost_estimate=pl.CostEstimate(
            flops=2 * heads * keys * queries * lat, bytes_accessed=26 << 20, transcendentals=heads * keys * queries
        ),
        name="main_forward",
    )(base, kt, qt, start, pos)


def index_kernel(base_ref, q_ref, kt_ref, w_ref, start_ref, pos_ref, s_ref, lse_ref):
    c = pl.program_id(0)
    rows, width = s_ref.shape[0], CHUNK
    heads = w_ref.shape[1]
    dim = kt_ref.shape[0]
    here = pl.ds(pl.multiple_of(c * width, width), width)
    kt = kt_ref[:, here]
    total = jnp.zeros((rows, width), jnp.float32)
    for j in range(heads):
        d = jnp.dot(q_ref[:, j * dim : (j + 1) * dim], kt, preferred_element_type=jnp.float32)
        total = total + w_ref[:, j : j + 1] * jnp.maximum(d, 0.0)
    s = base_ref[0] + c * width + lax.broadcasted_iota(jnp.int32, (rows, width), 1)
    seen = (s >= as_column(start_ref[...])) & (s <= as_column(pos_ref[...]))
    s_ref[:, here] = jnp.where(seen, total * (LOG2E / math.sqrt(dim)), LOW)

    @pl.when(c == pl.num_programs(0) - 1)
    def _():
        scores = s_ref[...]
        high = jnp.maximum(jnp.max(scores, axis=1, keepdims=True), FLOOR)
        total = jnp.sum(jnp.exp2(scores - high), axis=1, keepdims=True)
        row = as_row(jnp.where(total > 0.0, high + jnp.log2(total), FLOOR))
        row = jnp.concatenate([row, jnp.zeros_like(row)], axis=1)
        lse_ref[...] = jnp.broadcast_to(row[None], lse_ref.shape)


def index_forward(base, q, kt, w, start, pos, peers):
    rows, width = q.shape
    dim, keys = kt.shape
    heads = w.shape[1]
    whole = lambda *shape: pl.BlockSpec(shape, lambda c: (0,) * len(shape))
    return pl.pallas_call(
        index_kernel,
        grid=(keys // CHUNK,),
        in_specs=[
            pl.BlockSpec(memory_space=pltpu.SMEM),
            whole(rows, width),
            whole(dim, keys),
            whole(rows, heads),
            whole(1, rows),
            whole(1, rows),
        ],
        out_specs=[whole(rows, keys), whole(peers, 8, 2 * rows)],
        out_shape=[
            jax.ShapeDtypeStruct((rows, keys), jnp.float32),
            jax.ShapeDtypeStruct((peers, 8, 2 * rows), jnp.float32),
        ],
        cost_estimate=pl.CostEstimate(flops=2 * rows * width * keys, bytes_accessed=2 << 20, transcendentals=rows * keys),
        name="index_forward",
    )(base, q, kt, w, start, pos)


def sum_kernel(first, e_ref, m_ref, stats_ref, t_ref, lse_ref):
    c = pl.program_id(0)
    heads, width, queries = e_ref.shape
    rows = t_ref.shape[1]
    chunks = m_ref.shape[0] // heads
    lanes = 128

    @pl.when(c == 0)
    def _():
        stats = [stats_ref[i] for i in range(stats_ref.shape[0])]
        high = functools.reduce(jnp.maximum, stats)
        lse_ref[...] = high + jnp.log2(sum(jnp.exp2(x - high) for x in stats))

    chunk = (first + c) * width // CHUNK
    weights = [jnp.exp2(m_ref[pl.ds(h * chunks + chunk, 1), :] - lse_ref[h : h + 1, :]) for h in range(heads)]
    for b in range(queries // lanes):
        cols = slice(b * lanes, (b + 1) * lanes)
        total = e_ref[0, :, cols].astype(jnp.float32) * weights[0][:, cols]
        for h in range(1, heads):
            total = total + e_ref[h, :, cols].astype(jnp.float32) * weights[h][:, cols]
        flipped = total.T
        for o in range(lanes // rows):
            t_ref[b * (lanes // rows) + o] = flipped[o * rows : (o + 1) * rows]


def weighted_sum(e, m, stats, owners, part):
    heads, keys, queries = e.shape
    rows = queries // owners
    width = 128
    steps = keys // PARTS // width
    first = part * steps
    return pl.pallas_call(
        functools.partial(sum_kernel, first),
        grid=(steps,),
        in_specs=[
            pl.BlockSpec((heads, width, queries), lambda c: (0, first + c, 0)),
            pl.BlockSpec(m.shape, lambda c: (0, 0)),
            pl.BlockSpec(stats.shape, lambda c: (0, 0, 0)),
        ],
        out_specs=pl.BlockSpec((owners, rows, width), lambda c: (0, 0, c)),
        out_shape=jax.ShapeDtypeStruct((owners, rows, keys // PARTS), jnp.float32),
        scratch_shapes=[pltpu.VMEM((heads, queries), jnp.float32)],
        compiler_params=pltpu.CompilerParams(vmem_limit_bytes=VMEM),
        cost_estimate=pl.CostEstimate(
            flops=2 * heads * keys * queries // PARTS, bytes_accessed=18 << 19, transcendentals=heads * queries
        ),
    )(e, m, stats)


def back_kernel(last, place_ref, t_ref, s_ref, stats_ref, c_ref, q_ref, k_ref, kt_ref, w_ref, *refs):
    if last:
        former_ref, fk_ref, far_ref, near_ref, *gk_refs, g_ref, gkt_ref, turned_ref = refs
    else:
        gq_ref, gk_ref, g_ref, gkt_ref = refs
    i, steps = pl.program_id(0), pl.num_programs(0)
    rows, _ = g_ref.shape
    dim = kt_ref.shape[0]
    width = dim * GROUP
    index_scale = 1.0 / math.sqrt(dim)
    dest = far_first(i, steps, place_ref) if last else i

    @pl.when(i == 0)
    def _():
        target = jnp.sum(t_ref[...], axis=0) * (1.0 / H)
        scores = s_ref[...]
        stats = [stats_ref[n, 0:1, :rows] for n in range(stats_ref.shape[0])]
        high = functools.reduce(jnp.maximum, stats)
        lse = high + jnp.log2(sum(jnp.exp2(x - high) for x in stats))
        probs = jnp.exp2(scores - as_column(lse))
        g_ref[...] = jnp.where(scores > FLOOR, as_column(c_ref[...]) * (probs - target), 0.0)
        gkt_ref[...] = jnp.zeros_like(gkt_ref)

    q = q_ref[:, pl.ds(pl.multiple_of(dest * width, width), width)]
    q = jnp.concatenate([q[:, j * dim : (j + 1) * dim] for j in range(GROUP)], axis=0)
    d = jnp.dot(q, kt_ref[...], preferred_element_type=jnp.float32)
    g = g_ref[...]
    w = w_ref[dest]
    parts, sums = [], []
    for j in range(GROUP):
        dots = d[j * rows : (j + 1) * rows]
        kept = jnp.where(dots > 0.0, g, 0.0)
        parts.append((kept * (w[:, j : j + 1] * index_scale)).astype(jnp.bfloat16))
        sums.append(as_row(jnp.sum(kept * dots, axis=1, keepdims=True)))
    head_grad = jnp.concatenate(parts, axis=0)
    gq = jnp.dot(head_grad, k_ref[...], preferred_element_type=jnp.float32)
    pad = jnp.zeros((1, width - rows), jnp.float32)
    low = [jnp.concatenate([x * index_scale, pad], axis=1) for x in sums]
    low = jnp.concatenate([*low, jnp.zeros((8 - GROUP, width), jnp.float32)], axis=0)
    gq = jnp.concatenate([gq[j * rows : (j + 1) * rows] for j in range(GROUP)], axis=1)
    gq = jnp.concatenate([gq, low], axis=0)
    gkt_ref[...] += lax.dot_general(q, head_grad, (((0,), (0,)), ((), ())), preferred_element_type=jnp.float32)
    if not last:
        gq_ref[0] = gq

        @pl.when(i == steps - 1)
        def _():
            gk_ref[...] = gkt_ref[...].T.reshape(gk_ref.shape)

        return
    gq = gq + former_ref[0]

    @pl.when(i < steps // 2)
    def _():
        far_ref[0] = gq

    @pl.when(i >= steps // 2)
    def _():
        near_ref[0] = gq

    @pl.when(i == steps - 1)
    def _():
        turned_ref[...] = gkt_ref[...].T.reshape(turned_ref.shape)
        rounds, lines = len(gk_refs), turned_ref.shape[1]
        for n, ref in enumerate(gk_refs):
            for y in range(ref.shape[0]):
                owner = y * rounds + (place_ref[1] + n) % rounds
                ref[y, :lines] = fk_ref[owner]
                ref[y, lines:] = turned_ref[owner]


def far_first(i, steps, place):
    half = steps // 2
    return 2 * (i % half) + jnp.where(i < half, 1 - place[0], place[0])


def backward(place, t, s, stats, c, q, k, kt, w, part, owners, former=None):
    rows, width = q.shape
    keys, dim = k.shape
    keys = keys // PARTS
    steps = width // (dim * GROUP)
    last = former is not None
    whole = lambda *shape: pl.BlockSpec(shape, lambda i, place: (0,) * len(shape))
    w = jnp.moveaxis(w.reshape(rows, steps, GROUP), 1, 0)
    block, shape = (1, rows + 8, dim * GROUP), (owners, keys // owners, dim)
    array = lambda *shape: jax.ShapeDtypeStruct(shape, jnp.float32)
    in_specs = [
        whole(*t.shape),
        pl.BlockSpec((rows, keys), lambda i, place: (0, part)),
        whole(*stats.shape),
        whole(1, rows),
        whole(rows, width),
        pl.BlockSpec((keys, dim), lambda i, place: (part, 0)),
        pl.BlockSpec((dim, keys), lambda i, place: (0, part)),
        whole(*w.shape),
    ]
    args = [t, s, stats, c, q, k, kt, w]
    scratch = [pltpu.VMEM((rows, keys), jnp.float32), pltpu.VMEM((dim, keys), jnp.float32)]
    if last:
        half = steps // 2
        in_specs += [pl.BlockSpec(block, lambda i, place: (far_first(i, steps, place), 0, 0)), whole(*shape)]
        args += former
        scratch.append(pltpu.VMEM(shape, jnp.float32))
        piece = (owners // ROUNDS, PARTS * shape[1], dim)
        out_specs = [
            pl.BlockSpec(block, lambda i, place: (jnp.minimum(i, half - 1), 0, 0)),
            pl.BlockSpec(block, lambda i, place: (jnp.maximum(i - half, 0), 0, 0)),
        ] + [whole(*piece)] * ROUNDS
        out_shape = [array(half, *block[1:])] * 2 + [array(*piece)] * ROUNDS
    else:
        out_specs = [pl.BlockSpec(block, lambda i, place: (i, 0, 0)), whole(*shape)]
        out_shape = [array(steps, *block[1:]), array(*shape)]
    return pl.pallas_call(
        functools.partial(back_kernel, last),
        grid_spec=pltpu.PrefetchScalarGridSpec(
            num_scalar_prefetch=1, grid=(steps,), in_specs=in_specs, out_specs=out_specs, scratch_shapes=scratch
        ),
        out_shape=out_shape,
        compiler_params=pltpu.CompilerParams(vmem_limit_bytes=VMEM),
        cost_estimate=pl.CostEstimate(
            flops=6 * rows * width * keys, bytes_accessed=4 << 20, transcendentals=rows * keys
        ),
    )(place, *args)


def end_kernel(x_ref, gq_ref, gw_ref):
    rows = gq_ref.shape[0]
    total = jnp.sum(x_ref[...], axis=0)
    gq_ref[...] = total[:rows]
    gw_ref[...] = total[rows : rows + GROUP, :rows]


def ended(x):
    _, rows, width = x.shape
    rows -= 8
    return pl.pallas_call(
        end_kernel,
        out_shape=[
            jax.ShapeDtypeStruct((rows, width), jnp.float32),
            jax.ShapeDtypeStruct((GROUP, rows), jnp.float32),
        ],
        compiler_params=pltpu.CompilerParams(vmem_limit_bytes=VMEM),
        name="end",
    )(x)


def join_kernel(place_ref, *refs):
    *in_refs, out_ref = refs
    parts, _, rows, _ = out_ref.shape
    rounds = len(in_refs)
    for n, ref in enumerate(in_refs):
        for y in range(ref.shape[0]):
            for p in range(parts):
                owner = y * rounds + (place_ref[1] + rounds - n) % rounds
                out_ref[p, owner] = ref[y, p * rows : (p + 1) * rows]


def joined(place, pieces):
    count, rows, dim = pieces[0].shape
    vmem = pl.BlockSpec(memory_space=pltpu.VMEM)
    return pl.pallas_call(
        join_kernel,
        in_specs=[pl.BlockSpec(memory_space=pltpu.SMEM)] + [vmem] * len(pieces),
        out_specs=vmem,
        out_shape=jax.ShapeDtypeStruct((PARTS, count * len(pieces), rows // PARTS, dim), jnp.float32),
        compiler_params=pltpu.CompilerParams(vmem_limit_bytes=VMEM),
        name="join",
    )(place, *pieces)


def exchanged(x, axis, groups=None):
    return lax.all_to_all(x, axis, 0, 0, axis_index_groups=groups, tiled=True)


def flipped(x, axis, mask):
    return lax.ppermute(x, axis, [(i, i ^ mask) for i in range(lax.axis_size(axis))])


def turned(x, k):
    n = lax.axis_size("head")
    return lax.ppermute(x, "head", [(i, i // ROUNDS * ROUNDS + (i + k) % ROUNDS) for i in range(n)])


def shards(q_latent, k_latent, q_index, k_index, head_weight, loss_weight, query_pos, key_start):
    keys = k_latent.shape[0]
    rows = q_index.shape[0]
    owners, peers = lax.axis_size("head"), lax.axis_size("key")
    at_key, at_head = (lax.axis_index(name).astype(jnp.int32) for name in ("key", "head"))
    base, place = (at_key * keys).reshape(1), jnp.stack([at_key % 2, at_head])
    own = at_head * rows
    start, pos = key_start.reshape(1, -1), query_pos.reshape(1, -1)
    own_start = lax.dynamic_slice_in_dim(start, own, rows, axis=1)
    own_pos = lax.dynamic_slice_in_dim(pos, own, rows, axis=1)
    kt_index = k_index.T
    e, high, lse = main_forward(base, k_latent.T, jnp.swapaxes(q_latent, 1, 2), start, pos, peers)
    stats = exchanged(lse, "key")
    scores, index_lse = index_forward(base, q_index, kt_index, head_weight, own_start, own_pos, peers)
    index_stats = exchanged(index_lse, "key")
    targets = []
    for part in range(PARTS):
        partial = weighted_sum(e, high, stats, owners, part)
        targets.append(exchanged(partial, "head"))

    def back(part, *former):
        fixed = (scores, index_stats, loss_weight.reshape(1, -1), q_index, k_index, kt_index, head_weight)
        return backward(place, targets[part], *fixed, part, owners, *former)

    former = back(0)
    far, near, *pieces = back(1, former)
    moved = flipped(far, "key", 1)
    groups = [list(range(c, peers, 2)) for c in (0, 1)]
    gq = exchanged(near + moved, "key", groups)
    gk = sum([turned(x, k) for k, x in enumerate(pieces) if k], pieces[0])
    gk = gk + flipped(gk, "head", ROUNDS)
    gk = joined(place, [gk] + [turned(gk, k) for k in range(1, ROUNDS)]).reshape(keys, -1)
    gq, gw = ended(gq)
    return (gq, gk, gw.T)


def solution(mesh):
    return jax.shard_map(
        shards,
        mesh=mesh,
        in_specs=(
            P("head", None, None),
            P("key", None),
            P("head", None),
            P("key", None),
            P("head", None),
            P("head"),
            P(),
            P(),
        ),
        out_specs=(P("head", "key"), P("key", None), P("head", "key")),
        check_vma=False,
    )
```

```python
import functools
import math

import jax
import jax.numpy as jnp
from jax import lax
from jax.experimental import pallas as pl
from jax.experimental.pallas import tpu as pltpu
from jax.sharding import PartitionSpec as P


H = 128
QK_DIM = 192
LOG2E = 1.4426950408889634
LOW = -1e30
FLOOR = -1e29
CHUNK = 256
TILE = 256
RUN = 4
GROUP = 4
PARTS = 2
ROUNDS = 4
VMEM = 48 << 20


def eye_of(n):
    rows = lax.broadcasted_iota(jnp.int32, (n, n), 0)
    return rows == lax.broadcasted_iota(jnp.int32, (n, n), 1)


def as_column(row):
    n = row.shape[1]
    return jnp.sum(jnp.where(eye_of(n), row, jnp.zeros_like(row)), axis=1, keepdims=True)


def as_row(column):
    n = column.shape[0]
    return jnp.sum(jnp.where(eye_of(n), column, jnp.zeros_like(column)), axis=0, keepdims=True)


def split_dot(x, onehot, dims, pieces):
    total = 0.0
    for _ in range(pieces):
        high = x.astype(jnp.bfloat16)
        x = x - high.astype(jnp.float32)
        total = total + lax.dot_general(*dims(high, onehot), preferred_element_type=jnp.float32)
    return total


def in_use(t, info):
    return (t == 0) | (info[1] > t * TILE)


def main_kernel(info_ref, kt_ref, q0_ref, *refs):
    qt_refs, refs = refs[:RUN], refs[RUN:]
    start_ref, pos_ref, e_ref, sel_ref, m_ref, lse_ref, k_ref, bias_ref, part_ref, picked_ref = refs
    step, steps = pl.program_id(0), pl.num_programs(0)
    heads = part_ref.shape[1]
    tiles = bias_ref.shape[0]
    keys, queries = k_ref.shape[0], start_ref.shape[1]
    chunks = keys // CHUNK
    scale = LOG2E / math.sqrt(QK_DIM)
    first = info_ref[0]

    def pick(t, q):
        return jnp.dot(q, sel_ref[t], preferred_element_type=jnp.float32).astype(jnp.bfloat16)

    def any_seen():
        return (start_ref[...] < first + keys) & (pos_ref[...] >= first)

    @pl.when(step == 0)
    def _():
        k_ref[...] = kt_ref[...].T

    def prepare(t):
        seen = any_seen()
        rows = lax.broadcasted_iota(jnp.int32, (queries, queries), 0)
        before = rows < lax.broadcasted_iota(jnp.int32, (queries, queries), 1)
        rank = jnp.dot(
            jnp.broadcast_to(seen.astype(jnp.float32), (8, queries)).astype(jnp.bfloat16),
            before.astype(jnp.bfloat16),
            preferred_element_type=jnp.float32,
        )[0:1]
        rank = as_column(jnp.where(seen, rank, -1.0))
        places = t * TILE + lax.broadcasted_iota(jnp.int32, (queries, TILE), 1)
        chosen = rank == places.astype(jnp.float32)
        sel_ref[t] = chosen.astype(jnp.bfloat16)
        left, right = start_ref[...].astype(jnp.float32), pos_ref[...].astype(jnp.float32) + 1.0
        left = jnp.sum(jnp.where(chosen, as_column(left), 0.0), axis=0, keepdims=True)
        right = jnp.sum(jnp.where(chosen, as_column(right), 0.0), axis=0, keepdims=True)
        s = (first + lax.broadcasted_iota(jnp.int32, (keys, TILE), 0)).astype(jnp.float32)
        bias_ref[t] = jnp.where((s >= left) & (s < right), 0.0, LOW)
        picked_ref[t, 0] = pick(t, q0_ref[0])

    def score(t, n):
        h = step * RUN + n
        qt = picked_ref[t, n % 2]
        highs, sums = [], []
        for c in range(chunks):
            here = pl.ds(c * CHUNK, CHUNK)
            s = jnp.dot(k_ref[here, :], qt, preferred_element_type=jnp.float32)
            if c == chunks - 1:
                picked_ref[t, (n + 1) % 2] = pick(t, qt_refs[n][0])
            s = s * scale + bias_ref[t, here, :]
            high = jnp.maximum(jnp.max(s, axis=0, keepdims=True), FLOOR)
            e = jnp.exp2(s - high)
            e_ref[t, n, here, :] = e.astype(jnp.bfloat16)
            highs.append(high)
            sums.append(jnp.sum(e, axis=0, keepdims=True))
            m_ref[pl.ds((t * heads + h) * chunks + c, 1), :] = high
        top = functools.reduce(jnp.maximum, highs)
        total = sum(l * jnp.exp2(m - top) for l, m in zip(sums, highs))
        part_ref[t, pl.ds(h, 1), :] = jnp.where(total > 0.0, top + jnp.log2(total), 0.0)

    def scores(t):
        for n in range(RUN):
            score(t, n)

    def send(t):
        dims = lambda x, y: (x, y, (((1,), (1,)), ((), ())))
        lse = split_dot(part_ref[t], sel_ref[t], dims, 3)
        lse = jnp.where(any_seen(), lse, FLOOR) if t == 0 else lse_ref[0] + lse
        for i in range(lse_ref.shape[0]):
            lse_ref[i] = lse

    for t in range(tiles):
        used = in_use(t, info_ref)
        pl.when(used & (step == 0))(functools.partial(prepare, t))
        pl.when(used)(functools.partial(scores, t)) if t else scores(t)
        pl.when(used & (step == steps - 1))(functools.partial(send, t))


def main_forward(info, kt, qt, start, pos, peers):
    heads, lat, queries = qt.shape
    keys = kt.shape[1]
    chunks, tiles = keys // CHUNK, queries // TILE
    whole = lambda *shape: pl.BlockSpec(shape, lambda i, info: (0,) * len(shape))
    later = lambda n, i, info: (jnp.minimum(i * RUN + n, heads - 1), 0, 0)
    return pl.pallas_call(
        main_kernel,
        grid_spec=pltpu.PrefetchScalarGridSpec(
            num_scalar_prefetch=1,
            grid=(heads // RUN,),
            in_specs=[
                whole(lat, keys),
                whole(1, lat, queries),
                *(pl.BlockSpec((1, lat, queries), functools.partial(later, n)) for n in range(1, RUN + 1)),
                whole(1, queries),
                whole(1, queries),
            ],
            out_specs=[
                pl.BlockSpec((tiles, RUN, keys, TILE), lambda i, info: (0, i, 0, 0)),
                whole(tiles, queries, TILE),
                whole(tiles * heads * chunks, TILE),
                whole(peers, heads, queries),
            ],
            scratch_shapes=[
                pltpu.VMEM((keys, lat), jnp.bfloat16),
                pltpu.VMEM((tiles, keys, TILE), jnp.float32),
                pltpu.VMEM((tiles, heads, TILE), jnp.float32),
                pltpu.VMEM((tiles, 2, lat, TILE), jnp.bfloat16),
            ],
        ),
        out_shape=[
            jax.ShapeDtypeStruct((tiles, heads, keys, TILE), jnp.bfloat16),
            jax.ShapeDtypeStruct((tiles, queries, TILE), jnp.bfloat16),
            jax.ShapeDtypeStruct((tiles * heads * chunks, TILE), jnp.float32),
            jax.ShapeDtypeStruct((peers, heads, queries), jnp.float32),
        ],
        cost_estimate=pl.CostEstimate(
            flops=2 * heads * keys * queries * lat, bytes_accessed=26 << 20, transcendentals=heads * keys * queries
        ),
        name="main_forward",
    )(info, kt, *([qt] * (RUN + 1)), start, pos)


def index_kernel(base_ref, q_ref, kt_ref, w_ref, start_ref, pos_ref, s_ref, lse_ref):
    c = pl.program_id(0)
    rows, width = s_ref.shape[0], CHUNK
    heads = w_ref.shape[1]
    dim = kt_ref.shape[0]
    here = pl.ds(pl.multiple_of(c * width, width), width)
    kt = kt_ref[:, here]
    total = jnp.zeros((rows, width), jnp.float32)
    for j in range(heads):
        d = jnp.dot(q_ref[:, j * dim : (j + 1) * dim], kt, preferred_element_type=jnp.float32)
        total = total + w_ref[:, j : j + 1] * jnp.maximum(d, 0.0)
    s = base_ref[0] + c * width + lax.broadcasted_iota(jnp.int32, (rows, width), 1)
    seen = (s >= as_column(start_ref[...])) & (s <= as_column(pos_ref[...]))
    s_ref[:, here] = jnp.where(seen, total * (LOG2E / math.sqrt(dim)), LOW)

    @pl.when(c == pl.num_programs(0) - 1)
    def _():
        scores = s_ref[...]
        high = jnp.maximum(jnp.max(scores, axis=1, keepdims=True), FLOOR)
        total = jnp.sum(jnp.exp2(scores - high), axis=1, keepdims=True)
        row = as_row(jnp.where(total > 0.0, high + jnp.log2(total), FLOOR))
        row = jnp.concatenate([row, jnp.zeros_like(row)], axis=1)
        lse_ref[...] = jnp.broadcast_to(row[None], lse_ref.shape)


def index_forward(base, q, kt, w, start, pos, peers):
    rows, width = q.shape
    dim, keys = kt.shape
    heads = w.shape[1]
    whole = lambda *shape: pl.BlockSpec(shape, lambda c: (0,) * len(shape))
    return pl.pallas_call(
        index_kernel,
        grid=(keys // CHUNK,),
        in_specs=[
            pl.BlockSpec(memory_space=pltpu.SMEM),
            whole(rows, width),
            whole(dim, keys),
            whole(rows, heads),
            whole(1, rows),
            whole(1, rows),
        ],
        out_specs=[whole(rows, keys), whole(peers, 8, 2 * rows)],
        out_shape=[
            jax.ShapeDtypeStruct((rows, keys), jnp.float32),
            jax.ShapeDtypeStruct((peers, 8, 2 * rows), jnp.float32),
        ],
        cost_estimate=pl.CostEstimate(flops=2 * rows * width * keys, bytes_accessed=2 << 20, transcendentals=rows * keys),
        name="index_forward",
    )(base, q, kt, w, start, pos)


def sum_kernel(first, info_ref, e_ref, sel_ref, m_ref, stats_ref, t_ref, lse_ref):
    c, t = pl.program_id(0), pl.program_id(1)
    _, heads, width, _ = e_ref.shape
    owners, rows, _ = t_ref.shape
    chunks = m_ref.shape[0] // heads // pl.num_programs(1)
    lanes = 128

    @pl.when(in_use(t, info_ref) & (c == 0))
    def _():
        stats = [stats_ref[i] for i in range(stats_ref.shape[0])]
        high = functools.reduce(jnp.maximum, stats)
        lse = high + jnp.log2(sum(jnp.exp2(x - high) for x in stats))
        lse_ref[t] = split_dot(lse, sel_ref[0], lambda x, y: (x, y, (((1,), (0,)), ((), ()))), 3)

    @pl.when(in_use(t, info_ref))
    def _():
        lse = lse_ref[t]
        row = t * heads * chunks + first + c
        weights = [jnp.exp2(m_ref[pl.ds(row + h * chunks, 1), :] - lse[h : h + 1]) for h in range(heads)]
        strips = []
        for r in range(width // lanes):
            at = slice(r * lanes, (r + 1) * lanes)
            total = e_ref[0, 0, at, :].astype(jnp.float32) * weights[0]
            for h in range(1, heads):
                total = total + e_ref[0, h, at, :].astype(jnp.float32) * weights[h]
            strips.append(total)
        total = jnp.concatenate(strips, axis=0)
        dense = split_dot(total, sel_ref[0], lambda x, y: (y, x, (((1,), (1,)), ((), ()))), 2)
        dense = dense.reshape(owners, rows, width)

        @pl.when(t == 0)
        def _():
            t_ref[...] = dense

        @pl.when(t > 0)
        def _():
            t_ref[...] += dense


def weighted_sum(info, e, sel, m, stats, owners, part):
    tiles, heads, keys, tile = e.shape
    queries = sel.shape[1]
    rows = queries // owners
    steps = keys // PARTS // CHUNK
    first = part * steps
    used = lambda t, info: jnp.where(in_use(t, info), t, 0)
    return pl.pallas_call(
        functools.partial(sum_kernel, first),
        grid_spec=pltpu.PrefetchScalarGridSpec(
            num_scalar_prefetch=1,
            grid=(steps, tiles),
            in_specs=[
                pl.BlockSpec((1, heads, CHUNK, tile), lambda c, t, info: (used(t, info), 0, first + c, 0)),
                pl.BlockSpec((1, queries, tile), lambda c, t, info: (used(t, info), 0, 0)),
                pl.BlockSpec(m.shape, lambda c, t, info: (0, 0)),
                pl.BlockSpec(stats.shape, lambda c, t, info: (0, 0, 0)),
            ],
            out_specs=pl.BlockSpec((owners, rows, CHUNK), lambda c, t, info: (0, 0, c)),
            scratch_shapes=[pltpu.VMEM((tiles, heads, tile), jnp.float32)],
        ),
        out_shape=jax.ShapeDtypeStruct((owners, rows, keys // PARTS), jnp.float32),
        compiler_params=pltpu.CompilerParams(vmem_limit_bytes=VMEM),
        cost_estimate=pl.CostEstimate(
            flops=2 * heads * keys * queries // PARTS, bytes_accessed=18 << 19, transcendentals=heads * queries
        ),
    )(info, e, sel, m, stats)


def back_kernel(last, place_ref, t_ref, s_ref, stats_ref, c_ref, q_ref, k_ref, kt_ref, w_ref, *refs):
    if last:
        former_ref, fk_ref, far_ref, near_ref, *gk_refs, g_ref, gkt_ref, turned_ref = refs
    else:
        gq_ref, gk_ref, g_ref, gkt_ref = refs
    i, steps = pl.program_id(0), pl.num_programs(0)
    rows, _ = g_ref.shape
    dim = kt_ref.shape[0]
    width = dim * GROUP
    index_scale = 1.0 / math.sqrt(dim)
    dest = far_first(i, steps, place_ref) if last else i

    @pl.when(i == 0)
    def _():
        target = jnp.sum(t_ref[...], axis=0) * (1.0 / H)
        scores = s_ref[...]
        stats = [stats_ref[n, 0:1, :rows] for n in range(stats_ref.shape[0])]
        high = functools.reduce(jnp.maximum, stats)
        lse = high + jnp.log2(sum(jnp.exp2(x - high) for x in stats))
        probs = jnp.exp2(scores - as_column(lse))
        g_ref[...] = jnp.where(scores > FLOOR, as_column(c_ref[...]) * (probs - target), 0.0)
        gkt_ref[...] = jnp.zeros_like(gkt_ref)

    q = q_ref[:, pl.ds(pl.multiple_of(dest * width, width), width)]
    q = jnp.concatenate([q[:, j * dim : (j + 1) * dim] for j in range(GROUP)], axis=0)
    d = jnp.dot(q, kt_ref[...], preferred_element_type=jnp.float32)
    g = g_ref[...]
    w = w_ref[dest]
    parts, sums = [], []
    for j in range(GROUP):
        dots = d[j * rows : (j + 1) * rows]
        kept = jnp.where(dots > 0.0, g, 0.0)
        parts.append((kept * (w[:, j : j + 1] * index_scale)).astype(jnp.bfloat16))
        sums.append(as_row(jnp.sum(kept * dots, axis=1, keepdims=True)))
    head_grad = jnp.concatenate(parts, axis=0)
    gq = jnp.dot(head_grad, k_ref[...], preferred_element_type=jnp.float32)
    pad = jnp.zeros((1, width - rows), jnp.float32)
    low = [jnp.concatenate([x * index_scale, pad], axis=1) for x in sums]
    low = jnp.concatenate([*low, jnp.zeros((8 - GROUP, width), jnp.float32)], axis=0)
    gq = jnp.concatenate([gq[j * rows : (j + 1) * rows] for j in range(GROUP)], axis=1)
    gq = jnp.concatenate([gq, low], axis=0)
    gkt_ref[...] += lax.dot_general(q, head_grad, (((0,), (0,)), ((), ())), preferred_element_type=jnp.float32)
    if not last:
        gq_ref[0] = gq

        @pl.when(i == steps - 1)
        def _():
            gk_ref[...] = gkt_ref[...].T.reshape(gk_ref.shape)

        return
    gq = gq + former_ref[dest]

    @pl.when(i < steps // 2)
    def _():
        far_ref[0] = gq

    @pl.when(i >= steps // 2)
    def _():
        near_ref[0] = gq

    @pl.when(i == steps - 1)
    def _():
        turned_ref[...] = gkt_ref[...].T.reshape(turned_ref.shape)
        rounds, lines = len(gk_refs), turned_ref.shape[1]
        for n, ref in enumerate(gk_refs):
            for y in range(ref.shape[0]):
                owner = y * rounds + (place_ref[1] + n) % rounds
                ref[y, :lines] = fk_ref[owner]
                ref[y, lines:] = turned_ref[owner]


def far_first(i, steps, place):
    half = steps // 2
    return 2 * (i % half) + jnp.where(i < half, 1 - place[0], place[0])


def backward(place, t, s, stats, c, q, k, kt, w, part, owners, former=None):
    rows, width = q.shape
    keys, dim = k.shape
    keys = keys // PARTS
    steps = width // (dim * GROUP)
    last = former is not None
    whole = lambda *shape: pl.BlockSpec(shape, lambda i, place: (0,) * len(shape))
    w = jnp.moveaxis(w.reshape(rows, steps, GROUP), 1, 0)
    block, shape = (1, rows + 8, dim * GROUP), (owners, keys // owners, dim)
    array = lambda *shape: jax.ShapeDtypeStruct(shape, jnp.float32)
    in_specs = [
        whole(*t.shape),
        pl.BlockSpec((rows, keys), lambda i, place: (0, part)),
        whole(*stats.shape),
        whole(1, rows),
        whole(rows, width),
        pl.BlockSpec((keys, dim), lambda i, place: (part, 0)),
        pl.BlockSpec((dim, keys), lambda i, place: (0, part)),
        whole(*w.shape),
    ]
    args = [t, s, stats, c, q, k, kt, w]
    scratch = [pltpu.VMEM((rows, keys), jnp.float32), pltpu.VMEM((dim, keys), jnp.float32)]
    if last:
        half = steps // 2
        in_specs += [whole(*former[0].shape), whole(*shape)]
        args += former
        scratch.append(pltpu.VMEM(shape, jnp.float32))
        piece = (owners // ROUNDS, PARTS * shape[1], dim)
        out_specs = [
            pl.BlockSpec(block, lambda i, place: (jnp.minimum(i, half - 1), 0, 0)),
            pl.BlockSpec(block, lambda i, place: (jnp.maximum(i - half, 0), 0, 0)),
        ] + [whole(*piece)] * ROUNDS
        out_shape = [array(half, *block[1:])] * 2 + [array(*piece)] * ROUNDS
    else:
        out_specs = [pl.BlockSpec(block, lambda i, place: (i, 0, 0)), whole(*shape)]
        out_shape = [array(steps, *block[1:]), array(*shape)]
    return pl.pallas_call(
        functools.partial(back_kernel, last),
        grid_spec=pltpu.PrefetchScalarGridSpec(
            num_scalar_prefetch=1, grid=(steps,), in_specs=in_specs, out_specs=out_specs, scratch_shapes=scratch
        ),
        out_shape=out_shape,
        cost_estimate=pl.CostEstimate(
            flops=6 * rows * width * keys, bytes_accessed=4 << 20, transcendentals=rows * keys
        ),
    )(place, *args)


def end_kernel(x_ref, gq_ref, gw_ref):
    rows = gq_ref.shape[0]
    total = jnp.sum(x_ref[...], axis=0)
    gq_ref[...] = total[:rows]
    gw_ref[...] = total[rows : rows + GROUP, :rows]


def ended(x):
    _, rows, width = x.shape
    rows -= 8
    return pl.pallas_call(
        end_kernel,
        out_shape=[
            jax.ShapeDtypeStruct((rows, width), jnp.float32),
            jax.ShapeDtypeStruct((GROUP, rows), jnp.float32),
        ],
        compiler_params=pltpu.CompilerParams(vmem_limit_bytes=VMEM),
        name="end",
    )(x)


def join_kernel(place_ref, *refs):
    *in_refs, out_ref = refs
    parts, _, rows, _ = out_ref.shape
    rounds = len(in_refs)
    for n, ref in enumerate(in_refs):
        for y in range(ref.shape[0]):
            for p in range(parts):
                owner = y * rounds + (place_ref[1] + rounds - n) % rounds
                out_ref[p, owner] = ref[y, p * rows : (p + 1) * rows]


def joined(place, pieces):
    count, rows, dim = pieces[0].shape
    vmem = pl.BlockSpec(memory_space=pltpu.VMEM)
    return pl.pallas_call(
        join_kernel,
        in_specs=[pl.BlockSpec(memory_space=pltpu.SMEM)] + [vmem] * len(pieces),
        out_specs=vmem,
        out_shape=jax.ShapeDtypeStruct((PARTS, count * len(pieces), rows // PARTS, dim), jnp.float32),
        compiler_params=pltpu.CompilerParams(vmem_limit_bytes=VMEM),
        name="join",
    )(place, *pieces)


def exchanged(x, axis, groups=None):
    return lax.all_to_all(x, axis, 0, 0, axis_index_groups=groups, tiled=True)


def flipped(x, axis, mask):
    return lax.ppermute(x, axis, [(i, i ^ mask) for i in range(lax.axis_size(axis))])


def turned(x, k):
    n = lax.axis_size("head")
    return lax.ppermute(x, "head", [(i, i // ROUNDS * ROUNDS + (i + k) % ROUNDS) for i in range(n)])


def shards(q_latent, k_latent, q_index, k_index, head_weight, loss_weight, query_pos, key_start):
    keys = k_latent.shape[0]
    rows = q_index.shape[0]
    owners, peers = lax.axis_size("head"), lax.axis_size("key")
    at_key, at_head = (lax.axis_index(name).astype(jnp.int32) for name in ("key", "head"))
    base, place = (at_key * keys).reshape(1), jnp.stack([at_key % 2, at_head])
    own = at_head * rows
    start, pos = key_start.reshape(1, -1), query_pos.reshape(1, -1)
    own_start = lax.dynamic_slice_in_dim(start, own, rows, axis=1)
    own_pos = lax.dynamic_slice_in_dim(pos, own, rows, axis=1)
    kt_index = k_index.T
    count = jnp.sum((key_start < base + keys) & (query_pos >= base), dtype=jnp.int32)
    info = jnp.stack([at_key * keys, count])
    e, sel, high, lse = main_forward(info, k_latent.T, jnp.swapaxes(q_latent, 1, 2), start, pos, peers)
    stats = exchanged(lse, "key")
    scores, index_lse = index_forward(base, q_index, kt_index, head_weight, own_start, own_pos, peers)
    index_stats = exchanged(index_lse, "key")
    targets = []
    for part in range(PARTS):
        partial = weighted_sum(info, e, sel, high, stats, owners, part)
        targets.append(exchanged(partial, "head"))

    def back(part, *former):
        fixed = (scores, index_stats, loss_weight.reshape(1, -1), q_index, k_index, kt_index, head_weight)
        return backward(place, targets[part], *fixed, part, owners, *former)

    former = back(0)
    far, near, *pieces = back(1, former)
    moved = flipped(far, "key", 1)
    groups = [list(range(c, peers, 2)) for c in (0, 1)]
    gq = exchanged(near + moved, "key", groups)
    pieces = [turned(x, k) if k else x for k, x in enumerate(pieces)]
    gk = sum(pieces[1:], pieces[0])
    gk = gk + flipped(gk, "head", ROUNDS)
    gk = joined(place, [gk] + [turned(gk, k) for k in range(1, ROUNDS)]).reshape(keys, -1)
    gq, gw = ended(gq)
    return (gq, gk, gw.T)


def solution(mesh):
    return jax.shard_map(
        shards,
        mesh=mesh,
        in_specs=(
            P("head", None, None),
            P("key", None),
            P("head", None),
            P("key", None),
            P("head", None),
            P("head"),
            P(),
            P(),
        ),
        out_specs=(P("head", "key"), P("key", None), P("head", "key")),
        check_vma=False,
    )
```

```python
import functools
import math

import jax
import jax.numpy as jnp
from jax import lax
from jax.experimental import pallas as pl
from jax.experimental.pallas import tpu as pltpu
from jax.sharding import PartitionSpec as P


H = 128
QK_DIM = 192
LOG2E = 1.4426950408889634
LOW = -1e30
FLOOR = -1e29
CHUNK = 256
TILE = 256
RUN = 4
GROUP = 4
PARTS = 2
ROUNDS = 4
VMEM = 48 << 20


def eye_of(n):
    rows = lax.broadcasted_iota(jnp.int32, (n, n), 0)
    return rows == lax.broadcasted_iota(jnp.int32, (n, n), 1)


def as_column(row):
    n = row.shape[1]
    return jnp.sum(jnp.where(eye_of(n), row, jnp.zeros_like(row)), axis=1, keepdims=True)


def as_row(column):
    n = column.shape[0]
    return jnp.sum(jnp.where(eye_of(n), column, jnp.zeros_like(column)), axis=0, keepdims=True)


def split_dot(x, onehot, dims, pieces):
    total = 0.0
    for _ in range(pieces):
        high = x.astype(jnp.bfloat16)
        x = x - high.astype(jnp.float32)
        total = total + lax.dot_general(*dims(high, onehot), preferred_element_type=jnp.float32)
    return total


def in_use(t, info):
    return (t == 0) | (info[0] > t * TILE)


def main_kernel(base_ref, kt_ref, q0_ref, *refs):
    qt_refs, refs = refs[:RUN], refs[RUN:]
    start_ref, pos_ref, e_ref, sel_ref, m_ref, lse_ref, k_ref, bias_ref, part_ref, picked_ref, count_ref = refs
    step, steps = pl.program_id(0), pl.num_programs(0)
    heads = part_ref.shape[1]
    tiles = bias_ref.shape[0]
    keys, queries = k_ref.shape[0], start_ref.shape[1]
    chunks = keys // CHUNK
    scale = LOG2E / math.sqrt(QK_DIM)
    first = base_ref[0]

    def pick(t, q):
        return jnp.dot(q, sel_ref[t], preferred_element_type=jnp.float32).astype(jnp.bfloat16)

    def any_seen():
        return (start_ref[...] < first + keys) & (pos_ref[...] >= first)

    @pl.when(step == 0)
    def _():
        k_ref[...] = kt_ref[...].T
        count_ref[0] = jnp.sum(any_seen().astype(jnp.int32))

    def prepare(t):
        seen = any_seen()
        rows = lax.broadcasted_iota(jnp.int32, (queries, queries), 0)
        before = rows < lax.broadcasted_iota(jnp.int32, (queries, queries), 1)
        rank = jnp.dot(
            jnp.broadcast_to(seen.astype(jnp.float32), (8, queries)).astype(jnp.bfloat16),
            before.astype(jnp.bfloat16),
            preferred_element_type=jnp.float32,
        )[0:1]
        rank = as_column(jnp.where(seen, rank, -1.0))
        places = t * TILE + lax.broadcasted_iota(jnp.int32, (queries, TILE), 1)
        chosen = rank == places.astype(jnp.float32)
        sel_ref[t] = chosen.astype(jnp.bfloat16)
        left, right = start_ref[...].astype(jnp.float32), pos_ref[...].astype(jnp.float32) + 1.0
        left = jnp.sum(jnp.where(chosen, as_column(left), 0.0), axis=0, keepdims=True)
        right = jnp.sum(jnp.where(chosen, as_column(right), 0.0), axis=0, keepdims=True)
        s = (first + lax.broadcasted_iota(jnp.int32, (keys, TILE), 0)).astype(jnp.float32)
        bias_ref[t] = jnp.where((s >= left) & (s < right), 0.0, LOW)
        picked_ref[t, 0] = pick(t, q0_ref[0])

    def score(t, n):
        h = step * RUN + n
        qt = picked_ref[t, n % 2]
        highs, sums = [], []
        for c in range(chunks):
            here = pl.ds(c * CHUNK, CHUNK)
            s = jnp.dot(k_ref[here, :], qt, preferred_element_type=jnp.float32)
            if c == chunks - 1:
                picked_ref[t, (n + 1) % 2] = pick(t, qt_refs[n][0])
            s = s * scale + bias_ref[t, here, :]
            high = jnp.maximum(jnp.max(s, axis=0, keepdims=True), FLOOR)
            e = jnp.exp2(s - high)
            e_ref[t, n, here, :] = e.astype(jnp.bfloat16)
            highs.append(high)
            sums.append(jnp.sum(e, axis=0, keepdims=True))
            m_ref[pl.ds((t * heads + h) * chunks + c, 1), :] = high
        top = functools.reduce(jnp.maximum, highs)
        total = sum(l * jnp.exp2(m - top) for l, m in zip(sums, highs))
        part_ref[t, pl.ds(h, 1), :] = jnp.where(total > 0.0, top + jnp.log2(total), 0.0)

    def scores(t):
        for n in range(RUN):
            score(t, n)

    def send(t):
        dims = lambda x, y: (x, y, (((1,), (1,)), ((), ())))
        lse = split_dot(part_ref[t], sel_ref[t], dims, 3)
        lse = jnp.where(any_seen(), lse, FLOOR) if t == 0 else lse_ref[0] + lse
        for i in range(lse_ref.shape[0]):
            lse_ref[i] = lse

    for t in range(tiles):
        used = in_use(t, count_ref)
        pl.when(used & (step == 0))(functools.partial(prepare, t))
        pl.when(used)(functools.partial(scores, t)) if t else scores(t)
        pl.when(used & (step == steps - 1))(functools.partial(send, t))


def main_forward(base, kt, qt, start, pos, peers):
    heads, lat, queries = qt.shape
    keys = kt.shape[1]
    chunks, tiles = keys // CHUNK, queries // TILE
    whole = lambda *shape: pl.BlockSpec(shape, lambda i, info: (0,) * len(shape))
    later = lambda n, i, info: (jnp.minimum(i * RUN + n, heads - 1), 0, 0)
    return pl.pallas_call(
        main_kernel,
        grid_spec=pltpu.PrefetchScalarGridSpec(
            num_scalar_prefetch=1,
            grid=(heads // RUN,),
            in_specs=[
                whole(lat, keys),
                whole(1, lat, queries),
                *(pl.BlockSpec((1, lat, queries), functools.partial(later, n)) for n in range(1, RUN + 1)),
                whole(1, queries),
                whole(1, queries),
            ],
            out_specs=[
                pl.BlockSpec((tiles, RUN, keys, TILE), lambda i, info: (0, i, 0, 0)),
                whole(tiles, queries, TILE),
                whole(tiles * heads * chunks, TILE),
                whole(peers, heads, queries),
            ],
            scratch_shapes=[
                pltpu.VMEM((keys, lat), jnp.bfloat16),
                pltpu.VMEM((tiles, keys, TILE), jnp.float32),
                pltpu.VMEM((tiles, heads, TILE), jnp.float32),
                pltpu.VMEM((tiles, 2, lat, TILE), jnp.bfloat16),
                pltpu.SMEM((1,), jnp.int32),
            ],
        ),
        out_shape=[
            jax.ShapeDtypeStruct((tiles, heads, keys, TILE), jnp.bfloat16),
            jax.ShapeDtypeStruct((tiles, queries, TILE), jnp.bfloat16),
            jax.ShapeDtypeStruct((tiles * heads * chunks, TILE), jnp.float32),
            jax.ShapeDtypeStruct((peers, heads, queries), jnp.float32),
        ],
        cost_estimate=pl.CostEstimate(
            flops=2 * heads * keys * queries * lat, bytes_accessed=26 << 20, transcendentals=heads * keys * queries
        ),
        name="main_forward",
    )(base, kt, *([qt] * (RUN + 1)), start, pos)


def index_kernel(base_ref, q_ref, kt_ref, w_ref, start_ref, pos_ref, s_ref, lse_ref):
    c = pl.program_id(0)
    rows, width = s_ref.shape[0], CHUNK
    heads = w_ref.shape[1]
    dim = kt_ref.shape[0]
    here = pl.ds(pl.multiple_of(c * width, width), width)
    kt = kt_ref[:, here]
    total = jnp.zeros((rows, width), jnp.float32)
    for j in range(heads):
        d = jnp.dot(q_ref[:, j * dim : (j + 1) * dim], kt, preferred_element_type=jnp.float32)
        total = total + w_ref[:, j : j + 1] * jnp.maximum(d, 0.0)
    s = base_ref[0] + c * width + lax.broadcasted_iota(jnp.int32, (rows, width), 1)
    seen = (s >= as_column(start_ref[...])) & (s <= as_column(pos_ref[...]))
    s_ref[:, here] = jnp.where(seen, total * (LOG2E / math.sqrt(dim)), LOW)

    @pl.when(c == pl.num_programs(0) - 1)
    def _():
        scores = s_ref[...]
        high = jnp.maximum(jnp.max(scores, axis=1, keepdims=True), FLOOR)
        total = jnp.sum(jnp.exp2(scores - high), axis=1, keepdims=True)
        row = as_row(jnp.where(total > 0.0, high + jnp.log2(total), FLOOR))
        row = jnp.concatenate([row, jnp.zeros_like(row)], axis=1)
        lse_ref[...] = jnp.broadcast_to(row[None], lse_ref.shape)


def index_forward(base, q, kt, w, start, pos, peers):
    rows, width = q.shape
    dim, keys = kt.shape
    heads = w.shape[1]
    whole = lambda *shape: pl.BlockSpec(shape, lambda c: (0,) * len(shape))
    return pl.pallas_call(
        index_kernel,
        grid=(keys // CHUNK,),
        in_specs=[
            pl.BlockSpec(memory_space=pltpu.SMEM),
            whole(rows, width),
            whole(dim, keys),
            whole(rows, heads),
            whole(1, rows),
            whole(1, rows),
        ],
        out_specs=[whole(rows, keys), whole(peers, 8, 2 * rows)],
        out_shape=[
            jax.ShapeDtypeStruct((rows, keys), jnp.float32),
            jax.ShapeDtypeStruct((peers, 8, 2 * rows), jnp.float32),
        ],
        cost_estimate=pl.CostEstimate(flops=2 * rows * width * keys, bytes_accessed=2 << 20, transcendentals=rows * keys),
        name="index_forward",
    )(base, q, kt, w, start, pos)


def sum_kernel(first, info_ref, e_ref, sel_ref, m_ref, stats_ref, t_ref, lse_ref):
    c, t = pl.program_id(0), pl.program_id(1)
    _, heads, width, _ = e_ref.shape
    owners, rows, _ = t_ref.shape
    chunks = m_ref.shape[0] // heads // pl.num_programs(1)
    lanes = 128

    @pl.when(in_use(t, info_ref) & (c == 0))
    def _():
        stats = [stats_ref[i] for i in range(stats_ref.shape[0])]
        high = functools.reduce(jnp.maximum, stats)
        lse = high + jnp.log2(sum(jnp.exp2(x - high) for x in stats))
        lse_ref[t] = split_dot(lse, sel_ref[0], lambda x, y: (x, y, (((1,), (0,)), ((), ()))), 3)

    @pl.when(in_use(t, info_ref))
    def _():
        lse = lse_ref[t]
        row = t * heads * chunks + first + c
        weights = [jnp.exp2(m_ref[pl.ds(row + h * chunks, 1), :] - lse[h : h + 1]) for h in range(heads)]
        strips = []
        for r in range(width // lanes):
            at = slice(r * lanes, (r + 1) * lanes)
            total = e_ref[0, 0, at, :].astype(jnp.float32) * weights[0]
            for h in range(1, heads):
                total = total + e_ref[0, h, at, :].astype(jnp.float32) * weights[h]
            strips.append(total)
        total = jnp.concatenate(strips, axis=0)
        dense = split_dot(total, sel_ref[0], lambda x, y: (y, x, (((1,), (1,)), ((), ()))), 2)
        dense = dense.reshape(owners, rows, width)

        @pl.when(t == 0)
        def _():
            t_ref[...] = dense

        @pl.when(t > 0)
        def _():
            t_ref[...] += dense


def weighted_sum(info, e, sel, m, stats, owners, part):
    tiles, heads, keys, tile = e.shape
    queries = sel.shape[1]
    rows = queries // owners
    steps = keys // PARTS // CHUNK
    first = part * steps
    used = lambda t, info: jnp.where(in_use(t, info), t, 0)
    return pl.pallas_call(
        functools.partial(sum_kernel, first),
        grid_spec=pltpu.PrefetchScalarGridSpec(
            num_scalar_prefetch=1,
            grid=(steps, tiles),
            in_specs=[
                pl.BlockSpec((1, heads, CHUNK, tile), lambda c, t, info: (used(t, info), 0, first + c, 0)),
                pl.BlockSpec((1, queries, tile), lambda c, t, info: (used(t, info), 0, 0)),
                pl.BlockSpec(m.shape, lambda c, t, info: (0, 0)),
                pl.BlockSpec(stats.shape, lambda c, t, info: (0, 0, 0)),
            ],
            out_specs=pl.BlockSpec((owners, rows, CHUNK), lambda c, t, info: (0, 0, c)),
            scratch_shapes=[pltpu.VMEM((tiles, heads, tile), jnp.float32)],
        ),
        out_shape=jax.ShapeDtypeStruct((owners, rows, keys // PARTS), jnp.float32),
        compiler_params=pltpu.CompilerParams(vmem_limit_bytes=VMEM),
        cost_estimate=pl.CostEstimate(
            flops=2 * heads * keys * queries // PARTS, bytes_accessed=18 << 19, transcendentals=heads * queries
        ),
    )(info, e, sel, m, stats)


def back_kernel(last, place_ref, t_ref, s_ref, stats_ref, c_ref, q_ref, k_ref, kt_ref, w_ref, *refs):
    if last:
        former_ref, fk_ref, far_ref, near_ref, *gk_refs, g_ref, gkt_ref, turned_ref = refs
    else:
        gq_ref, gk_ref, g_ref, gkt_ref = refs
    i, steps = pl.program_id(0), pl.num_programs(0)
    rows, _ = g_ref.shape
    dim = kt_ref.shape[0]
    width = dim * GROUP
    index_scale = 1.0 / math.sqrt(dim)
    dest = far_first(i, steps, place_ref) if last else i

    @pl.when(i == 0)
    def _():
        target = jnp.sum(t_ref[...], axis=0) * (1.0 / H)
        scores = s_ref[...]
        stats = [stats_ref[n, 0:1, :rows] for n in range(stats_ref.shape[0])]
        high = functools.reduce(jnp.maximum, stats)
        lse = high + jnp.log2(sum(jnp.exp2(x - high) for x in stats))
        probs = jnp.exp2(scores - as_column(lse))
        g_ref[...] = jnp.where(scores > FLOOR, as_column(c_ref[...]) * (probs - target), 0.0)
        gkt_ref[...] = jnp.zeros_like(gkt_ref)

    q = q_ref[:, pl.ds(pl.multiple_of(dest * width, width), width)]
    q = jnp.concatenate([q[:, j * dim : (j + 1) * dim] for j in range(GROUP)], axis=0)
    d = jnp.dot(q, kt_ref[...], preferred_element_type=jnp.float32)
    g = g_ref[...]
    w = w_ref[dest]
    parts, sums = [], []
    for j in range(GROUP):
        dots = d[j * rows : (j + 1) * rows]
        kept = jnp.where(dots > 0.0, g, 0.0)
        parts.append((kept * (w[:, j : j + 1] * index_scale)).astype(jnp.bfloat16))
        sums.append(as_row(jnp.sum(kept * dots, axis=1, keepdims=True)))
    head_grad = jnp.concatenate(parts, axis=0)
    gq = jnp.dot(head_grad, k_ref[...], preferred_element_type=jnp.float32)
    pad = jnp.zeros((1, width - rows), jnp.float32)
    low = [jnp.concatenate([x * index_scale, pad], axis=1) for x in sums]
    low = jnp.concatenate([*low, jnp.zeros((8 - GROUP, width), jnp.float32)], axis=0)
    gq = jnp.concatenate([gq[j * rows : (j + 1) * rows] for j in range(GROUP)], axis=1)
    gq = jnp.concatenate([gq, low], axis=0)
    gkt_ref[...] += lax.dot_general(q, head_grad, (((0,), (0,)), ((), ())), preferred_element_type=jnp.float32)
    if not last:
        gq_ref[0] = gq

        @pl.when(i == steps - 1)
        def _():
            gk_ref[...] = gkt_ref[...].T.reshape(gk_ref.shape)

        return
    gq = gq + former_ref[dest]

    @pl.when(i < steps // 2)
    def _():
        far_ref[0] = gq

    @pl.when(i >= steps // 2)
    def _():
        near_ref[0] = gq

    @pl.when(i == steps - 1)
    def _():
        turned_ref[...] = gkt_ref[...].T.reshape(turned_ref.shape)
        rounds, lines = len(gk_refs), turned_ref.shape[1]
        for n, ref in enumerate(gk_refs):
            for y in range(ref.shape[0]):
                owner = y * rounds + (place_ref[1] + n) % rounds
                ref[y, :lines] = fk_ref[owner]
                ref[y, lines:] = turned_ref[owner]


def far_first(i, steps, place):
    half = steps // 2
    return 2 * (i % half) + jnp.where(i < half, 1 - place[0], place[0])


def backward(place, t, s, stats, c, q, k, kt, w, part, owners, former=None):
    rows, width = q.shape
    keys, dim = k.shape
    keys = keys // PARTS
    steps = width // (dim * GROUP)
    last = former is not None
    whole = lambda *shape: pl.BlockSpec(shape, lambda i, place: (0,) * len(shape))
    w = jnp.moveaxis(w.reshape(rows, steps, GROUP), 1, 0)
    block, shape = (1, rows + 8, dim * GROUP), (owners, keys // owners, dim)
    array = lambda *shape: jax.ShapeDtypeStruct(shape, jnp.float32)
    in_specs = [
        whole(*t.shape),
        pl.BlockSpec((rows, keys), lambda i, place: (0, part)),
        whole(*stats.shape),
        whole(1, rows),
        whole(rows, width),
        pl.BlockSpec((keys, dim), lambda i, place: (part, 0)),
        pl.BlockSpec((dim, keys), lambda i, place: (0, part)),
        whole(*w.shape),
    ]
    args = [t, s, stats, c, q, k, kt, w]
    scratch = [pltpu.VMEM((rows, keys), jnp.float32), pltpu.VMEM((dim, keys), jnp.float32)]
    if last:
        half = steps // 2
        in_specs += [whole(*former[0].shape), whole(*shape)]
        args += former
        scratch.append(pltpu.VMEM(shape, jnp.float32))
        piece = (owners // ROUNDS, PARTS * shape[1], dim)
        out_specs = [
            pl.BlockSpec(block, lambda i, place: (jnp.minimum(i, half - 1), 0, 0)),
            pl.BlockSpec(block, lambda i, place: (jnp.maximum(i - half, 0), 0, 0)),
        ] + [whole(*piece)] * ROUNDS
        out_shape = [array(half, *block[1:])] * 2 + [array(*piece)] * ROUNDS
    else:
        out_specs = [pl.BlockSpec(block, lambda i, place: (i, 0, 0)), whole(*shape)]
        out_shape = [array(steps, *block[1:]), array(*shape)]
    return pl.pallas_call(
        functools.partial(back_kernel, last),
        grid_spec=pltpu.PrefetchScalarGridSpec(
            num_scalar_prefetch=1, grid=(steps,), in_specs=in_specs, out_specs=out_specs, scratch_shapes=scratch
        ),
        out_shape=out_shape,
        compiler_params=pltpu.CompilerParams(vmem_limit_bytes=VMEM),
        cost_estimate=pl.CostEstimate(
            flops=6 * rows * width * keys, bytes_accessed=4 << 20, transcendentals=rows * keys
        ),
    )(place, *args)


def half_kernel(place_ref, x_ref, own_ref, other_ref):
    mine = place_ref[2]
    total = lambda half: functools.reduce(jnp.add, [x_ref[n, half] for n in range(x_ref.shape[0])])
    own_ref[...] = total(mine)
    other_ref[...] = total(1 - mine)


def halves(place, x):
    vmem = pl.BlockSpec(memory_space=pltpu.VMEM)
    return pl.pallas_call(
        half_kernel,
        in_specs=[pl.BlockSpec(memory_space=pltpu.SMEM), vmem],
        out_specs=[vmem, vmem],
        out_shape=[jax.ShapeDtypeStruct(x.shape[2:], jnp.float32)] * 2,
        compiler_params=pltpu.CompilerParams(vmem_limit_bytes=VMEM),
        name="halves",
    )(place, x)


def end_kernel(x_ref, y_ref, gq_ref, gw_ref):
    rows = gq_ref.shape[0]
    total = x_ref[...] + y_ref[...]
    gq_ref[...] = total[:rows]
    gw_ref[...] = total[rows : rows + GROUP, :rows]


def ended(x, y):
    rows, width = x.shape
    rows -= 8
    return pl.pallas_call(
        end_kernel,
        out_shape=[
            jax.ShapeDtypeStruct((rows, width), jnp.float32),
            jax.ShapeDtypeStruct((GROUP, rows), jnp.float32),
        ],
        compiler_params=pltpu.CompilerParams(vmem_limit_bytes=VMEM),
        name="end",
    )(x, y)


def join_kernel(place_ref, *refs):
    *in_refs, out_ref = refs
    parts, _, rows, _ = out_ref.shape
    rounds = len(in_refs)
    for n, ref in enumerate(in_refs):
        for y in range(ref.shape[0]):
            for p in range(parts):
                owner = y * rounds + (place_ref[1] + rounds - n) % rounds
                out_ref[p, owner] = ref[y, p * rows : (p + 1) * rows]


def joined(place, pieces):
    count, rows, dim = pieces[0].shape
    vmem = pl.BlockSpec(memory_space=pltpu.VMEM)
    return pl.pallas_call(
        join_kernel,
        in_specs=[pl.BlockSpec(memory_space=pltpu.SMEM)] + [vmem] * len(pieces),
        out_specs=vmem,
        out_shape=jax.ShapeDtypeStruct((PARTS, count * len(pieces), rows // PARTS, dim), jnp.float32),
        compiler_params=pltpu.CompilerParams(vmem_limit_bytes=VMEM),
        name="join",
    )(place, *pieces)


def exchanged(x, axis, groups=None):
    return lax.all_to_all(x, axis, 0, 0, axis_index_groups=groups, tiled=True)


def flipped(x, axis, mask):
    return lax.ppermute(x, axis, [(i, i ^ mask) for i in range(lax.axis_size(axis))])


def turned(x, k):
    n = lax.axis_size("head")
    return lax.ppermute(x, "head", [(i, i // ROUNDS * ROUNDS + (i + k) % ROUNDS) for i in range(n)])


def shards(q_latent, k_latent, q_index, k_index, head_weight, loss_weight, query_pos, key_start):
    keys = k_latent.shape[0]
    rows = q_index.shape[0]
    owners, peers = lax.axis_size("head"), lax.axis_size("key")
    at_key, at_head = (lax.axis_index(name).astype(jnp.int32) for name in ("key", "head"))
    base, place = (at_key * keys).reshape(1), jnp.stack([at_key % 2, at_head, at_key // 2 % 2])
    own = at_head * rows
    start, pos = key_start.reshape(1, -1), query_pos.reshape(1, -1)
    own_start = lax.dynamic_slice_in_dim(start, own, rows, axis=1)
    own_pos = lax.dynamic_slice_in_dim(pos, own, rows, axis=1)
    kt_index = k_index.T
    count = jnp.sum((key_start < base + keys) & (query_pos >= base), dtype=jnp.int32)
    info = count.reshape(1)
    e, sel, high, lse = main_forward(base, k_latent.T, jnp.swapaxes(q_latent, 1, 2), start, pos, peers)
    stats = exchanged(lse, "key")
    scores, index_lse = index_forward(base, q_index, kt_index, head_weight, own_start, own_pos, peers)
    index_stats = exchanged(index_lse, "key")
    targets = []
    for part in range(PARTS):
        partial = weighted_sum(info, e, sel, high, stats, owners, part)
        targets.append(exchanged(partial, "head"))

    def back(part, *former):
        fixed = (scores, index_stats, loss_weight.reshape(1, -1), q_index, k_index, kt_index, head_weight)
        return backward(place, targets[part], *fixed, part, owners, *former)

    former = back(0)
    far, near, *pieces = back(1, former)
    moved = flipped(far, "key", 1)
    groups = [list(range(c, peers, 4)) for c in range(4)]
    gq = near + moved
    gq = exchanged(gq.reshape(peers // 4, 2, *gq.shape[1:]), "key", groups)
    pieces = [turned(x, k) if k else x for k, x in enumerate(pieces)]
    gk = sum(pieces[1:], pieces[0])
    gk = gk + flipped(gk, "head", ROUNDS)
    gk = joined(place, [gk] + [turned(gk, k) for k in range(1, ROUNDS)]).reshape(keys, -1)
    mine, other = halves(place, gq)
    gq, gw = ended(mine, flipped(other, "key", 2))
    return (gq, gk, gw.T)


def solution(mesh):
    return jax.shard_map(
        shards,
        mesh=mesh,
        in_specs=(
            P("head", None, None),
            P("key", None),
            P("head", None),
            P("key", None),
            P("head", None),
            P("head"),
            P(),
            P(),
        ),
        out_specs=(P("head", "key"), P("key", None), P("head", "key")),
        check_vma=False,
    )
```

```python
import functools
import math

import jax
import jax.numpy as jnp
from jax import lax
from jax.experimental import pallas as pl
from jax.experimental.pallas import tpu as pltpu
from jax.sharding import PartitionSpec as P


H = 128
QK_DIM = 192
LOG2E = 1.4426950408889634
LOW = -1e30
FLOOR = -1e29
CHUNK = 256
TILE = 256
RUN = 4
GROUP = 4
PARTS = 2
ROUNDS = 4
VMEM = 48 << 20


def eye_of(n):
    rows = lax.broadcasted_iota(jnp.int32, (n, n), 0)
    return rows == lax.broadcasted_iota(jnp.int32, (n, n), 1)


def as_column(row):
    n = row.shape[1]
    return jnp.sum(jnp.where(eye_of(n), row, jnp.zeros_like(row)), axis=1, keepdims=True)


def as_row(column):
    n = column.shape[0]
    return jnp.sum(jnp.where(eye_of(n), column, jnp.zeros_like(column)), axis=0, keepdims=True)


def split_dot(x, onehot, dims, pieces):
    total = 0.0
    for _ in range(pieces):
        high = x.astype(jnp.bfloat16)
        x = x - high.astype(jnp.float32)
        total = total + lax.dot_general(*dims(high, onehot), preferred_element_type=jnp.float32)
    return total


def in_use(t, info):
    return (t == 0) | (info[0] > t * TILE)


def main_kernel(base_ref, kt_ref, q0_ref, *refs):
    qt_refs, refs = refs[:RUN], refs[RUN:]
    start_ref, pos_ref, e_ref, sel_ref, m_ref, lse_ref, k_ref, bias_ref, part_ref, picked_ref, count_ref = refs
    step, steps = pl.program_id(0), pl.num_programs(0)
    heads = part_ref.shape[1]
    tiles = bias_ref.shape[0]
    keys, queries = k_ref.shape[0], start_ref.shape[1]
    chunks = keys // CHUNK
    scale = LOG2E / math.sqrt(QK_DIM)
    first = base_ref[0]

    def pick(t, q):
        return jnp.dot(q, sel_ref[t], preferred_element_type=jnp.float32).astype(jnp.bfloat16)

    def any_seen():
        return (start_ref[...] < first + keys) & (pos_ref[...] >= first)

    @pl.when(step == 0)
    def _():
        k_ref[...] = kt_ref[...].T
        count_ref[0] = jnp.sum(any_seen().astype(jnp.int32))

    def prepare(t):
        seen = any_seen()
        rows = lax.broadcasted_iota(jnp.int32, (queries, queries), 0)
        before = rows < lax.broadcasted_iota(jnp.int32, (queries, queries), 1)
        rank = jnp.dot(
            jnp.broadcast_to(seen.astype(jnp.float32), (8, queries)).astype(jnp.bfloat16),
            before.astype(jnp.bfloat16),
            preferred_element_type=jnp.float32,
        )[0:1]
        rank = as_column(jnp.where(seen, rank, -1.0))
        places = t * TILE + lax.broadcasted_iota(jnp.int32, (queries, TILE), 1)
        chosen = rank == places.astype(jnp.float32)
        sel_ref[t] = chosen.astype(jnp.bfloat16)
        left, right = start_ref[...].astype(jnp.float32), pos_ref[...].astype(jnp.float32) + 1.0
        left = jnp.sum(jnp.where(chosen, as_column(left), 0.0), axis=0, keepdims=True)
        right = jnp.sum(jnp.where(chosen, as_column(right), 0.0), axis=0, keepdims=True)
        s = (first + lax.broadcasted_iota(jnp.int32, (keys, TILE), 0)).astype(jnp.float32)
        bias_ref[t] = jnp.where((s >= left) & (s < right), 0.0, LOW)
        picked_ref[t, 0] = pick(t, q0_ref[0])

    def score(t, n):
        h = step * RUN + n
        qt = picked_ref[t, n % 2]
        highs, sums = [], []
        for c in range(chunks):
            here = pl.ds(c * CHUNK, CHUNK)
            s = jnp.dot(k_ref[here, :], qt, preferred_element_type=jnp.float32)
            if c == chunks - 1:
                picked_ref[t, (n + 1) % 2] = pick(t, qt_refs[n][0])
            s = s * scale + bias_ref[t, here, :]
            high = jnp.maximum(jnp.max(s, axis=0, keepdims=True), FLOOR)
            e = jnp.exp2(s - high)
            e_ref[t, n, here, :] = e.astype(jnp.bfloat16)
            highs.append(high)
            sums.append(jnp.sum(e, axis=0, keepdims=True))
            m_ref[pl.ds((t * heads + h) * chunks + c, 1), :] = high
        top = functools.reduce(jnp.maximum, highs)
        total = sum(l * jnp.exp2(m - top) for l, m in zip(sums, highs))
        part_ref[t, pl.ds(h, 1), :] = jnp.where(total > 0.0, top + jnp.log2(total), 0.0)

    def scores(t):
        for n in range(RUN):
            score(t, n)

    def send(t):
        dims = lambda x, y: (x, y, (((1,), (1,)), ((), ())))
        lse = split_dot(part_ref[t], sel_ref[t], dims, 3)
        lse_ref[...] = jnp.where(any_seen(), lse, FLOOR) if t == 0 else lse_ref[...] + lse

    for t in range(tiles):
        used = in_use(t, count_ref)
        pl.when(used & (step == 0))(functools.partial(prepare, t))
        pl.when(used)(functools.partial(scores, t)) if t else scores(t)
        pl.when(used & (step == steps - 1))(functools.partial(send, t))


def main_forward(base, kt, qt, start, pos):
    heads, lat, queries = qt.shape
    keys = kt.shape[1]
    chunks, tiles = keys // CHUNK, queries // TILE
    whole = lambda *shape: pl.BlockSpec(shape, lambda i, info: (0,) * len(shape))
    later = lambda n, i, info: (jnp.minimum(i * RUN + n, heads - 1), 0, 0)
    return pl.pallas_call(
        main_kernel,
        grid_spec=pltpu.PrefetchScalarGridSpec(
            num_scalar_prefetch=1,
            grid=(heads // RUN,),
            in_specs=[
                whole(lat, keys),
                whole(1, lat, queries),
                *(pl.BlockSpec((1, lat, queries), functools.partial(later, n)) for n in range(1, RUN + 1)),
                whole(1, queries),
                whole(1, queries),
            ],
            out_specs=[
                pl.BlockSpec((tiles, RUN, keys, TILE), lambda i, info: (0, i, 0, 0)),
                whole(tiles, queries, TILE),
                whole(tiles * heads * chunks, TILE),
                whole(heads, queries),
            ],
            scratch_shapes=[
                pltpu.VMEM((keys, lat), jnp.bfloat16),
                pltpu.VMEM((tiles, keys, TILE), jnp.float32),
                pltpu.VMEM((tiles, heads, TILE), jnp.float32),
                pltpu.VMEM((tiles, 2, lat, TILE), jnp.bfloat16),
                pltpu.SMEM((1,), jnp.int32),
            ],
        ),
        out_shape=[
            jax.ShapeDtypeStruct((tiles, heads, keys, TILE), jnp.bfloat16),
            jax.ShapeDtypeStruct((tiles, queries, TILE), jnp.bfloat16),
            jax.ShapeDtypeStruct((tiles * heads * chunks, TILE), jnp.float32),
            jax.ShapeDtypeStruct((heads, queries), jnp.float32),
        ],
        cost_estimate=pl.CostEstimate(
            flops=2 * heads * keys * queries * lat, bytes_accessed=26 << 20, transcendentals=heads * keys * queries
        ),
        name="main_forward",
    )(base, kt, *([qt] * (RUN + 1)), start, pos)


def index_kernel(base_ref, q_ref, kt_ref, w_ref, start_ref, pos_ref, s_ref, lse_ref):
    c = pl.program_id(0)
    rows, width = s_ref.shape[0], CHUNK
    heads = w_ref.shape[1]
    dim = kt_ref.shape[0]
    here = pl.ds(pl.multiple_of(c * width, width), width)
    kt = kt_ref[:, here]
    total = jnp.zeros((rows, width), jnp.float32)
    for j in range(heads):
        d = jnp.dot(q_ref[:, j * dim : (j + 1) * dim], kt, preferred_element_type=jnp.float32)
        total = total + w_ref[:, j : j + 1] * jnp.maximum(d, 0.0)
    s = base_ref[0] + c * width + lax.broadcasted_iota(jnp.int32, (rows, width), 1)
    seen = (s >= as_column(start_ref[...])) & (s <= as_column(pos_ref[...]))
    s_ref[:, here] = jnp.where(seen, total * (LOG2E / math.sqrt(dim)), LOW)

    @pl.when(c == pl.num_programs(0) - 1)
    def _():
        scores = s_ref[...]
        high = jnp.maximum(jnp.max(scores, axis=1, keepdims=True), FLOOR)
        total = jnp.sum(jnp.exp2(scores - high), axis=1, keepdims=True)
        row = as_row(jnp.where(total > 0.0, high + jnp.log2(total), FLOOR))
        row = jnp.concatenate([row, jnp.zeros_like(row)], axis=1)
        lse_ref[...] = jnp.broadcast_to(row[None], lse_ref.shape)


def index_forward(base, q, kt, w, start, pos, peers):
    rows, width = q.shape
    dim, keys = kt.shape
    heads = w.shape[1]
    whole = lambda *shape: pl.BlockSpec(shape, lambda c: (0,) * len(shape))
    return pl.pallas_call(
        index_kernel,
        grid=(keys // CHUNK,),
        in_specs=[
            pl.BlockSpec(memory_space=pltpu.SMEM),
            whole(rows, width),
            whole(dim, keys),
            whole(rows, heads),
            whole(1, rows),
            whole(1, rows),
        ],
        out_specs=[whole(rows, keys), whole(peers, 8, 2 * rows)],
        out_shape=[
            jax.ShapeDtypeStruct((rows, keys), jnp.float32),
            jax.ShapeDtypeStruct((peers, 8, 2 * rows), jnp.float32),
        ],
        cost_estimate=pl.CostEstimate(flops=2 * rows * width * keys, bytes_accessed=2 << 20, transcendentals=rows * keys),
        name="index_forward",
    )(base, q, kt, w, start, pos)


def sum_kernel(first, info_ref, e_ref, sel_ref, m_ref, stats_ref, t_ref, lse_ref):
    c, t = pl.program_id(0), pl.program_id(1)
    _, heads, width, _ = e_ref.shape
    owners, rows, _ = t_ref.shape
    chunks = m_ref.shape[0] // heads // pl.num_programs(1)
    lanes = 128

    @pl.when(in_use(t, info_ref) & (c == 0))
    def _():
        stats = [stats_ref[i] for i in range(stats_ref.shape[0])]
        high = functools.reduce(jnp.maximum, stats)
        lse = high + jnp.log2(sum(jnp.exp2(x - high) for x in stats))
        lse_ref[t] = split_dot(lse, sel_ref[0], lambda x, y: (x, y, (((1,), (0,)), ((), ()))), 3)

    @pl.when(in_use(t, info_ref))
    def _():
        lse = lse_ref[t]
        row = t * heads * chunks + first + c
        weights = [jnp.exp2(m_ref[pl.ds(row + h * chunks, 1), :] - lse[h : h + 1]) for h in range(heads)]
        strips = []
        for r in range(width // lanes):
            at = slice(r * lanes, (r + 1) * lanes)
            total = e_ref[0, 0, at, :].astype(jnp.float32) * weights[0]
            for h in range(1, heads):
                total = total + e_ref[0, h, at, :].astype(jnp.float32) * weights[h]
            strips.append(total)
        total = jnp.concatenate(strips, axis=0)
        dense = split_dot(total, sel_ref[0], lambda x, y: (y, x, (((1,), (1,)), ((), ()))), 2)
        dense = dense.reshape(owners, rows, width)

        @pl.when(t == 0)
        def _():
            t_ref[...] = dense

        @pl.when(t > 0)
        def _():
            t_ref[...] += dense


def weighted_sum(info, e, sel, m, stats, owners, part):
    tiles, heads, keys, tile = e.shape
    queries = sel.shape[1]
    rows = queries // owners
    steps = keys // PARTS // CHUNK
    first = part * steps
    used = lambda t, info: jnp.where(in_use(t, info), t, 0)
    return pl.pallas_call(
        functools.partial(sum_kernel, first),
        grid_spec=pltpu.PrefetchScalarGridSpec(
            num_scalar_prefetch=1,
            grid=(steps, tiles),
            in_specs=[
                pl.BlockSpec((1, heads, CHUNK, tile), lambda c, t, info: (used(t, info), 0, first + c, 0)),
                pl.BlockSpec((1, queries, tile), lambda c, t, info: (used(t, info), 0, 0)),
                pl.BlockSpec(m.shape, lambda c, t, info: (0, 0)),
                pl.BlockSpec(stats.shape, lambda c, t, info: (0, 0, 0)),
            ],
            out_specs=pl.BlockSpec((owners, rows, CHUNK), lambda c, t, info: (0, 0, c)),
            scratch_shapes=[pltpu.VMEM((tiles, heads, tile), jnp.float32)],
        ),
        out_shape=jax.ShapeDtypeStruct((owners, rows, keys // PARTS), jnp.float32),
        compiler_params=pltpu.CompilerParams(vmem_limit_bytes=VMEM),
        cost_estimate=pl.CostEstimate(
            flops=2 * heads * keys * queries // PARTS, bytes_accessed=18 << 19, transcendentals=heads * queries
        ),
    )(info, e, sel, m, stats)


def back_kernel(last, place_ref, t_ref, s_ref, stats_ref, c_ref, q_ref, k_ref, kt_ref, w_ref, *refs):
    if last:
        former_ref, fk_ref, far_ref, near_ref, *gk_refs, g_ref, gkt_ref, turned_ref = refs
    else:
        gq_ref, gk_ref, g_ref, gkt_ref = refs
    i, steps = pl.program_id(0), pl.num_programs(0)
    rows, _ = g_ref.shape
    dim = kt_ref.shape[0]
    width = dim * GROUP
    index_scale = 1.0 / math.sqrt(dim)
    dest = far_first(i, steps, place_ref) if last else i

    @pl.when(i == 0)
    def _():
        target = jnp.sum(t_ref[...], axis=0) * (1.0 / H)
        scores = s_ref[...]
        stats = [stats_ref[n, 0:1, :rows] for n in range(stats_ref.shape[0])]
        high = functools.reduce(jnp.maximum, stats)
        lse = high + jnp.log2(sum(jnp.exp2(x - high) for x in stats))
        probs = jnp.exp2(scores - as_column(lse))
        g_ref[...] = jnp.where(scores > FLOOR, as_column(c_ref[...]) * (probs - target), 0.0)
        gkt_ref[...] = jnp.zeros_like(gkt_ref)

    q = q_ref[:, pl.ds(pl.multiple_of(dest * width, width), width)]
    q = jnp.concatenate([q[:, j * dim : (j + 1) * dim] for j in range(GROUP)], axis=0)
    d = jnp.dot(q, kt_ref[...], preferred_element_type=jnp.float32)
    g = g_ref[...]
    w = w_ref[dest]
    parts, sums = [], []
    for j in range(GROUP):
        dots = d[j * rows : (j + 1) * rows]
        kept = jnp.where(dots > 0.0, g, 0.0)
        parts.append((kept * (w[:, j : j + 1] * index_scale)).astype(jnp.bfloat16))
        sums.append(as_row(jnp.sum(kept * dots, axis=1, keepdims=True)))
    head_grad = jnp.concatenate(parts, axis=0)
    gq = jnp.dot(head_grad, k_ref[...], preferred_element_type=jnp.float32)
    pad = jnp.zeros((1, width - rows), jnp.float32)
    low = [jnp.concatenate([x * index_scale, pad], axis=1) for x in sums]
    low = jnp.concatenate([*low, jnp.zeros((8 - GROUP, width), jnp.float32)], axis=0)
    gq = jnp.concatenate([gq[j * rows : (j + 1) * rows] for j in range(GROUP)], axis=1)
    gq = jnp.concatenate([gq, low], axis=0)
    gkt_ref[...] += lax.dot_general(q, head_grad, (((0,), (0,)), ((), ())), preferred_element_type=jnp.float32)
    if not last:
        gq_ref[0] = gq

        @pl.when(i == steps - 1)
        def _():
            gk_ref[...] = gkt_ref[...].T.reshape(gk_ref.shape)

        return
    gq = gq + former_ref[dest]

    @pl.when(i < steps // 2)
    def _():
        far_ref[0] = gq

    @pl.when(i >= steps // 2)
    def _():
        near_ref[0] = gq

    @pl.when(i == steps - 1)
    def _():
        turned_ref[...] = gkt_ref[...].T.reshape(turned_ref.shape)
        rounds, lines = len(gk_refs), turned_ref.shape[1]
        for n, ref in enumerate(gk_refs):
            for y in range(ref.shape[0]):
                owner = y * rounds + (place_ref[1] + n) % rounds
                ref[y, :lines] = fk_ref[owner]
                ref[y, lines:] = turned_ref[owner]


def far_first(i, steps, place):
    half = steps // 2
    return 2 * (i % half) + jnp.where(i < half, 1 - place[0], place[0])


def backward(place, t, s, stats, c, q, k, kt, w, part, owners, former=None):
    rows, width = q.shape
    keys, dim = k.shape
    keys = keys // PARTS
    steps = width // (dim * GROUP)
    last = former is not None
    whole = lambda *shape: pl.BlockSpec(shape, lambda i, place: (0,) * len(shape))
    w = jnp.moveaxis(w.reshape(rows, steps, GROUP), 1, 0)
    block, shape = (1, rows + 8, dim * GROUP), (owners, keys // owners, dim)
    array = lambda *shape: jax.ShapeDtypeStruct(shape, jnp.float32)
    in_specs = [
        whole(*t.shape),
        pl.BlockSpec((rows, keys), lambda i, place: (0, part)),
        whole(*stats.shape),
        whole(1, rows),
        whole(rows, width),
        pl.BlockSpec((keys, dim), lambda i, place: (part, 0)),
        pl.BlockSpec((dim, keys), lambda i, place: (0, part)),
        whole(*w.shape),
    ]
    args = [t, s, stats, c, q, k, kt, w]
    scratch = [pltpu.VMEM((rows, keys), jnp.float32), pltpu.VMEM((dim, keys), jnp.float32)]
    if last:
        half = steps // 2
        in_specs += [whole(*former[0].shape), whole(*shape)]
        args += former
        scratch.append(pltpu.VMEM(shape, jnp.float32))
        piece = (owners // ROUNDS, PARTS * shape[1], dim)
        out_specs = [
            pl.BlockSpec(block, lambda i, place: (jnp.minimum(i, half - 1), 0, 0)),
            pl.BlockSpec(block, lambda i, place: (jnp.maximum(i - half, 0), 0, 0)),
        ] + [whole(*piece)] * ROUNDS
        out_shape = [array(half, *block[1:])] * 2 + [array(*piece)] * ROUNDS
    else:
        out_specs = [pl.BlockSpec(block, lambda i, place: (i, 0, 0)), whole(*shape)]
        out_shape = [array(steps, *block[1:]), array(*shape)]
    return pl.pallas_call(
        functools.partial(back_kernel, last),
        grid_spec=pltpu.PrefetchScalarGridSpec(
            num_scalar_prefetch=1, grid=(steps,), in_specs=in_specs, out_specs=out_specs, scratch_shapes=scratch
        ),
        out_shape=out_shape,
        compiler_params=pltpu.CompilerParams(vmem_limit_bytes=VMEM),
        cost_estimate=pl.CostEstimate(
            flops=6 * rows * width * keys, bytes_accessed=4 << 20, transcendentals=rows * keys
        ),
    )(place, *args)


def half_kernel(place_ref, x_ref, own_ref, other_ref):
    mine = place_ref[2]
    total = lambda half: functools.reduce(jnp.add, [x_ref[n, half] for n in range(x_ref.shape[0])])
    own_ref[...] = total(mine)
    other_ref[...] = total(1 - mine)


def halves(place, x):
    vmem = pl.BlockSpec(memory_space=pltpu.VMEM)
    return pl.pallas_call(
        half_kernel,
        in_specs=[pl.BlockSpec(memory_space=pltpu.SMEM), vmem],
        out_specs=[vmem, vmem],
        out_shape=[jax.ShapeDtypeStruct(x.shape[2:], jnp.float32)] * 2,
        compiler_params=pltpu.CompilerParams(vmem_limit_bytes=VMEM),
        name="halves",
    )(place, x)


def end_kernel(x_ref, y_ref, gq_ref, gw_ref):
    rows = gq_ref.shape[0]
    total = x_ref[...] + y_ref[...]
    gq_ref[...] = total[:rows]
    gw_ref[...] = total[rows : rows + GROUP, :rows]


def ended(x, y):
    rows, width = x.shape
    rows -= 8
    return pl.pallas_call(
        end_kernel,
        out_shape=[
            jax.ShapeDtypeStruct((rows, width), jnp.float32),
            jax.ShapeDtypeStruct((GROUP, rows), jnp.float32),
        ],
        compiler_params=pltpu.CompilerParams(vmem_limit_bytes=VMEM),
        name="end",
    )(x, y)


def join_kernel(place_ref, *refs):
    *in_refs, out_ref = refs
    parts, _, rows, _ = out_ref.shape
    rounds = len(in_refs)
    for n, ref in enumerate(in_refs):
        for y in range(ref.shape[0]):
            for p in range(parts):
                owner = y * rounds + (place_ref[1] + rounds - n) % rounds
                out_ref[p, owner] = ref[y, p * rows : (p + 1) * rows]


def joined(place, pieces):
    count, rows, dim = pieces[0].shape
    vmem = pl.BlockSpec(memory_space=pltpu.VMEM)
    return pl.pallas_call(
        join_kernel,
        in_specs=[pl.BlockSpec(memory_space=pltpu.SMEM)] + [vmem] * len(pieces),
        out_specs=vmem,
        out_shape=jax.ShapeDtypeStruct((PARTS, count * len(pieces), rows // PARTS, dim), jnp.float32),
        compiler_params=pltpu.CompilerParams(vmem_limit_bytes=VMEM),
        name="join",
    )(place, *pieces)


def exchanged(x, axis, groups=None):
    return lax.all_to_all(x, axis, 0, 0, axis_index_groups=groups, tiled=True)


def flipped(x, axis, mask):
    return lax.ppermute(x, axis, [(i, i ^ mask) for i in range(lax.axis_size(axis))])


def joined_lse(a, b):
    high = jnp.maximum(a, b)
    return high + jnp.log2(jnp.exp2(a - high) + jnp.exp2(b - high))


def turned(x, k):
    n = lax.axis_size("head")
    return lax.ppermute(x, "head", [(i, i // ROUNDS * ROUNDS + (i + k) % ROUNDS) for i in range(n)])


def shards(q_latent, k_latent, q_index, k_index, head_weight, loss_weight, query_pos, key_start):
    keys = k_latent.shape[0]
    rows = q_index.shape[0]
    owners, peers = lax.axis_size("head"), lax.axis_size("key")
    at_key, at_head = (lax.axis_index(name).astype(jnp.int32) for name in ("key", "head"))
    base, place = (at_key * keys).reshape(1), jnp.stack([at_key % 2, at_head, at_key // 2 % 2])
    own = at_head * rows
    start, pos = key_start.reshape(1, -1), query_pos.reshape(1, -1)
    own_start = lax.dynamic_slice_in_dim(start, own, rows, axis=1)
    own_pos = lax.dynamic_slice_in_dim(pos, own, rows, axis=1)
    kt_index = k_index.T
    count = jnp.sum((key_start < base + keys) & (query_pos >= base), dtype=jnp.int32)
    info = count.reshape(1)
    e, sel, high, lse = main_forward(base, k_latent.T, jnp.swapaxes(q_latent, 1, 2), start, pos)
    cores = [list(range(c, peers, 2)) for c in (0, 1)]
    lse = joined_lse(lse, flipped(lse, "key", 1))
    stats = exchanged(jnp.broadcast_to(lse, (peers // 2, *lse.shape)), "key", cores)
    scores, index_lse = index_forward(base, q_index, kt_index, head_weight, own_start, own_pos, peers)
    index_stats = exchanged(index_lse, "key")
    targets = []
    for part in range(PARTS):
        partial = weighted_sum(info, e, sel, high, stats, owners, part)
        targets.append(exchanged(partial, "head"))

    def back(part, *former):
        fixed = (scores, index_stats, loss_weight.reshape(1, -1), q_index, k_index, kt_index, head_weight)
        return backward(place, targets[part], *fixed, part, owners, *former)

    former = back(0)
    far, near, *pieces = back(1, former)
    moved = flipped(far, "key", 1)
    groups = [list(range(c, peers, 4)) for c in range(4)]
    gq = near + moved
    gq = exchanged(gq.reshape(peers // 4, 2, *gq.shape[1:]), "key", groups)
    pieces = [turned(x, k) if k else x for k, x in enumerate(pieces)]
    gk = sum(pieces[1:], pieces[0])
    gk = gk + flipped(gk, "head", ROUNDS)
    gk = joined(place, [gk] + [turned(gk, k) for k in range(1, ROUNDS)]).reshape(keys, -1)
    mine, other = halves(place, gq)
    gq, gw = ended(mine, flipped(other, "key", 2))
    return (gq, gk, gw.T)


def solution(mesh):
    return jax.shard_map(
        shards,
        mesh=mesh,
        in_specs=(
            P("head", None, None),
            P("key", None),
            P("head", None),
            P("key", None),
            P("head", None),
            P("head"),
            P(),
            P(),
        ),
        out_specs=(P("head", "key"), P("key", None), P("head", "key")),
        check_vma=False,
    )
```

```python
import functools
import math

import jax
import jax.numpy as jnp
from jax import lax
from jax.experimental import pallas as pl
from jax.experimental.pallas import tpu as pltpu
from jax.sharding import PartitionSpec as P


H = 128
QK_DIM = 192
LOG2E = 1.4426950408889634
LOW = -1e30
FLOOR = -1e29
CHUNK = 256
TILE = 256
RUN = 4
GROUP = 4
PAIR = 2
PARTS = 2
ROUNDS = 4
VMEM = 48 << 20


def eye_of(n):
    rows = lax.broadcasted_iota(jnp.int32, (n, n), 0)
    return rows == lax.broadcasted_iota(jnp.int32, (n, n), 1)


def as_column(row):
    n = row.shape[1]
    return jnp.sum(jnp.where(eye_of(n), row, jnp.zeros_like(row)), axis=1, keepdims=True)


def as_row(column):
    n = column.shape[0]
    return jnp.sum(jnp.where(eye_of(n), column, jnp.zeros_like(column)), axis=0, keepdims=True)


def split_dot(x, onehot, dims, pieces):
    total = 0.0
    for _ in range(pieces):
        high = x.astype(jnp.bfloat16)
        x = x - high.astype(jnp.float32)
        total = total + lax.dot_general(*dims(high, onehot), preferred_element_type=jnp.float32)
    return total


def in_use(t, info):
    return (t == 0) | (info[0] > t * TILE)


def main_kernel(base_ref, kt_ref, q0_ref, *refs):
    qt_refs, refs = refs[:RUN], refs[RUN:]
    start_ref, pos_ref, e_ref, sel_ref, m_ref, lse_ref, k_ref, bias_ref, part_ref, picked_ref, count_ref = refs
    step, steps = pl.program_id(0), pl.num_programs(0)
    heads = part_ref.shape[1]
    tiles = bias_ref.shape[0]
    keys, queries = k_ref.shape[0], start_ref.shape[1]
    chunks = keys // CHUNK
    scale = LOG2E / math.sqrt(QK_DIM)
    first = base_ref[0]

    def pick(t, q):
        return jnp.dot(q, sel_ref[t], preferred_element_type=jnp.float32).astype(jnp.bfloat16)

    def any_seen():
        return (start_ref[...] < first + keys) & (pos_ref[...] >= first)

    @pl.when(step == 0)
    def _():
        k_ref[...] = kt_ref[...].T
        count_ref[0] = jnp.sum(any_seen().astype(jnp.int32))

    def prepare(t):
        seen = any_seen()
        rows = lax.broadcasted_iota(jnp.int32, (queries, queries), 0)
        before = rows < lax.broadcasted_iota(jnp.int32, (queries, queries), 1)
        rank = jnp.dot(
            jnp.broadcast_to(seen.astype(jnp.float32), (8, queries)).astype(jnp.bfloat16),
            before.astype(jnp.bfloat16),
            preferred_element_type=jnp.float32,
        )[0:1]
        rank = as_column(jnp.where(seen, rank, -1.0))
        places = t * TILE + lax.broadcasted_iota(jnp.int32, (queries, TILE), 1)
        chosen = rank == places.astype(jnp.float32)
        sel_ref[t] = chosen.astype(jnp.bfloat16)
        left, right = start_ref[...].astype(jnp.float32), pos_ref[...].astype(jnp.float32) + 1.0
        left = jnp.sum(jnp.where(chosen, as_column(left), 0.0), axis=0, keepdims=True)
        right = jnp.sum(jnp.where(chosen, as_column(right), 0.0), axis=0, keepdims=True)
        s = (first + lax.broadcasted_iota(jnp.int32, (keys, TILE), 0)).astype(jnp.float32)
        bias_ref[t] = jnp.where((s >= left) & (s < right), 0.0, LOW)
        picked_ref[t, 0] = pick(t, q0_ref[0])

    def score(t, n):
        h = step * RUN + n
        qt = picked_ref[t, n % 2]
        highs, sums = [], []
        for c in range(chunks):
            here = pl.ds(c * CHUNK, CHUNK)
            s = jnp.dot(k_ref[here, :], qt, preferred_element_type=jnp.float32)
            if c == chunks - 1:
                picked_ref[t, (n + 1) % 2] = pick(t, qt_refs[n][0])
            s = s * scale + bias_ref[t, here, :]
            high = jnp.maximum(jnp.max(s, axis=0, keepdims=True), FLOOR)
            e = jnp.exp2(s - high)
            e_ref[t, n, here, :] = e.astype(jnp.bfloat16)
            highs.append(high)
            sums.append(jnp.sum(e, axis=0, keepdims=True))
            m_ref[pl.ds((t * heads + h) * chunks + c, 1), :] = high
        top = functools.reduce(jnp.maximum, highs)
        total = sum(l * jnp.exp2(m - top) for l, m in zip(sums, highs))
        part_ref[t, pl.ds(h, 1), :] = jnp.where(total > 0.0, top + jnp.log2(total), 0.0)

    def scores(t):
        for n in range(RUN):
            score(t, n)

    def send(t):
        dims = lambda x, y: (x, y, (((1,), (1,)), ((), ())))
        lse = split_dot(part_ref[t], sel_ref[t], dims, 3)
        lse = jnp.where(any_seen(), lse, FLOOR) if t == 0 else lse_ref[0] + lse
        for i in range(lse_ref.shape[0]):
            lse_ref[i] = lse

    for t in range(tiles):
        used = in_use(t, count_ref)
        pl.when(used & (step == 0))(functools.partial(prepare, t))
        pl.when(used)(functools.partial(scores, t)) if t else scores(t)
        pl.when(used & (step == steps - 1))(functools.partial(send, t))


def main_forward(base, kt, qt, start, pos, peers):
    heads, lat, queries = qt.shape
    keys = kt.shape[1]
    chunks, tiles = keys // CHUNK, queries // TILE
    whole = lambda *shape: pl.BlockSpec(shape, lambda i, info: (0,) * len(shape))
    later = lambda n, i, info: (jnp.minimum(i * RUN + n, heads - 1), 0, 0)
    return pl.pallas_call(
        main_kernel,
        grid_spec=pltpu.PrefetchScalarGridSpec(
            num_scalar_prefetch=1,
            grid=(heads // RUN,),
            in_specs=[
                whole(lat, keys),
                whole(1, lat, queries),
                *(pl.BlockSpec((1, lat, queries), functools.partial(later, n)) for n in range(1, RUN + 1)),
                whole(1, queries),
                whole(1, queries),
            ],
            out_specs=[
                pl.BlockSpec((tiles, RUN, keys, TILE), lambda i, info: (0, i, 0, 0)),
                whole(tiles, queries, TILE),
                whole(tiles * heads * chunks, TILE),
                whole(peers, heads, queries),
            ],
            scratch_shapes=[
                pltpu.VMEM((keys, lat), jnp.bfloat16),
                pltpu.VMEM((tiles, keys, TILE), jnp.float32),
                pltpu.VMEM((tiles, heads, TILE), jnp.float32),
                pltpu.VMEM((tiles, 2, lat, TILE), jnp.bfloat16),
                pltpu.SMEM((1,), jnp.int32),
            ],
        ),
        out_shape=[
            jax.ShapeDtypeStruct((tiles, heads, keys, TILE), jnp.bfloat16),
            jax.ShapeDtypeStruct((tiles, queries, TILE), jnp.bfloat16),
            jax.ShapeDtypeStruct((tiles * heads * chunks, TILE), jnp.float32),
            jax.ShapeDtypeStruct((peers, heads, queries), jnp.float32),
        ],
        cost_estimate=pl.CostEstimate(
            flops=2 * heads * keys * queries * lat, bytes_accessed=26 << 20, transcendentals=heads * keys * queries
        ),
        name="main_forward",
    )(base, kt, *([qt] * (RUN + 1)), start, pos)


def index_kernel(base_ref, q_ref, kt_ref, w_ref, start_ref, pos_ref, s_ref, lse_ref):
    c = pl.program_id(0)
    rows, width = s_ref.shape[0], CHUNK
    heads = w_ref.shape[1]
    dim = kt_ref.shape[0]
    here = pl.ds(pl.multiple_of(c * width, width), width)
    kt = kt_ref[:, here]
    total = jnp.zeros((rows, width), jnp.float32)
    for j in range(heads):
        d = jnp.dot(q_ref[:, j * dim : (j + 1) * dim], kt, preferred_element_type=jnp.float32)
        total = total + w_ref[:, j : j + 1] * jnp.maximum(d, 0.0)
    s = base_ref[0] + c * width + lax.broadcasted_iota(jnp.int32, (rows, width), 1)
    seen = (s >= as_column(start_ref[...])) & (s <= as_column(pos_ref[...]))
    s_ref[:, here] = jnp.where(seen, total * (LOG2E / math.sqrt(dim)), LOW)

    @pl.when(c == pl.num_programs(0) - 1)
    def _():
        scores = s_ref[...]
        high = jnp.maximum(jnp.max(scores, axis=1, keepdims=True), FLOOR)
        total = jnp.sum(jnp.exp2(scores - high), axis=1, keepdims=True)
        row = as_row(jnp.where(total > 0.0, high + jnp.log2(total), FLOOR))
        row = jnp.concatenate([row, jnp.zeros_like(row)], axis=1)
        lse_ref[...] = jnp.broadcast_to(row[None], lse_ref.shape)


def index_forward(base, q, kt, w, start, pos, peers):
    rows, width = q.shape
    dim, keys = kt.shape
    heads = w.shape[1]
    whole = lambda *shape: pl.BlockSpec(shape, lambda c: (0,) * len(shape))
    return pl.pallas_call(
        index_kernel,
        grid=(keys // CHUNK,),
        in_specs=[
            pl.BlockSpec(memory_space=pltpu.SMEM),
            whole(rows, width),
            whole(dim, keys),
            whole(rows, heads),
            whole(1, rows),
            whole(1, rows),
        ],
        out_specs=[whole(rows, keys), whole(peers, 8, 2 * rows)],
        out_shape=[
            jax.ShapeDtypeStruct((rows, keys), jnp.float32),
            jax.ShapeDtypeStruct((peers, 8, 2 * rows), jnp.float32),
        ],
        cost_estimate=pl.CostEstimate(flops=2 * rows * width * keys, bytes_accessed=2 << 20, transcendentals=rows * keys),
        name="index_forward",
    )(base, q, kt, w, start, pos)


def sum_kernel(first, info_ref, e_ref, sel_ref, m_ref, stats_ref, t_ref, lse_ref):
    c, t = pl.program_id(0), pl.program_id(1)
    _, heads, width, _ = e_ref.shape
    owners, rows, _ = t_ref.shape
    chunks = m_ref.shape[0] // heads // pl.num_programs(1)
    lanes = 128

    @pl.when(in_use(t, info_ref) & (c == 0))
    def _():
        stats = [stats_ref[i] for i in range(stats_ref.shape[0])]
        high = functools.reduce(jnp.maximum, stats)
        lse = high + jnp.log2(sum(jnp.exp2(x - high) for x in stats))
        lse_ref[t] = split_dot(lse, sel_ref[0], lambda x, y: (x, y, (((1,), (0,)), ((), ()))), 3)

    @pl.when(in_use(t, info_ref))
    def _():
        lse = lse_ref[t]
        row = t * heads * chunks + first + c
        weights = [jnp.exp2(m_ref[pl.ds(row + h * chunks, 1), :] - lse[h : h + 1]) for h in range(heads)]
        strips = []
        for r in range(width // lanes):
            at = slice(r * lanes, (r + 1) * lanes)
            total = e_ref[0, 0, at, :].astype(jnp.float32) * weights[0]
            for h in range(1, heads):
                total = total + e_ref[0, h, at, :].astype(jnp.float32) * weights[h]
            strips.append(total)
        total = jnp.concatenate(strips, axis=0)
        dense = split_dot(total, sel_ref[0], lambda x, y: (y, x, (((1,), (1,)), ((), ()))), 2)
        dense = dense.reshape(owners, rows, width)

        @pl.when(t == 0)
        def _():
            t_ref[...] = dense

        @pl.when(t > 0)
        def _():
            t_ref[...] += dense


def weighted_sum(info, e, sel, m, stats, owners, part):
    tiles, heads, keys, tile = e.shape
    queries = sel.shape[1]
    rows = queries // owners
    steps = keys // PARTS // CHUNK
    first = part * steps
    used = lambda t, info: jnp.where(in_use(t, info), t, 0)
    return pl.pallas_call(
        functools.partial(sum_kernel, first),
        grid_spec=pltpu.PrefetchScalarGridSpec(
            num_scalar_prefetch=1,
            grid=(steps, tiles),
            in_specs=[
                pl.BlockSpec((1, heads, CHUNK, tile), lambda c, t, info: (used(t, info), 0, first + c, 0)),
                pl.BlockSpec((1, queries, tile), lambda c, t, info: (used(t, info), 0, 0)),
                pl.BlockSpec(m.shape, lambda c, t, info: (0, 0)),
                pl.BlockSpec(stats.shape, lambda c, t, info: (0, 0, 0)),
            ],
            out_specs=pl.BlockSpec((owners, rows, CHUNK), lambda c, t, info: (0, 0, c)),
            scratch_shapes=[pltpu.VMEM((tiles, heads, tile), jnp.float32)],
        ),
        out_shape=jax.ShapeDtypeStruct((owners, rows, keys // PARTS), jnp.float32),
        compiler_params=pltpu.CompilerParams(vmem_limit_bytes=VMEM),
        cost_estimate=pl.CostEstimate(
            flops=2 * heads * keys * queries // PARTS, bytes_accessed=18 << 19, transcendentals=heads * queries
        ),
    )(info, e, sel, m, stats)


def back_kernel(last, place_ref, t_ref, s_ref, stats_ref, c_ref, q_ref, k_ref, kt_ref, w_ref, *refs):
    if last:
        former_ref, fk_ref, far_ref, near_ref, *gk_refs, g_ref, gkt_ref, turned_ref = refs
    else:
        gq_ref, gk_ref, g_ref, gkt_ref = refs
    i, steps = pl.program_id(0), pl.num_programs(0)
    rows, _ = g_ref.shape
    dim = kt_ref.shape[0]
    width = dim * GROUP
    index_scale = 1.0 / math.sqrt(dim)

    @pl.when(i == 0)
    def _():
        target = jnp.sum(t_ref[...], axis=0) * (1.0 / H)
        scores = s_ref[...]
        stats = [stats_ref[n, 0:1, :rows] for n in range(stats_ref.shape[0])]
        high = functools.reduce(jnp.maximum, stats)
        lse = high + jnp.log2(sum(jnp.exp2(x - high) for x in stats))
        probs = jnp.exp2(scores - as_column(lse))
        g_ref[...] = jnp.where(scores > FLOOR, as_column(c_ref[...]) * (probs - target), 0.0)
        gkt_ref[...] = jnp.zeros_like(gkt_ref)

    g = g_ref[...]
    blocks, keys_total = [], gkt_ref[...]
    for n in range(PAIR):
        dest = far_first(i * PAIR + n, steps * PAIR, place_ref) if last else i * PAIR + n
        q = q_ref[:, pl.ds(pl.multiple_of(dest * width, width), width)]
        q = jnp.concatenate([q[:, j * dim : (j + 1) * dim] for j in range(GROUP)], axis=0)
        d = jnp.dot(q, kt_ref[...], preferred_element_type=jnp.float32)
        w = w_ref[dest]
        parts, sums = [], []
        for j in range(GROUP):
            dots = d[j * rows : (j + 1) * rows]
            kept = jnp.where(dots > 0.0, g, 0.0)
            parts.append((kept * (w[:, j : j + 1] * index_scale)).astype(jnp.bfloat16))
            sums.append(as_row(jnp.sum(kept * dots, axis=1, keepdims=True)))
        head_grad = jnp.concatenate(parts, axis=0)
        gq = jnp.dot(head_grad, k_ref[...], preferred_element_type=jnp.float32)
        pad = jnp.zeros((1, width - rows), jnp.float32)
        low = [jnp.concatenate([x * index_scale, pad], axis=1) for x in sums]
        low = jnp.concatenate([*low, jnp.zeros((8 - GROUP, width), jnp.float32)], axis=0)
        gq = jnp.concatenate([gq[j * rows : (j + 1) * rows] for j in range(GROUP)], axis=1)
        gq = jnp.concatenate([gq, low], axis=0)
        keys_total = keys_total + lax.dot_general(
            q, head_grad, (((0,), (0,)), ((), ())), preferred_element_type=jnp.float32
        )
        blocks.append(gq + former_ref[dest] if last else gq)
    gkt_ref[...] = keys_total
    if not last:
        for n in range(PAIR):
            gq_ref[n] = blocks[n]

        @pl.when(i == steps - 1)
        def _():
            gk_ref[...] = gkt_ref[...].T.reshape(gk_ref.shape)

        return

    @pl.when(i < steps // 2)
    def _():
        for n in range(PAIR):
            far_ref[n] = blocks[n]

    @pl.when(i >= steps // 2)
    def _():
        for n in range(PAIR):
            near_ref[n] = blocks[n]

    @pl.when(i == steps - 1)
    def _():
        turned_ref[...] = gkt_ref[...].T.reshape(turned_ref.shape)
        rounds, lines = len(gk_refs), turned_ref.shape[1]
        for n, ref in enumerate(gk_refs):
            for y in range(ref.shape[0]):
                owner = y * rounds + (place_ref[1] + n) % rounds
                ref[y, :lines] = fk_ref[owner]
                ref[y, lines:] = turned_ref[owner]


def far_first(i, steps, place):
    half = steps // 2
    return 2 * (i % half) + jnp.where(i < half, 1 - place[0], place[0])


def backward(place, t, s, stats, c, q, k, kt, w, part, owners, former=None):
    rows, width = q.shape
    keys, dim = k.shape
    keys = keys // PARTS
    blocks = width // (dim * GROUP)
    steps = blocks // PAIR
    last = former is not None
    whole = lambda *shape: pl.BlockSpec(shape, lambda i, place: (0,) * len(shape))
    w = jnp.moveaxis(w.reshape(rows, blocks, GROUP), 1, 0)
    block, shape = (PAIR, rows + 8, dim * GROUP), (owners, keys // owners, dim)
    array = lambda *shape: jax.ShapeDtypeStruct(shape, jnp.float32)
    in_specs = [
        whole(*t.shape),
        pl.BlockSpec((rows, keys), lambda i, place: (0, part)),
        whole(*stats.shape),
        whole(1, rows),
        whole(rows, width),
        pl.BlockSpec((keys, dim), lambda i, place: (part, 0)),
        pl.BlockSpec((dim, keys), lambda i, place: (0, part)),
        whole(*w.shape),
    ]
    args = [t, s, stats, c, q, k, kt, w]
    scratch = [pltpu.VMEM((rows, keys), jnp.float32), pltpu.VMEM((dim, keys), jnp.float32)]
    if last:
        half = steps // 2
        in_specs += [whole(*former[0].shape), whole(*shape)]
        args += former
        scratch.append(pltpu.VMEM(shape, jnp.float32))
        piece = (owners // ROUNDS, PARTS * shape[1], dim)
        out_specs = [
            pl.BlockSpec(block, lambda i, place: (jnp.minimum(i, half - 1), 0, 0)),
            pl.BlockSpec(block, lambda i, place: (jnp.maximum(i - half, 0), 0, 0)),
        ] + [whole(*piece)] * ROUNDS
        out_shape = [array(blocks // 2, *block[1:])] * 2 + [array(*piece)] * ROUNDS
    else:
        out_specs = [pl.BlockSpec(block, lambda i, place: (i, 0, 0)), whole(*shape)]
        out_shape = [array(blocks, *block[1:]), array(*shape)]
    return pl.pallas_call(
        functools.partial(back_kernel, last),
        grid_spec=pltpu.PrefetchScalarGridSpec(
            num_scalar_prefetch=1, grid=(steps,), in_specs=in_specs, out_specs=out_specs, scratch_shapes=scratch
        ),
        out_shape=out_shape,
        compiler_params=pltpu.CompilerParams(vmem_limit_bytes=VMEM),
        cost_estimate=pl.CostEstimate(
            flops=6 * rows * width * keys, bytes_accessed=4 << 20, transcendentals=rows * keys
        ),
    )(place, *args)


def half_kernel(place_ref, x_ref, own_ref, other_ref):
    mine = place_ref[2]
    total = lambda half: functools.reduce(jnp.add, [x_ref[n, half] for n in range(x_ref.shape[0])])
    own_ref[...] = total(mine)
    other_ref[...] = total(1 - mine)


def halves(place, x):
    vmem = pl.BlockSpec(memory_space=pltpu.VMEM)
    return pl.pallas_call(
        half_kernel,
        in_specs=[pl.BlockSpec(memory_space=pltpu.SMEM), vmem],
        out_specs=[vmem, vmem],
        out_shape=[jax.ShapeDtypeStruct(x.shape[2:], jnp.float32)] * 2,
        compiler_params=pltpu.CompilerParams(vmem_limit_bytes=VMEM),
        name="halves",
    )(place, x)


def end_kernel(x_ref, y_ref, gq_ref, gw_ref):
    rows = gq_ref.shape[0]
    total = x_ref[...] + y_ref[...]
    gq_ref[...] = total[:rows]
    gw_ref[...] = total[rows : rows + GROUP, :rows]


def ended(x, y):
    rows, width = x.shape
    rows -= 8
    return pl.pallas_call(
        end_kernel,
        out_shape=[
            jax.ShapeDtypeStruct((rows, width), jnp.float32),
            jax.ShapeDtypeStruct((GROUP, rows), jnp.float32),
        ],
        compiler_params=pltpu.CompilerParams(vmem_limit_bytes=VMEM),
        name="end",
    )(x, y)


def join_kernel(place_ref, *refs):
    *in_refs, out_ref = refs
    parts, _, rows, _ = out_ref.shape
    rounds = len(in_refs)
    for n, ref in enumerate(in_refs):
        for y in range(ref.shape[0]):
            for p in range(parts):
                owner = y * rounds + (place_ref[1] + rounds - n) % rounds
                out_ref[p, owner] = ref[y, p * rows : (p + 1) * rows]


def joined(place, pieces):
    count, rows, dim = pieces[0].shape
    vmem = pl.BlockSpec(memory_space=pltpu.VMEM)
    return pl.pallas_call(
        join_kernel,
        in_specs=[pl.BlockSpec(memory_space=pltpu.SMEM)] + [vmem] * len(pieces),
        out_specs=vmem,
        out_shape=jax.ShapeDtypeStruct((PARTS, count * len(pieces), rows // PARTS, dim), jnp.float32),
        compiler_params=pltpu.CompilerParams(vmem_limit_bytes=VMEM),
        name="join",
    )(place, *pieces)


def exchanged(x, axis, groups=None):
    return lax.all_to_all(x, axis, 0, 0, axis_index_groups=groups, tiled=True)


def flipped(x, axis, mask):
    return lax.ppermute(x, axis, [(i, i ^ mask) for i in range(lax.axis_size(axis))])


def turned(x, k):
    n = lax.axis_size("head")
    return lax.ppermute(x, "head", [(i, i // ROUNDS * ROUNDS + (i + k) % ROUNDS) for i in range(n)])


def shards(q_latent, k_latent, q_index, k_index, head_weight, loss_weight, query_pos, key_start):
    keys = k_latent.shape[0]
    rows = q_index.shape[0]
    owners, peers = lax.axis_size("head"), lax.axis_size("key")
    at_key, at_head = (lax.axis_index(name).astype(jnp.int32) for name in ("key", "head"))
    base, place = (at_key * keys).reshape(1), jnp.stack([at_key % 2, at_head, at_key // 2 % 2])
    own = at_head * rows
    start, pos = key_start.reshape(1, -1), query_pos.reshape(1, -1)
    own_start = lax.dynamic_slice_in_dim(start, own, rows, axis=1)
    own_pos = lax.dynamic_slice_in_dim(pos, own, rows, axis=1)
    kt_index = k_index.T
    count = jnp.sum((key_start < base + keys) & (query_pos >= base), dtype=jnp.int32)
    info = count.reshape(1)
    e, sel, high, lse = main_forward(base, k_latent.T, jnp.swapaxes(q_latent, 1, 2), start, pos, peers)
    stats = exchanged(lse, "key")
    scores, index_lse = index_forward(base, q_index, kt_index, head_weight, own_start, own_pos, peers)
    index_stats = exchanged(index_lse, "key")
    targets = []
    for part in range(PARTS):
        partial = weighted_sum(info, e, sel, high, stats, owners, part)
        targets.append(exchanged(partial, "head"))

    def back(part, *former):
        fixed = (scores, index_stats, loss_weight.reshape(1, -1), q_index, k_index, kt_index, head_weight)
        return backward(place, targets[part], *fixed, part, owners, *former)

    former = back(0)
    far, near, *pieces = back(1, former)
    moved = flipped(far, "key", 1)
    groups = [list(range(c, peers, 4)) for c in range(4)]
    gq = near + moved
    gq = exchanged(gq.reshape(peers // 4, 2, *gq.shape[1:]), "key", groups)
    pieces = [turned(x, k) if k else x for k, x in enumerate(pieces)]
    gk = sum(pieces[1:], pieces[0])
    gk = gk + flipped(gk, "head", ROUNDS)
    gk = joined(place, [gk] + [turned(gk, k) for k in range(1, ROUNDS)]).reshape(keys, -1)
    mine, other = halves(place, gq)
    other = flipped(other, "key", 2)
    gq, gw = ended(mine, other)
    return (gq, gk, gw.T)


def solution(mesh):
    return jax.shard_map(
        shards,
        mesh=mesh,
        in_specs=(
            P("head", None, None),
            P("key", None),
            P("head", None),
            P("key", None),
            P("head", None),
            P("head"),
            P(),
            P(),
        ),
        out_specs=(P("head", "key"), P("key", None), P("head", "key")),
        check_vma=False,
    )
```

```python
import functools
import math

import jax
import jax.numpy as jnp
from jax import lax
from jax.experimental import pallas as pl
from jax.experimental.pallas import tpu as pltpu
from jax.sharding import PartitionSpec as P


H = 128
QK_DIM = 192
LOG2E = 1.4426950408889634
LOW = -1e30
FLOOR = -1e29
CHUNK = 256
TILE = 256
RUN = 4
GROUP = 4
PAIR = 2
PARTS = 2
ROUNDS = 4
VMEM = 48 << 20


def eye_of(n):
    rows = lax.broadcasted_iota(jnp.int32, (n, n), 0)
    return rows == lax.broadcasted_iota(jnp.int32, (n, n), 1)


def as_column(row):
    n = row.shape[1]
    return jnp.sum(jnp.where(eye_of(n), row, jnp.zeros_like(row)), axis=1, keepdims=True)


def as_row(column):
    n = column.shape[0]
    return jnp.sum(jnp.where(eye_of(n), column, jnp.zeros_like(column)), axis=0, keepdims=True)


def split_dot(x, onehot, dims, pieces):
    total = 0.0
    for _ in range(pieces):
        high = x.astype(jnp.bfloat16)
        x = x - high.astype(jnp.float32)
        total = total + lax.dot_general(*dims(high, onehot), preferred_element_type=jnp.float32)
    return total


def in_use(t, info):
    return (t == 0) | (info[0] > t * TILE)


def main_kernel(base_ref, kt_ref, q0_ref, *refs):
    qt_refs, refs = refs[:RUN], refs[RUN:]
    start_ref, pos_ref, e_ref, sel_ref, m_ref, lse_ref, k_ref, bias_ref, part_ref, picked_ref, count_ref = refs
    step, steps = pl.program_id(0), pl.num_programs(0)
    heads = part_ref.shape[1]
    tiles = bias_ref.shape[0]
    keys, queries = k_ref.shape[0], start_ref.shape[1]
    chunks = keys // CHUNK
    scale = LOG2E / math.sqrt(QK_DIM)
    first = base_ref[0]

    def pick(t, q):
        return jnp.dot(q, sel_ref[t], preferred_element_type=jnp.float32).astype(jnp.bfloat16)

    def any_seen():
        return (start_ref[...] < first + keys) & (pos_ref[...] >= first)

    @pl.when(step == 0)
    def _():
        k_ref[...] = kt_ref[...].T
        count_ref[0] = jnp.sum(any_seen().astype(jnp.int32))

    def prepare(t):
        seen = any_seen()
        rows = lax.broadcasted_iota(jnp.int32, (queries, queries), 0)
        before = rows < lax.broadcasted_iota(jnp.int32, (queries, queries), 1)
        rank = jnp.dot(
            jnp.broadcast_to(seen.astype(jnp.float32), (8, queries)).astype(jnp.bfloat16),
            before.astype(jnp.bfloat16),
            preferred_element_type=jnp.float32,
        )[0:1]
        rank = as_column(jnp.where(seen, rank, -1.0))
        places = t * TILE + lax.broadcasted_iota(jnp.int32, (queries, TILE), 1)
        chosen = rank == places.astype(jnp.float32)
        sel_ref[t] = chosen.astype(jnp.bfloat16)
        left, right = start_ref[...].astype(jnp.float32), pos_ref[...].astype(jnp.float32) + 1.0
        left = jnp.sum(jnp.where(chosen, as_column(left), 0.0), axis=0, keepdims=True)
        right = jnp.sum(jnp.where(chosen, as_column(right), 0.0), axis=0, keepdims=True)
        s = (first + lax.broadcasted_iota(jnp.int32, (keys, TILE), 0)).astype(jnp.float32)
        bias_ref[t] = jnp.where((s >= left) & (s < right), 0.0, LOW)
        picked_ref[t, 0] = pick(t, q0_ref[0])

    def score(t, n):
        h = step * RUN + n
        qt = picked_ref[t, n % 2]
        highs, sums = [], []
        for c in range(chunks):
            here = pl.ds(c * CHUNK, CHUNK)
            s = jnp.dot(k_ref[here, :], qt, preferred_element_type=jnp.float32)
            if c == chunks - 1:
                picked_ref[t, (n + 1) % 2] = pick(t, qt_refs[n][0])
            s = s * scale + bias_ref[t, here, :]
            high = jnp.maximum(jnp.max(s, axis=0, keepdims=True), FLOOR)
            e = jnp.exp2(s - high)
            e_ref[t, n, here, :] = e.astype(jnp.bfloat16)
            highs.append(high)
            sums.append(jnp.sum(e, axis=0, keepdims=True))
            m_ref[pl.ds((t * heads + h) * chunks + c, 1), :] = high
        top = functools.reduce(jnp.maximum, highs)
        total = sum(l * jnp.exp2(m - top) for l, m in zip(sums, highs))
        part_ref[t, pl.ds(h, 1), :] = jnp.where(total > 0.0, top + jnp.log2(total), 0.0)

    def scores(t):
        for n in range(RUN):
            score(t, n)

    def send(t):
        dims = lambda x, y: (x, y, (((1,), (1,)), ((), ())))
        lse = split_dot(part_ref[t], sel_ref[t], dims, 3)
        lse = jnp.where(any_seen(), lse, FLOOR) if t == 0 else lse_ref[0] + lse
        for i in range(lse_ref.shape[0]):
            lse_ref[i] = lse

    for t in range(tiles):
        used = in_use(t, count_ref)
        pl.when(used & (step == 0))(functools.partial(prepare, t))
        pl.when(used)(functools.partial(scores, t)) if t else scores(t)
        pl.when(used & (step == steps - 1))(functools.partial(send, t))


def main_forward(base, kt, qt, start, pos, peers):
    heads, lat, queries = qt.shape
    keys = kt.shape[1]
    chunks, tiles = keys // CHUNK, queries // TILE
    whole = lambda *shape: pl.BlockSpec(shape, lambda i, info: (0,) * len(shape))
    later = lambda n, i, info: (jnp.minimum(i * RUN + n, heads - 1), 0, 0)
    return pl.pallas_call(
        main_kernel,
        grid_spec=pltpu.PrefetchScalarGridSpec(
            num_scalar_prefetch=1,
            grid=(heads // RUN,),
            in_specs=[
                whole(lat, keys),
                whole(1, lat, queries),
                *(pl.BlockSpec((1, lat, queries), functools.partial(later, n)) for n in range(1, RUN + 1)),
                whole(1, queries),
                whole(1, queries),
            ],
            out_specs=[
                pl.BlockSpec((tiles, RUN, keys, TILE), lambda i, info: (0, i, 0, 0)),
                whole(tiles, queries, TILE),
                whole(tiles * heads * chunks, TILE),
                whole(peers, heads, queries),
            ],
            scratch_shapes=[
                pltpu.VMEM((keys, lat), jnp.bfloat16),
                pltpu.VMEM((tiles, keys, TILE), jnp.float32),
                pltpu.VMEM((tiles, heads, TILE), jnp.float32),
                pltpu.VMEM((tiles, 2, lat, TILE), jnp.bfloat16),
                pltpu.SMEM((1,), jnp.int32),
            ],
        ),
        out_shape=[
            jax.ShapeDtypeStruct((tiles, heads, keys, TILE), jnp.bfloat16),
            jax.ShapeDtypeStruct((tiles, queries, TILE), jnp.bfloat16),
            jax.ShapeDtypeStruct((tiles * heads * chunks, TILE), jnp.float32),
            jax.ShapeDtypeStruct((peers, heads, queries), jnp.float32),
        ],
        cost_estimate=pl.CostEstimate(
            flops=2 * heads * keys * queries * lat, bytes_accessed=26 << 20, transcendentals=heads * keys * queries
        ),
        name="main_forward",
    )(base, kt, *([qt] * (RUN + 1)), start, pos)


def index_kernel(base_ref, q_ref, kt_ref, w_ref, start_ref, pos_ref, s_ref, lse_ref):
    c = pl.program_id(0)
    rows, width = s_ref.shape[0], CHUNK
    heads = w_ref.shape[1]
    dim = kt_ref.shape[0]
    here = pl.ds(pl.multiple_of(c * width, width), width)
    kt = kt_ref[:, here]
    total = jnp.zeros((rows, width), jnp.float32)
    for j in range(heads):
        d = jnp.dot(q_ref[:, j * dim : (j + 1) * dim], kt, preferred_element_type=jnp.float32)
        total = total + w_ref[:, j : j + 1] * jnp.maximum(d, 0.0)
    s = base_ref[0] + c * width + lax.broadcasted_iota(jnp.int32, (rows, width), 1)
    seen = (s >= as_column(start_ref[...])) & (s <= as_column(pos_ref[...]))
    s_ref[:, here] = jnp.where(seen, total * (LOG2E / math.sqrt(dim)), LOW)

    @pl.when(c == pl.num_programs(0) - 1)
    def _():
        scores = s_ref[...]
        high = jnp.maximum(jnp.max(scores, axis=1, keepdims=True), FLOOR)
        total = jnp.sum(jnp.exp2(scores - high), axis=1, keepdims=True)
        row = as_row(jnp.where(total > 0.0, high + jnp.log2(total), FLOOR))
        lse_ref[...] = row


def index_forward(base, q, kt, w, start, pos):
    rows, width = q.shape
    dim, keys = kt.shape
    heads = w.shape[1]
    whole = lambda *shape: pl.BlockSpec(shape, lambda c: (0,) * len(shape))
    return pl.pallas_call(
        index_kernel,
        grid=(keys // CHUNK,),
        in_specs=[
            pl.BlockSpec(memory_space=pltpu.SMEM),
            whole(rows, width),
            whole(dim, keys),
            whole(rows, heads),
            whole(1, rows),
            whole(1, rows),
        ],
        out_specs=[whole(rows, keys), whole(1, rows)],
        out_shape=[
            jax.ShapeDtypeStruct((rows, keys), jnp.float32),
            jax.ShapeDtypeStruct((1, rows), jnp.float32),
        ],
        cost_estimate=pl.CostEstimate(flops=2 * rows * width * keys, bytes_accessed=2 << 20, transcendentals=rows * keys),
        name="index_forward",
    )(base, q, kt, w, start, pos)


def sum_kernel(first, info_ref, e_ref, sel_ref, m_ref, stats_ref, t_ref, lse_ref):
    c, t = pl.program_id(0), pl.program_id(1)
    _, heads, width, _ = e_ref.shape
    owners, rows, _ = t_ref.shape
    chunks = m_ref.shape[0] // heads // pl.num_programs(1)
    lanes = 128

    @pl.when(in_use(t, info_ref) & (c == 0))
    def _():
        stats = [stats_ref[i] for i in range(stats_ref.shape[0])]
        high = functools.reduce(jnp.maximum, stats)
        lse = high + jnp.log2(sum(jnp.exp2(x - high) for x in stats))
        lse_ref[t] = split_dot(lse, sel_ref[0], lambda x, y: (x, y, (((1,), (0,)), ((), ()))), 3)

    @pl.when(in_use(t, info_ref))
    def _():
        lse = lse_ref[t]
        row = t * heads * chunks + first + c
        weights = [jnp.exp2(m_ref[pl.ds(row + h * chunks, 1), :] - lse[h : h + 1]) for h in range(heads)]
        strips = []
        for r in range(width // lanes):
            at = slice(r * lanes, (r + 1) * lanes)
            total = e_ref[0, 0, at, :].astype(jnp.float32) * weights[0]
            for h in range(1, heads):
                total = total + e_ref[0, h, at, :].astype(jnp.float32) * weights[h]
            strips.append(total)
        total = jnp.concatenate(strips, axis=0)
        dense = split_dot(total, sel_ref[0], lambda x, y: (y, x, (((1,), (1,)), ((), ()))), 2)
        dense = dense.reshape(owners, rows, width)

        @pl.when(t == 0)
        def _():
            t_ref[...] = dense

        @pl.when(t > 0)
        def _():
            t_ref[...] += dense


def weighted_sum(info, e, sel, m, stats, owners, part):
    tiles, heads, keys, tile = e.shape
    queries = sel.shape[1]
    rows = queries // owners
    steps = keys // PARTS // CHUNK
    first = part * steps
    used = lambda t, info: jnp.where(in_use(t, info), t, 0)
    return pl.pallas_call(
        functools.partial(sum_kernel, first),
        grid_spec=pltpu.PrefetchScalarGridSpec(
            num_scalar_prefetch=1,
            grid=(steps, tiles),
            in_specs=[
                pl.BlockSpec((1, heads, CHUNK, tile), lambda c, t, info: (used(t, info), 0, first + c, 0)),
                pl.BlockSpec((1, queries, tile), lambda c, t, info: (used(t, info), 0, 0)),
                pl.BlockSpec(m.shape, lambda c, t, info: (0, 0)),
                pl.BlockSpec(stats.shape, lambda c, t, info: (0, 0, 0)),
            ],
            out_specs=pl.BlockSpec((owners, rows, CHUNK), lambda c, t, info: (0, 0, c)),
            scratch_shapes=[pltpu.VMEM((tiles, heads, tile), jnp.float32)],
        ),
        out_shape=jax.ShapeDtypeStruct((owners, rows, keys // PARTS), jnp.float32),
        compiler_params=pltpu.CompilerParams(vmem_limit_bytes=VMEM),
        cost_estimate=pl.CostEstimate(
            flops=2 * heads * keys * queries // PARTS, bytes_accessed=18 << 19, transcendentals=heads * queries
        ),
    )(info, e, sel, m, stats)


def back_kernel(last, place_ref, t_ref, s_ref, stats_ref, c_ref, q_ref, k_ref, kt_ref, w_ref, *refs):
    if last:
        former_ref, fk_ref, far_ref, near_ref, *gk_refs, g_ref, gkt_ref, turned_ref = refs
    else:
        gq_ref, gk_ref, g_ref, gkt_ref = refs
    i, steps = pl.program_id(0), pl.num_programs(0)
    rows, _ = g_ref.shape
    dim = kt_ref.shape[0]
    width = dim * GROUP
    index_scale = 1.0 / math.sqrt(dim)

    @pl.when(i == 0)
    def _():
        target = jnp.sum(t_ref[...], axis=0) * (1.0 / H)
        scores = s_ref[...]
        probs = jnp.exp2(scores - as_column(stats_ref[...]))
        g_ref[...] = jnp.where(scores > FLOOR, as_column(c_ref[...]) * (probs - target), 0.0)
        gkt_ref[...] = jnp.zeros_like(gkt_ref)

    g = g_ref[...]
    blocks, keys_total = [], gkt_ref[...]
    for n in range(PAIR):
        dest = far_first(i * PAIR + n, steps * PAIR, place_ref) if last else i * PAIR + n
        q = q_ref[:, pl.ds(pl.multiple_of(dest * width, width), width)]
        q = jnp.concatenate([q[:, j * dim : (j + 1) * dim] for j in range(GROUP)], axis=0)
        d = jnp.dot(q, kt_ref[...], preferred_element_type=jnp.float32)
        w = w_ref[dest]
        parts, sums = [], []
        for j in range(GROUP):
            dots = d[j * rows : (j + 1) * rows]
            kept = jnp.where(dots > 0.0, g, 0.0)
            parts.append((kept * (w[:, j : j + 1] * index_scale)).astype(jnp.bfloat16))
            sums.append(as_row(jnp.sum(kept * dots, axis=1, keepdims=True)))
        head_grad = jnp.concatenate(parts, axis=0)
        gq = jnp.dot(head_grad, k_ref[...], preferred_element_type=jnp.float32)
        pad = jnp.zeros((1, width - rows), jnp.float32)
        low = [jnp.concatenate([x * index_scale, pad], axis=1) for x in sums]
        low = jnp.concatenate([*low, jnp.zeros((8 - GROUP, width), jnp.float32)], axis=0)
        gq = jnp.concatenate([gq[j * rows : (j + 1) * rows] for j in range(GROUP)], axis=1)
        gq = jnp.concatenate([gq, low], axis=0)
        keys_total = keys_total + lax.dot_general(
            q, head_grad, (((0,), (0,)), ((), ())), preferred_element_type=jnp.float32
        )
        blocks.append(gq + former_ref[dest] if last else gq)
    gkt_ref[...] = keys_total
    if not last:
        for n in range(PAIR):
            gq_ref[n] = blocks[n]

        @pl.when(i == steps - 1)
        def _():
            gk_ref[...] = gkt_ref[...].T.reshape(gk_ref.shape)

        return

    @pl.when(i < steps // 2)
    def _():
        for n in range(PAIR):
            far_ref[n] = blocks[n]

    @pl.when(i >= steps // 2)
    def _():
        for n in range(PAIR):
            near_ref[n] = blocks[n]

    @pl.when(i == steps - 1)
    def _():
        turned_ref[...] = gkt_ref[...].T.reshape(turned_ref.shape)
        rounds, lines = len(gk_refs), turned_ref.shape[1]
        for n, ref in enumerate(gk_refs):
            for y in range(ref.shape[0]):
                owner = y * rounds + (place_ref[1] + n) % rounds
                ref[y, :lines] = fk_ref[owner]
                ref[y, lines:] = turned_ref[owner]


def far_first(i, steps, place):
    half = steps // 2
    return 2 * (i % half) + jnp.where(i < half, 1 - place[0], place[0])


def backward(place, t, s, stats, c, q, k, kt, w, part, owners, former=None):
    rows, width = q.shape
    keys, dim = k.shape
    keys = keys // PARTS
    blocks = width // (dim * GROUP)
    steps = blocks // PAIR
    last = former is not None
    whole = lambda *shape: pl.BlockSpec(shape, lambda i, place: (0,) * len(shape))
    w = jnp.moveaxis(w.reshape(rows, blocks, GROUP), 1, 0)
    block, shape = (PAIR, rows + 8, dim * GROUP), (owners, keys // owners, dim)
    array = lambda *shape: jax.ShapeDtypeStruct(shape, jnp.float32)
    in_specs = [
        whole(*t.shape),
        pl.BlockSpec((rows, keys), lambda i, place: (0, part)),
        whole(*stats.shape),
        whole(1, rows),
        whole(rows, width),
        pl.BlockSpec((keys, dim), lambda i, place: (part, 0)),
        pl.BlockSpec((dim, keys), lambda i, place: (0, part)),
        whole(*w.shape),
    ]
    args = [t, s, stats, c, q, k, kt, w]
    scratch = [pltpu.VMEM((rows, keys), jnp.float32), pltpu.VMEM((dim, keys), jnp.float32)]
    if last:
        half = steps // 2
        in_specs += [whole(*former[0].shape), whole(*shape)]
        args += former
        scratch.append(pltpu.VMEM(shape, jnp.float32))
        piece = (owners // ROUNDS, PARTS * shape[1], dim)
        out_specs = [
            pl.BlockSpec(block, lambda i, place: (jnp.minimum(i, half - 1), 0, 0)),
            pl.BlockSpec(block, lambda i, place: (jnp.maximum(i - half, 0), 0, 0)),
        ] + [whole(*piece)] * ROUNDS
        out_shape = [array(blocks // 2, *block[1:])] * 2 + [array(*piece)] * ROUNDS
    else:
        out_specs = [pl.BlockSpec(block, lambda i, place: (i, 0, 0)), whole(*shape)]
        out_shape = [array(blocks, *block[1:]), array(*shape)]
    return pl.pallas_call(
        functools.partial(back_kernel, last),
        grid_spec=pltpu.PrefetchScalarGridSpec(
            num_scalar_prefetch=1, grid=(steps,), in_specs=in_specs, out_specs=out_specs, scratch_shapes=scratch
        ),
        out_shape=out_shape,
        compiler_params=pltpu.CompilerParams(vmem_limit_bytes=VMEM),
        cost_estimate=pl.CostEstimate(
            flops=6 * rows * width * keys, bytes_accessed=4 << 20, transcendentals=rows * keys
        ),
    )(place, *args)


def half_kernel(place_ref, x_ref, own_ref, other_ref):
    mine = place_ref[2]
    total = lambda half: functools.reduce(jnp.add, [x_ref[n, half] for n in range(x_ref.shape[0])])
    own_ref[...] = total(mine)
    other_ref[...] = total(1 - mine)


def halves(place, x):
    vmem = pl.BlockSpec(memory_space=pltpu.VMEM)
    return pl.pallas_call(
        half_kernel,
        in_specs=[pl.BlockSpec(memory_space=pltpu.SMEM), vmem],
        out_specs=[vmem, vmem],
        out_shape=[jax.ShapeDtypeStruct(x.shape[2:], jnp.float32)] * 2,
        compiler_params=pltpu.CompilerParams(vmem_limit_bytes=VMEM),
        name="halves",
    )(place, x)


def end_kernel(x_ref, y_ref, gq_ref, gw_ref):
    rows = gq_ref.shape[0]
    total = x_ref[...] + y_ref[...]
    gq_ref[...] = total[:rows]
    gw_ref[...] = total[rows : rows + GROUP, :rows]


def ended(x, y):
    rows, width = x.shape
    rows -= 8
    return pl.pallas_call(
        end_kernel,
        out_shape=[
            jax.ShapeDtypeStruct((rows, width), jnp.float32),
            jax.ShapeDtypeStruct((GROUP, rows), jnp.float32),
        ],
        compiler_params=pltpu.CompilerParams(vmem_limit_bytes=VMEM),
        name="end",
    )(x, y)


def join_kernel(place_ref, *refs):
    *in_refs, out_ref = refs
    parts, _, rows, _ = out_ref.shape
    rounds = len(in_refs)
    for n, ref in enumerate(in_refs):
        for y in range(ref.shape[0]):
            for p in range(parts):
                owner = y * rounds + (place_ref[1] + rounds - n) % rounds
                out_ref[p, owner] = ref[y, p * rows : (p + 1) * rows]


def joined(place, pieces):
    count, rows, dim = pieces[0].shape
    vmem = pl.BlockSpec(memory_space=pltpu.VMEM)
    return pl.pallas_call(
        join_kernel,
        in_specs=[pl.BlockSpec(memory_space=pltpu.SMEM)] + [vmem] * len(pieces),
        out_specs=vmem,
        out_shape=jax.ShapeDtypeStruct((PARTS, count * len(pieces), rows // PARTS, dim), jnp.float32),
        compiler_params=pltpu.CompilerParams(vmem_limit_bytes=VMEM),
        name="join",
    )(place, *pieces)


def exchanged(x, axis, groups=None):
    return lax.all_to_all(x, axis, 0, 0, axis_index_groups=groups, tiled=True)


def flipped(x, axis, mask):
    return lax.ppermute(x, axis, [(i, i ^ mask) for i in range(lax.axis_size(axis))])


def joined_lse(a, b):
    high = jnp.maximum(a, b)
    return high + jnp.log2(jnp.exp2(a - high) + jnp.exp2(b - high))


def turned(x, k):
    n = lax.axis_size("head")
    return lax.ppermute(x, "head", [(i, i // ROUNDS * ROUNDS + (i + k) % ROUNDS) for i in range(n)])


def shards(q_latent, k_latent, q_index, k_index, head_weight, loss_weight, query_pos, key_start):
    keys = k_latent.shape[0]
    rows = q_index.shape[0]
    owners, peers = lax.axis_size("head"), lax.axis_size("key")
    at_key, at_head = (lax.axis_index(name).astype(jnp.int32) for name in ("key", "head"))
    base, place = (at_key * keys).reshape(1), jnp.stack([at_key % 2, at_head, at_key // 2 % 2])
    own = at_head * rows
    start, pos = key_start.reshape(1, -1), query_pos.reshape(1, -1)
    own_start = lax.dynamic_slice_in_dim(start, own, rows, axis=1)
    own_pos = lax.dynamic_slice_in_dim(pos, own, rows, axis=1)
    kt_index = k_index.T
    count = jnp.sum((key_start < base + keys) & (query_pos >= base), dtype=jnp.int32)
    info = count.reshape(1)
    e, sel, high, lse = main_forward(base, k_latent.T, jnp.swapaxes(q_latent, 1, 2), start, pos, peers)
    stats = exchanged(lse, "key")
    scores, index_lse = index_forward(base, q_index, kt_index, head_weight, own_start, own_pos)
    index_lse = joined_lse(index_lse, flipped(index_lse, "key", 1))
    moved = flipped(index_lse, "key", 2)
    index_lse = joined_lse(index_lse, moved)
    others = [lax.ppermute(index_lse, "key", [(i, (i + 4 * k) % peers) for i in range(peers)]) for k in (1, 2, 3)]
    top = functools.reduce(jnp.maximum, others, index_lse)
    index_stats = top + jnp.log2(sum(jnp.exp2(y - top) for y in [index_lse, *others]))
    targets = []
    for part in range(PARTS):
        partial = weighted_sum(info, e, sel, high, stats, owners, part)
        targets.append(exchanged(partial, "head"))

    def back(part, *former):
        fixed = (scores, index_stats, loss_weight.reshape(1, -1), q_index, k_index, kt_index, head_weight)
        return backward(place, targets[part], *fixed, part, owners, *former)

    former = back(0)
    far, near, *pieces = back(1, former)
    moved = flipped(far, "key", 1)
    groups = [list(range(c, peers, 4)) for c in range(4)]
    gq = near + moved
    gq = exchanged(gq.reshape(peers // 4, 2, *gq.shape[1:]), "key", groups)
    pieces[1:3] = [turned(pieces[k], k) for k in (1, 2)]
    pieces[3] = turned(pieces[3], 3)
    gk = sum(pieces[1:], pieces[0])
    gk = gk + flipped(gk, "head", ROUNDS)
    gk = joined(place, [gk] + [turned(gk, k) for k in range(1, ROUNDS)]).reshape(keys, -1)
    mine, other = halves(place, gq)
    other = flipped(other, "key", 2)
    gq, gw = ended(mine, other)
    return (gq, gk, gw.T)


def solution(mesh):
    return jax.shard_map(
        shards,
        mesh=mesh,
        in_specs=(
            P("head", None, None),
            P("key", None),
            P("head", None),
            P("key", None),
            P("head", None),
            P("head"),
            P(),
            P(),
        ),
        out_specs=(P("head", "key"), P("key", None), P("head", "key")),
        check_vma=False,
    )
```

```python
import functools
import math

import jax
import jax.numpy as jnp
from jax import lax
from jax.experimental import pallas as pl
from jax.experimental.pallas import tpu as pltpu
from jax.sharding import PartitionSpec as P


H = 128
QK_DIM = 192
LOG2E = 1.4426950408889634
LOW = -1e30
FLOOR = -1e29
CHUNK = 256
TILE = 256
RUN = 4
GROUP = 4
PAIR = 4
PARTS = 2
ROUNDS = 4
VMEM = 48 << 20


def eye_of(n):
    rows = lax.broadcasted_iota(jnp.int32, (n, n), 0)
    return rows == lax.broadcasted_iota(jnp.int32, (n, n), 1)


def as_column(row):
    n = row.shape[1]
    return jnp.sum(jnp.where(eye_of(n), row, jnp.zeros_like(row)), axis=1, keepdims=True)


def as_row(column):
    n = column.shape[0]
    return jnp.sum(jnp.where(eye_of(n), column, jnp.zeros_like(column)), axis=0, keepdims=True)


def split_dot(x, onehot, dims, pieces):
    total = 0.0
    for _ in range(pieces):
        high = x.astype(jnp.bfloat16)
        x = x - high.astype(jnp.float32)
        total = total + lax.dot_general(*dims(high, onehot), preferred_element_type=jnp.float32)
    return total


def in_use(t, info):
    return (t == 0) | (info[0] > t * TILE)


def main_kernel(base_ref, kt_ref, q0_ref, *refs):
    qt_refs, refs = refs[:RUN], refs[RUN:]
    start_ref, pos_ref, e_ref, sel_ref, m_ref, lse_ref, k_ref, bias_ref, part_ref, picked_ref, count_ref = refs
    step, steps = pl.program_id(0), pl.num_programs(0)
    heads = part_ref.shape[1]
    tiles = bias_ref.shape[0]
    keys, queries = k_ref.shape[0], start_ref.shape[1]
    chunks = keys // CHUNK
    scale = LOG2E / math.sqrt(QK_DIM)
    first = base_ref[0]

    def pick(t, q):
        return jnp.dot(q, sel_ref[t], preferred_element_type=jnp.float32).astype(jnp.bfloat16)

    def any_seen():
        return (start_ref[...] < first + keys) & (pos_ref[...] >= first)

    @pl.when(step == 0)
    def _():
        k_ref[...] = kt_ref[...].T
        count_ref[0] = jnp.sum(any_seen().astype(jnp.int32))

    def prepare(t):
        seen = any_seen()
        rows = lax.broadcasted_iota(jnp.int32, (queries, queries), 0)
        before = rows < lax.broadcasted_iota(jnp.int32, (queries, queries), 1)
        rank = jnp.dot(
            jnp.broadcast_to(seen.astype(jnp.float32), (8, queries)).astype(jnp.bfloat16),
            before.astype(jnp.bfloat16),
            preferred_element_type=jnp.float32,
        )[0:1]
        rank = as_column(jnp.where(seen, rank, -1.0))
        places = t * TILE + lax.broadcasted_iota(jnp.int32, (queries, TILE), 1)
        chosen = rank == places.astype(jnp.float32)
        sel_ref[t] = chosen.astype(jnp.bfloat16)
        left, right = start_ref[...].astype(jnp.float32), pos_ref[...].astype(jnp.float32) + 1.0
        left = jnp.sum(jnp.where(chosen, as_column(left), 0.0), axis=0, keepdims=True)
        right = jnp.sum(jnp.where(chosen, as_column(right), 0.0), axis=0, keepdims=True)
        s = (first + lax.broadcasted_iota(jnp.int32, (keys, TILE), 0)).astype(jnp.float32)
        bias_ref[t] = jnp.where((s >= left) & (s < right), 0.0, LOW)
        picked_ref[t, 0] = pick(t, q0_ref[0])

    def score(t, n):
        h = step * RUN + n
        qt = picked_ref[t, n % 2]
        highs, sums = [], []
        for c in range(chunks):
            here = pl.ds(c * CHUNK, CHUNK)
            s = jnp.dot(k_ref[here, :], qt, preferred_element_type=jnp.float32)
            if c == chunks - 1:
                picked_ref[t, (n + 1) % 2] = pick(t, qt_refs[n][0])
            s = s * scale + bias_ref[t, here, :]
            high = jnp.maximum(jnp.max(s, axis=0, keepdims=True), FLOOR)
            e = jnp.exp2(s - high)
            e_ref[t, n, here, :] = e.astype(jnp.bfloat16)
            highs.append(high)
            sums.append(jnp.sum(e, axis=0, keepdims=True))
            m_ref[pl.ds((t * heads + h) * chunks + c, 1), :] = high
        top = functools.reduce(jnp.maximum, highs)
        total = sum(l * jnp.exp2(m - top) for l, m in zip(sums, highs))
        part_ref[t, pl.ds(h, 1), :] = jnp.where(total > 0.0, top + jnp.log2(total), 0.0)

    def scores(t):
        for n in range(RUN):
            score(t, n)

    def send(t):
        dims = lambda x, y: (x, y, (((1,), (1,)), ((), ())))
        lse = split_dot(part_ref[t], sel_ref[t], dims, 3)
        lse = jnp.where(any_seen(), lse, FLOOR) if t == 0 else lse_ref[0] + lse
        for i in range(lse_ref.shape[0]):
            lse_ref[i] = lse

    for t in range(tiles):
        used = in_use(t, count_ref)
        pl.when(used & (step == 0))(functools.partial(prepare, t))
        pl.when(used)(functools.partial(scores, t)) if t else scores(t)
        pl.when(used & (step == steps - 1))(functools.partial(send, t))


def main_forward(base, kt, qt, start, pos, peers):
    heads, lat, queries = qt.shape
    keys = kt.shape[1]
    chunks, tiles = keys // CHUNK, queries // TILE
    whole = lambda *shape: pl.BlockSpec(shape, lambda i, info: (0,) * len(shape))
    later = lambda n, i, info: (jnp.minimum(i * RUN + n, heads - 1), 0, 0)
    return pl.pallas_call(
        main_kernel,
        grid_spec=pltpu.PrefetchScalarGridSpec(
            num_scalar_prefetch=1,
            grid=(heads // RUN,),
            in_specs=[
                whole(lat, keys),
                whole(1, lat, queries),
                *(pl.BlockSpec((1, lat, queries), functools.partial(later, n)) for n in range(1, RUN + 1)),
                whole(1, queries),
                whole(1, queries),
            ],
            out_specs=[
                pl.BlockSpec((tiles, RUN, keys, TILE), lambda i, info: (0, i, 0, 0)),
                whole(tiles, queries, TILE),
                whole(tiles * heads * chunks, TILE),
                whole(peers, heads, queries),
            ],
            scratch_shapes=[
                pltpu.VMEM((keys, lat), jnp.bfloat16),
                pltpu.VMEM((tiles, keys, TILE), jnp.float32),
                pltpu.VMEM((tiles, heads, TILE), jnp.float32),
                pltpu.VMEM((tiles, 2, lat, TILE), jnp.bfloat16),
                pltpu.SMEM((1,), jnp.int32),
            ],
        ),
        out_shape=[
            jax.ShapeDtypeStruct((tiles, heads, keys, TILE), jnp.bfloat16),
            jax.ShapeDtypeStruct((tiles, queries, TILE), jnp.bfloat16),
            jax.ShapeDtypeStruct((tiles * heads * chunks, TILE), jnp.float32),
            jax.ShapeDtypeStruct((peers, heads, queries), jnp.float32),
        ],
        cost_estimate=pl.CostEstimate(
            flops=2 * heads * keys * queries * lat, bytes_accessed=26 << 20, transcendentals=heads * keys * queries
        ),
        name="main_forward",
    )(base, kt, *([qt] * (RUN + 1)), start, pos)


def index_kernel(base_ref, q_ref, kt_ref, w_ref, start_ref, pos_ref, s_ref, lse_ref):
    c = pl.program_id(0)
    rows, width = s_ref.shape[0], CHUNK
    heads = w_ref.shape[1]
    dim = kt_ref.shape[0]
    here = pl.ds(pl.multiple_of(c * width, width), width)
    kt = kt_ref[:, here]
    total = jnp.zeros((rows, width), jnp.float32)
    for j in range(heads):
        d = jnp.dot(q_ref[:, j * dim : (j + 1) * dim], kt, preferred_element_type=jnp.float32)
        total = total + w_ref[:, j : j + 1] * jnp.maximum(d, 0.0)
    s = base_ref[0] + c * width + lax.broadcasted_iota(jnp.int32, (rows, width), 1)
    seen = (s >= as_column(start_ref[...])) & (s <= as_column(pos_ref[...]))
    s_ref[:, here] = jnp.where(seen, total * (LOG2E / math.sqrt(dim)), LOW)

    @pl.when(c == pl.num_programs(0) - 1)
    def _():
        scores = s_ref[...]
        high = jnp.maximum(jnp.max(scores, axis=1, keepdims=True), FLOOR)
        total = jnp.sum(jnp.exp2(scores - high), axis=1, keepdims=True)
        row = as_row(jnp.where(total > 0.0, high + jnp.log2(total), FLOOR))
        lse_ref[...] = row


def index_forward(base, q, kt, w, start, pos):
    rows, width = q.shape
    dim, keys = kt.shape
    heads = w.shape[1]
    whole = lambda *shape: pl.BlockSpec(shape, lambda c: (0,) * len(shape))
    return pl.pallas_call(
        index_kernel,
        grid=(keys // CHUNK,),
        in_specs=[
            pl.BlockSpec(memory_space=pltpu.SMEM),
            whole(rows, width),
            whole(dim, keys),
            whole(rows, heads),
            whole(1, rows),
            whole(1, rows),
        ],
        out_specs=[whole(rows, keys), whole(1, rows)],
        out_shape=[
            jax.ShapeDtypeStruct((rows, keys), jnp.float32),
            jax.ShapeDtypeStruct((1, rows), jnp.float32),
        ],
        cost_estimate=pl.CostEstimate(flops=2 * rows * width * keys, bytes_accessed=2 << 20, transcendentals=rows * keys),
        name="index_forward",
    )(base, q, kt, w, start, pos)


def sum_kernel(first, info_ref, e_ref, sel_ref, m_ref, stats_ref, t_ref, lse_ref):
    c, t = pl.program_id(0), pl.program_id(1)
    _, heads, width, _ = e_ref.shape
    owners, rows, _ = t_ref.shape
    chunks = m_ref.shape[0] // heads // pl.num_programs(1)
    lanes = 128

    @pl.when(in_use(t, info_ref) & (c == 0))
    def _():
        stats = [stats_ref[i] for i in range(stats_ref.shape[0])]
        high = functools.reduce(jnp.maximum, stats)
        lse = high + jnp.log2(sum(jnp.exp2(x - high) for x in stats))
        lse_ref[t] = split_dot(lse, sel_ref[0], lambda x, y: (x, y, (((1,), (0,)), ((), ()))), 3)

    @pl.when(in_use(t, info_ref))
    def _():
        lse = lse_ref[t]
        row = t * heads * chunks + first + c
        weights = [jnp.exp2(m_ref[pl.ds(row + h * chunks, 1), :] - lse[h : h + 1]) for h in range(heads)]
        strips = []
        for r in range(width // lanes):
            at = slice(r * lanes, (r + 1) * lanes)
            total = e_ref[0, 0, at, :].astype(jnp.float32) * weights[0]
            for h in range(1, heads):
                total = total + e_ref[0, h, at, :].astype(jnp.float32) * weights[h]
            strips.append(total)
        total = jnp.concatenate(strips, axis=0)
        dense = split_dot(total, sel_ref[0], lambda x, y: (y, x, (((1,), (1,)), ((), ()))), 2)
        dense = dense.reshape(owners, rows, width)

        @pl.when(t == 0)
        def _():
            t_ref[...] = dense

        @pl.when(t > 0)
        def _():
            t_ref[...] += dense


def weighted_sum(info, e, sel, m, stats, owners, part):
    tiles, heads, keys, tile = e.shape
    queries = sel.shape[1]
    rows = queries // owners
    steps = keys // PARTS // CHUNK
    first = part * steps
    used = lambda t, info: jnp.where(in_use(t, info), t, 0)
    return pl.pallas_call(
        functools.partial(sum_kernel, first),
        grid_spec=pltpu.PrefetchScalarGridSpec(
            num_scalar_prefetch=1,
            grid=(steps, tiles),
            in_specs=[
                pl.BlockSpec((1, heads, CHUNK, tile), lambda c, t, info: (used(t, info), 0, first + c, 0)),
                pl.BlockSpec((1, queries, tile), lambda c, t, info: (used(t, info), 0, 0)),
                pl.BlockSpec(m.shape, lambda c, t, info: (0, 0)),
                pl.BlockSpec(stats.shape, lambda c, t, info: (0, 0, 0)),
            ],
            out_specs=pl.BlockSpec((owners, rows, CHUNK), lambda c, t, info: (0, 0, c)),
            scratch_shapes=[pltpu.VMEM((tiles, heads, tile), jnp.float32)],
        ),
        out_shape=jax.ShapeDtypeStruct((owners, rows, keys // PARTS), jnp.float32),
        compiler_params=pltpu.CompilerParams(vmem_limit_bytes=VMEM),
        cost_estimate=pl.CostEstimate(
            flops=2 * heads * keys * queries // PARTS, bytes_accessed=18 << 19, transcendentals=heads * queries
        ),
    )(info, e, sel, m, stats)


def back_kernel(last, place_ref, t_ref, s_ref, stats_ref, c_ref, q_ref, k_ref, kt_ref, w_ref, *refs):
    if last:
        former_ref, fk_ref, far_ref, near_ref, *gk_refs, g_ref, gkt_ref, turned_ref = refs
    else:
        gq_ref, gk_ref, g_ref, gkt_ref = refs
    i, steps = pl.program_id(0), pl.num_programs(0)
    rows, _ = g_ref.shape
    dim = kt_ref.shape[0]
    width = dim * GROUP
    index_scale = 1.0 / math.sqrt(dim)

    @pl.when(i == 0)
    def _():
        target = jnp.sum(t_ref[...], axis=0) * (1.0 / H)
        scores = s_ref[...]
        probs = jnp.exp2(scores - as_column(stats_ref[...]))
        g_ref[...] = jnp.where(scores > FLOOR, as_column(c_ref[...]) * (probs - target), 0.0)
        gkt_ref[...] = jnp.zeros_like(gkt_ref)

    g = g_ref[...]
    blocks, keys_total = [], gkt_ref[...]
    for n in range(PAIR):
        dest = far_first(i * PAIR + n, steps * PAIR, place_ref)
        q = q_ref[:, pl.ds(pl.multiple_of(dest * width, width), width)]
        q = jnp.concatenate([q[:, j * dim : (j + 1) * dim] for j in range(GROUP)], axis=0)
        d = jnp.dot(q, kt_ref[...], preferred_element_type=jnp.float32)
        w = w_ref[dest]
        parts, sums = [], []
        for j in range(GROUP):
            dots = d[j * rows : (j + 1) * rows]
            kept = jnp.where(dots > 0.0, g, 0.0)
            parts.append((kept * (w[:, j : j + 1] * index_scale)).astype(jnp.bfloat16))
            sums.append(as_row(jnp.sum(kept * dots, axis=1, keepdims=True)))
        head_grad = jnp.concatenate(parts, axis=0)
        gq = jnp.dot(head_grad, k_ref[...], preferred_element_type=jnp.float32)
        pad = jnp.zeros((1, width - rows), jnp.float32)
        low = [jnp.concatenate([x * index_scale, pad], axis=1) for x in sums]
        low = jnp.concatenate([*low, jnp.zeros((8 - GROUP, width), jnp.float32)], axis=0)
        gq = jnp.concatenate([gq[j * rows : (j + 1) * rows] for j in range(GROUP)], axis=1)
        gq = jnp.concatenate([gq, low], axis=0)
        keys_total = keys_total + lax.dot_general(
            q, head_grad, (((0,), (0,)), ((), ())), preferred_element_type=jnp.float32
        )
        blocks.append(gq + former_ref[n] if last else gq)
    gkt_ref[...] = keys_total
    if not last:
        for n in range(PAIR):
            gq_ref[n] = blocks[n]

        @pl.when(i == steps - 1)
        def _():
            gk_ref[...] = gkt_ref[...].T.reshape(gk_ref.shape)

        return

    @pl.when(i < steps // 2)
    def _():
        for n in range(PAIR):
            far_ref[n] = blocks[n]

    @pl.when(i >= steps // 2)
    def _():
        for n in range(PAIR):
            near_ref[n] = blocks[n]

    @pl.when(i == steps - 1)
    def _():
        turned_ref[...] = gkt_ref[...].T.reshape(turned_ref.shape)
        rounds, lines = len(gk_refs), turned_ref.shape[1]
        for n, ref in enumerate(gk_refs):
            for y in range(ref.shape[0]):
                owner = y * rounds + (place_ref[1] + n) % rounds
                ref[y, :lines] = fk_ref[owner]
                ref[y, lines:] = turned_ref[owner]


def far_first(i, steps, place):
    half = steps // 2
    return 2 * (i % half) + jnp.where(i < half, 1 - place[0], place[0])


def backward(place, t, s, stats, c, q, k, kt, w, part, owners, former=None):
    rows, width = q.shape
    keys, dim = k.shape
    keys = keys // PARTS
    blocks = width // (dim * GROUP)
    steps = blocks // PAIR
    last = former is not None
    whole = lambda *shape: pl.BlockSpec(shape, lambda i, place: (0,) * len(shape))
    w = jnp.moveaxis(w.reshape(rows, blocks, GROUP), 1, 0)
    block, shape = (PAIR, rows + 8, dim * GROUP), (owners, keys // owners, dim)
    array = lambda *shape: jax.ShapeDtypeStruct(shape, jnp.float32)
    in_specs = [
        whole(*t.shape),
        pl.BlockSpec((rows, keys), lambda i, place: (0, part)),
        whole(*stats.shape),
        whole(1, rows),
        whole(rows, width),
        pl.BlockSpec((keys, dim), lambda i, place: (part, 0)),
        pl.BlockSpec((dim, keys), lambda i, place: (0, part)),
        whole(*w.shape),
    ]
    args = [t, s, stats, c, q, k, kt, w]
    scratch = [pltpu.VMEM((rows, keys), jnp.float32), pltpu.VMEM((dim, keys), jnp.float32)]
    if last:
        half = steps // 2
        in_specs += [pl.BlockSpec(block, lambda i, place: (i, 0, 0)), whole(*shape)]
        args += former
        scratch.append(pltpu.VMEM(shape, jnp.float32))
        piece = (owners // ROUNDS, PARTS * shape[1], dim)
        out_specs = [
            pl.BlockSpec(block, lambda i, place: (jnp.minimum(i, half - 1), 0, 0)),
            pl.BlockSpec(block, lambda i, place: (jnp.maximum(i - half, 0), 0, 0)),
        ] + [whole(*piece)] * ROUNDS
        out_shape = [array(blocks // 2, *block[1:])] * 2 + [array(*piece)] * ROUNDS
    else:
        out_specs = [pl.BlockSpec(block, lambda i, place: (i, 0, 0)), whole(*shape)]
        out_shape = [array(blocks, *block[1:]), array(*shape)]
    return pl.pallas_call(
        functools.partial(back_kernel, last),
        grid_spec=pltpu.PrefetchScalarGridSpec(
            num_scalar_prefetch=1, grid=(steps,), in_specs=in_specs, out_specs=out_specs, scratch_shapes=scratch
        ),
        out_shape=out_shape,
        compiler_params=pltpu.CompilerParams(vmem_limit_bytes=VMEM),
        cost_estimate=pl.CostEstimate(
            flops=6 * rows * width * keys, bytes_accessed=4 << 20, transcendentals=rows * keys
        ),
    )(place, *args)


def half_kernel(place_ref, x_ref, own_ref, other_ref):
    mine = place_ref[2]
    total = lambda half: functools.reduce(jnp.add, [x_ref[n, half] for n in range(x_ref.shape[0])])
    own_ref[...] = total(mine)
    other_ref[...] = total(1 - mine)


def halves(place, x):
    vmem = pl.BlockSpec(memory_space=pltpu.VMEM)
    return pl.pallas_call(
        half_kernel,
        in_specs=[pl.BlockSpec(memory_space=pltpu.SMEM), vmem],
        out_specs=[vmem, vmem],
        out_shape=[jax.ShapeDtypeStruct(x.shape[2:], jnp.float32)] * 2,
        compiler_params=pltpu.CompilerParams(vmem_limit_bytes=VMEM),
        name="halves",
    )(place, x)


def end_kernel(x_ref, y_ref, gq_ref, gw_ref):
    rows = gq_ref.shape[0]
    total = x_ref[...] + y_ref[...]
    gq_ref[...] = total[:rows]
    gw_ref[...] = total[rows : rows + GROUP, :rows]


def ended(x, y):
    rows, width = x.shape
    rows -= 8
    return pl.pallas_call(
        end_kernel,
        out_shape=[
            jax.ShapeDtypeStruct((rows, width), jnp.float32),
            jax.ShapeDtypeStruct((GROUP, rows), jnp.float32),
        ],
        compiler_params=pltpu.CompilerParams(vmem_limit_bytes=VMEM),
        name="end",
    )(x, y)


def join_kernel(place_ref, *refs):
    *in_refs, out_ref = refs
    parts, _, rows, _ = out_ref.shape
    rounds = len(in_refs)
    for n, ref in enumerate(in_refs):
        for y in range(ref.shape[0]):
            for p in range(parts):
                owner = y * rounds + (place_ref[1] + rounds - n) % rounds
                out_ref[p, owner] = ref[y, p * rows : (p + 1) * rows]


def joined(place, pieces):
    count, rows, dim = pieces[0].shape
    vmem = pl.BlockSpec(memory_space=pltpu.VMEM)
    return pl.pallas_call(
        join_kernel,
        in_specs=[pl.BlockSpec(memory_space=pltpu.SMEM)] + [vmem] * len(pieces),
        out_specs=vmem,
        out_shape=jax.ShapeDtypeStruct((PARTS, count * len(pieces), rows // PARTS, dim), jnp.float32),
        compiler_params=pltpu.CompilerParams(vmem_limit_bytes=VMEM),
        name="join",
    )(place, *pieces)


def exchanged(x, axis, groups=None):
    return lax.all_to_all(x, axis, 0, 0, axis_index_groups=groups, tiled=True)


def flipped(x, axis, mask):
    return lax.ppermute(x, axis, [(i, i ^ mask) for i in range(lax.axis_size(axis))])


def joined_lse(a, b):
    high = jnp.maximum(a, b)
    return high + jnp.log2(jnp.exp2(a - high) + jnp.exp2(b - high))


def turned(x, k):
    n = lax.axis_size("head")
    return lax.ppermute(x, "head", [(i, i // ROUNDS * ROUNDS + (i + k) % ROUNDS) for i in range(n)])


def shards(q_latent, k_latent, q_index, k_index, head_weight, loss_weight, query_pos, key_start):
    keys = k_latent.shape[0]
    rows = q_index.shape[0]
    owners, peers = lax.axis_size("head"), lax.axis_size("key")
    at_key, at_head = (lax.axis_index(name).astype(jnp.int32) for name in ("key", "head"))
    base, place = (at_key * keys).reshape(1), jnp.stack([at_key % 2, at_head, at_key // 2 % 2])
    own = at_head * rows
    start, pos = key_start.reshape(1, -1), query_pos.reshape(1, -1)
    own_start = lax.dynamic_slice_in_dim(start, own, rows, axis=1)
    own_pos = lax.dynamic_slice_in_dim(pos, own, rows, axis=1)
    kt_index = k_index.T
    count = jnp.sum((key_start < base + keys) & (query_pos >= base), dtype=jnp.int32)
    info = count.reshape(1)
    e, sel, high, lse = main_forward(base, k_latent.T, jnp.swapaxes(q_latent, 1, 2), start, pos, peers)
    stats = exchanged(lse, "key")
    scores, index_lse = index_forward(base, q_index, kt_index, head_weight, own_start, own_pos)
    index_lse = joined_lse(index_lse, flipped(index_lse, "key", 1))
    moved = flipped(index_lse, "key", 2)
    index_lse = joined_lse(index_lse, moved)
    others = [lax.ppermute(index_lse, "key", [(i, (i + 4 * k) % peers) for i in range(peers)]) for k in (1, 2, 3)]
    top = functools.reduce(jnp.maximum, others, index_lse)
    index_stats = top + jnp.log2(sum(jnp.exp2(y - top) for y in [index_lse, *others]))
    targets = []
    for part in range(PARTS):
        partial = weighted_sum(info, e, sel, high, stats, owners, part)
        targets.append(exchanged(partial, "head"))

    def back(part, *former):
        fixed = (scores, index_stats, loss_weight.reshape(1, -1), q_index, k_index, kt_index, head_weight)
        return backward(place, targets[part], *fixed, part, owners, *former)

    former = back(0)
    far, near, *pieces = back(1, former)
    moved = flipped(far, "key", 1)
    groups = [list(range(c, peers, 4)) for c in range(4)]
    gq = near + moved
    gq = exchanged(gq.reshape(peers // 4, 2, *gq.shape[1:]), "key", groups)
    pieces[1:3] = [turned(pieces[k], k) for k in (1, 2)]
    pieces[3] = turned(pieces[3], 3)
    gk = sum(pieces[1:], pieces[0])
    gk = gk + flipped(gk, "head", ROUNDS)
    gk = joined(place, [gk] + [turned(gk, k) for k in range(1, ROUNDS)]).reshape(keys, -1)
    mine, other = halves(place, gq)
    other = flipped(other, "key", 2)
    gq, gw = ended(mine, other)
    return (gq, gk, gw.T)


def solution(mesh):
    return jax.shard_map(
        shards,
        mesh=mesh,
        in_specs=(
            P("head", None, None),
            P("key", None),
            P("head", None),
            P("key", None),
            P("head", None),
            P("head"),
            P(),
            P(),
        ),
        out_specs=(P("head", "key"), P("key", None), P("head", "key")),
        check_vma=False,
    )
```

```python
import functools
import math

import jax
import jax.numpy as jnp
from jax import lax
from jax.experimental import pallas as pl
from jax.experimental.pallas import tpu as pltpu
from jax.sharding import PartitionSpec as P


H = 128
QK_DIM = 192
LOG2E = 1.4426950408889634
LOW = -1e30
FLOOR = -1e29
CHUNK = 256
TILE = 256
WIDTH = 256
RUN = 4
GROUP = 4
PAIR = 4
PARTS = 2
ROUNDS = 4
VMEM = 48 << 20


def eye_of(n):
    rows = lax.broadcasted_iota(jnp.int32, (n, n), 0)
    return rows == lax.broadcasted_iota(jnp.int32, (n, n), 1)


def as_column(row):
    n = row.shape[1]
    return jnp.sum(jnp.where(eye_of(n), row, jnp.zeros_like(row)), axis=1, keepdims=True)


def as_row(column):
    n = column.shape[0]
    return jnp.sum(jnp.where(eye_of(n), column, jnp.zeros_like(column)), axis=0, keepdims=True)


def split_dot(x, onehot, dims, pieces):
    total = 0.0
    for _ in range(pieces):
        high = x.astype(jnp.bfloat16)
        x = x - high.astype(jnp.float32)
        total = total + lax.dot_general(*dims(high, onehot), preferred_element_type=jnp.float32)
    return total


def in_use(t, info):
    return (t == 0) | (info[0] > t * TILE)


def main_kernel(base_ref, kt_ref, q0_ref, *refs):
    qt_refs, refs = refs[:RUN], refs[RUN:]
    start_ref, pos_ref, e_ref, sel_ref, m_ref, lse_ref, k_ref, bias_ref, part_ref, picked_ref, count_ref = refs
    step, steps = pl.program_id(0), pl.num_programs(0)
    heads = part_ref.shape[1]
    tiles = bias_ref.shape[0]
    keys, queries = k_ref.shape[0], start_ref.shape[1]
    chunks = keys // CHUNK
    scale = LOG2E / math.sqrt(QK_DIM)
    first = base_ref[0]

    def pick(t, q):
        return jnp.dot(q, sel_ref[t], preferred_element_type=jnp.float32).astype(jnp.bfloat16)

    def any_seen():
        return (start_ref[...] < first + keys) & (pos_ref[...] >= first)

    @pl.when(step == 0)
    def _():
        k_ref[...] = kt_ref[...].T
        count_ref[0] = jnp.sum(any_seen().astype(jnp.int32))

    def prepare(t):
        seen = any_seen()
        rows = lax.broadcasted_iota(jnp.int32, (queries, queries), 0)
        before = rows < lax.broadcasted_iota(jnp.int32, (queries, queries), 1)
        rank = jnp.dot(
            jnp.broadcast_to(seen.astype(jnp.float32), (8, queries)).astype(jnp.bfloat16),
            before.astype(jnp.bfloat16),
            preferred_element_type=jnp.float32,
        )[0:1]
        rank = as_column(jnp.where(seen, rank, -1.0))
        places = t * TILE + lax.broadcasted_iota(jnp.int32, (queries, TILE), 1)
        chosen = rank == places.astype(jnp.float32)
        sel_ref[t] = chosen.astype(jnp.bfloat16)
        left, right = start_ref[...].astype(jnp.float32), pos_ref[...].astype(jnp.float32) + 1.0
        left = jnp.sum(jnp.where(chosen, as_column(left), 0.0), axis=0, keepdims=True)
        right = jnp.sum(jnp.where(chosen, as_column(right), 0.0), axis=0, keepdims=True)
        s = (first + lax.broadcasted_iota(jnp.int32, (keys, TILE), 0)).astype(jnp.float32)
        bias_ref[t] = jnp.where((s >= left) & (s < right), 0.0, LOW)
        picked_ref[t, 0] = pick(t, q0_ref[0])

    def score(t, n):
        h = step * RUN + n
        qt = picked_ref[t, n % 2]
        highs, sums = [], []
        for c in range(chunks):
            here = pl.ds(c * CHUNK, CHUNK)
            s = jnp.dot(k_ref[here, :], qt, preferred_element_type=jnp.float32)
            if c == chunks - 1:
                picked_ref[t, (n + 1) % 2] = pick(t, qt_refs[n][0])
            s = s * scale + bias_ref[t, here, :]
            high = jnp.maximum(jnp.max(s, axis=0, keepdims=True), FLOOR)
            e = jnp.exp2(s - high)
            e_ref[t, n, here, :] = e.astype(jnp.bfloat16)
            highs.append(high)
            sums.append(jnp.sum(e, axis=0, keepdims=True))
            m_ref[pl.ds((t * heads + h) * chunks + c, 1), :] = high
        top = functools.reduce(jnp.maximum, highs)
        total = sum(l * jnp.exp2(m - top) for l, m in zip(sums, highs))
        part_ref[t, pl.ds(h, 1), :] = jnp.where(total > 0.0, top + jnp.log2(total), 0.0)

    def scores(t):
        for n in range(RUN):
            score(t, n)

    def send(t):
        dims = lambda x, y: (x, y, (((1,), (1,)), ((), ())))
        lse = split_dot(part_ref[t], sel_ref[t], dims, 3)
        lse = jnp.where(any_seen(), lse, FLOOR) if t == 0 else lse_ref[0] + lse
        for i in range(lse_ref.shape[0]):
            lse_ref[i] = lse

    for t in range(tiles):
        used = in_use(t, count_ref)
        pl.when(used & (step == 0))(functools.partial(prepare, t))
        pl.when(used)(functools.partial(scores, t)) if t else scores(t)
        pl.when(used & (step == steps - 1))(functools.partial(send, t))


def main_forward(base, kt, qt, start, pos, peers):
    heads, lat, queries = qt.shape
    keys = kt.shape[1]
    chunks, tiles = keys // CHUNK, queries // TILE
    whole = lambda *shape: pl.BlockSpec(shape, lambda i, info: (0,) * len(shape))
    later = lambda n, i, info: (jnp.minimum(i * RUN + n, heads - 1), 0, 0)
    return pl.pallas_call(
        main_kernel,
        grid_spec=pltpu.PrefetchScalarGridSpec(
            num_scalar_prefetch=1,
            grid=(heads // RUN,),
            in_specs=[
                whole(lat, keys),
                whole(1, lat, queries),
                *(pl.BlockSpec((1, lat, queries), functools.partial(later, n)) for n in range(1, RUN + 1)),
                whole(1, queries),
                whole(1, queries),
            ],
            out_specs=[
                pl.BlockSpec((tiles, RUN, keys, TILE), lambda i, info: (0, i, 0, 0)),
                whole(tiles, queries, TILE),
                whole(tiles * heads * chunks, TILE),
                whole(peers, heads, queries),
            ],
            scratch_shapes=[
                pltpu.VMEM((keys, lat), jnp.bfloat16),
                pltpu.VMEM((tiles, keys, TILE), jnp.float32),
                pltpu.VMEM((tiles, heads, TILE), jnp.float32),
                pltpu.VMEM((tiles, 2, lat, TILE), jnp.bfloat16),
                pltpu.SMEM((1,), jnp.int32),
            ],
        ),
        out_shape=[
            jax.ShapeDtypeStruct((tiles, heads, keys, TILE), jnp.bfloat16),
            jax.ShapeDtypeStruct((tiles, queries, TILE), jnp.bfloat16),
            jax.ShapeDtypeStruct((tiles * heads * chunks, TILE), jnp.float32),
            jax.ShapeDtypeStruct((peers, heads, queries), jnp.float32),
        ],
        cost_estimate=pl.CostEstimate(
            flops=2 * heads * keys * queries * lat, bytes_accessed=26 << 20, transcendentals=heads * keys * queries
        ),
        name="main_forward",
    )(base, kt, *([qt] * (RUN + 1)), start, pos)


def index_kernel(base_ref, q_ref, kt_ref, w_ref, start_ref, pos_ref, s_ref, lse_ref):
    c = pl.program_id(0)
    rows, width = s_ref.shape[0], CHUNK
    heads = w_ref.shape[1]
    dim = kt_ref.shape[0]
    here = pl.ds(pl.multiple_of(c * width, width), width)
    kt = kt_ref[:, here]
    total = jnp.zeros((rows, width), jnp.float32)
    for j in range(heads):
        d = jnp.dot(q_ref[:, j * dim : (j + 1) * dim], kt, preferred_element_type=jnp.float32)
        total = total + w_ref[:, j : j + 1] * jnp.maximum(d, 0.0)
    s = base_ref[0] + c * width + lax.broadcasted_iota(jnp.int32, (rows, width), 1)
    seen = (s >= as_column(start_ref[...])) & (s <= as_column(pos_ref[...]))
    s_ref[:, here] = jnp.where(seen, total * (LOG2E / math.sqrt(dim)), LOW)

    @pl.when(c == pl.num_programs(0) - 1)
    def _():
        scores = s_ref[...]
        high = jnp.maximum(jnp.max(scores, axis=1, keepdims=True), FLOOR)
        total = jnp.sum(jnp.exp2(scores - high), axis=1, keepdims=True)
        row = as_row(jnp.where(total > 0.0, high + jnp.log2(total), FLOOR))
        lse_ref[...] = row


def index_forward(base, q, kt, w, start, pos):
    rows, width = q.shape
    dim, keys = kt.shape
    heads = w.shape[1]
    whole = lambda *shape: pl.BlockSpec(shape, lambda c: (0,) * len(shape))
    return pl.pallas_call(
        index_kernel,
        grid=(keys // CHUNK,),
        in_specs=[
            pl.BlockSpec(memory_space=pltpu.SMEM),
            whole(rows, width),
            whole(dim, keys),
            whole(rows, heads),
            whole(1, rows),
            whole(1, rows),
        ],
        out_specs=[whole(rows, keys), whole(1, rows)],
        out_shape=[
            jax.ShapeDtypeStruct((rows, keys), jnp.float32),
            jax.ShapeDtypeStruct((1, rows), jnp.float32),
        ],
        cost_estimate=pl.CostEstimate(flops=2 * rows * width * keys, bytes_accessed=2 << 20, transcendentals=rows * keys),
        name="index_forward",
    )(base, q, kt, w, start, pos)


def sum_kernel(first, info_ref, e_ref, sel_ref, m_ref, stats_ref, t_ref, lse_ref):
    c, t = pl.program_id(0), pl.program_id(1)
    _, heads, width, _ = e_ref.shape
    owners, rows, _ = t_ref.shape
    chunks = m_ref.shape[0] // heads // pl.num_programs(1)
    lanes = 128

    @pl.when(in_use(t, info_ref) & (c == 0))
    def _():
        stats = [stats_ref[i] for i in range(stats_ref.shape[0])]
        high = functools.reduce(jnp.maximum, stats)
        lse = high + jnp.log2(sum(jnp.exp2(x - high) for x in stats))
        lse_ref[t] = split_dot(lse, sel_ref[0], lambda x, y: (x, y, (((1,), (0,)), ((), ()))), 3)

    @pl.when(in_use(t, info_ref))
    def _():
        lse = lse_ref[t]
        row = t * heads * chunks + (first + c) * width // CHUNK
        weights = [jnp.exp2(m_ref[pl.ds(row + h * chunks, 1), :] - lse[h : h + 1]) for h in range(heads)]
        strips = []
        for r in range(width // lanes):
            at = slice(r * lanes, (r + 1) * lanes)
            total = e_ref[0, 0, at, :].astype(jnp.float32) * weights[0]
            for h in range(1, heads):
                total = total + e_ref[0, h, at, :].astype(jnp.float32) * weights[h]
            strips.append(total)
        total = jnp.concatenate(strips, axis=0)
        dense = split_dot(total, sel_ref[0], lambda x, y: (y, x, (((1,), (1,)), ((), ()))), 2)
        dense = dense.reshape(owners, rows, width)

        @pl.when(t == 0)
        def _():
            t_ref[...] = dense

        @pl.when(t > 0)
        def _():
            t_ref[...] += dense


def weighted_sum(info, e, sel, m, stats, owners, part):
    tiles, heads, keys, tile = e.shape
    queries = sel.shape[1]
    rows = queries // owners
    steps = keys // PARTS // WIDTH
    first = part * steps
    used = lambda t, info: jnp.where(in_use(t, info), t, 0)
    return pl.pallas_call(
        functools.partial(sum_kernel, first),
        grid_spec=pltpu.PrefetchScalarGridSpec(
            num_scalar_prefetch=1,
            grid=(steps, tiles),
            in_specs=[
                pl.BlockSpec((1, heads, WIDTH, tile), lambda c, t, info: (used(t, info), 0, first + c, 0)),
                pl.BlockSpec((1, queries, tile), lambda c, t, info: (used(t, info), 0, 0)),
                pl.BlockSpec(m.shape, lambda c, t, info: (0, 0)),
                pl.BlockSpec(stats.shape, lambda c, t, info: (0, 0, 0)),
            ],
            out_specs=pl.BlockSpec((owners, rows, WIDTH), lambda c, t, info: (0, 0, c)),
            scratch_shapes=[pltpu.VMEM((tiles, heads, tile), jnp.float32)],
        ),
        out_shape=jax.ShapeDtypeStruct((owners, rows, keys // PARTS), jnp.float32),
        compiler_params=pltpu.CompilerParams(vmem_limit_bytes=VMEM),
        cost_estimate=pl.CostEstimate(
            flops=2 * heads * keys * queries // PARTS, bytes_accessed=18 << 19, transcendentals=heads * queries
        ),
    )(info, e, sel, m, stats)


def back_kernel(last, place_ref, t_ref, s_ref, stats_ref, c_ref, q_hbm, k_ref, kt_ref, w_ref, *refs):
    if last:
        former_ref, gk_hbm, far_ref, near_ref, *gk_refs, g_ref, gkt_ref, q_ref, q_sem, turned_ref, fk_ref, fk_sem = refs
        fk_copy = pltpu.make_async_copy(gk_hbm, fk_ref, fk_sem)
    else:
        gq_ref, gk_ref, g_ref, gkt_ref, q_ref, q_sem = refs
    q_copy = pltpu.make_async_copy(q_hbm, q_ref, q_sem)
    i, steps = pl.program_id(0), pl.num_programs(0)
    rows, _ = g_ref.shape
    dim = kt_ref.shape[0]
    width = dim * GROUP
    index_scale = 1.0 / math.sqrt(dim)

    @pl.when(i == 0)
    def _():
        q_copy.start()
        if last:
            fk_copy.start()
        target = jnp.sum(t_ref[...], axis=0) * (1.0 / H)
        scores = s_ref[...]
        probs = jnp.exp2(scores - as_column(stats_ref[...]))
        g_ref[...] = jnp.where(scores > FLOOR, as_column(c_ref[...]) * (probs - target), 0.0)
        gkt_ref[...] = jnp.zeros_like(gkt_ref)
        q_copy.wait()

    g = g_ref[...]
    blocks, keys_total = [], gkt_ref[...]
    for n in range(PAIR):
        dest = far_first(i * PAIR + n, steps * PAIR, place_ref)
        q = q_ref[:, pl.ds(pl.multiple_of(dest * width, width), width)]
        q = jnp.concatenate([q[:, j * dim : (j + 1) * dim] for j in range(GROUP)], axis=0)
        d = jnp.dot(q, kt_ref[...], preferred_element_type=jnp.float32)
        w = w_ref[dest]
        parts, sums = [], []
        for j in range(GROUP):
            dots = d[j * rows : (j + 1) * rows]
            kept = jnp.where(dots > 0.0, g, 0.0)
            parts.append((kept * (w[:, j : j + 1] * index_scale)).astype(jnp.bfloat16))
            sums.append(as_row(jnp.sum(kept * dots, axis=1, keepdims=True)))
        head_grad = jnp.concatenate(parts, axis=0)
        gq = jnp.dot(head_grad, k_ref[...], preferred_element_type=jnp.float32)
        pad = jnp.zeros((1, width - rows), jnp.float32)
        low = [jnp.concatenate([x * index_scale, pad], axis=1) for x in sums]
        low = jnp.concatenate([*low, jnp.zeros((8 - GROUP, width), jnp.float32)], axis=0)
        gq = jnp.concatenate([gq[j * rows : (j + 1) * rows] for j in range(GROUP)], axis=1)
        gq = jnp.concatenate([gq, low], axis=0)
        keys_total = keys_total + lax.dot_general(
            q, head_grad, (((0,), (0,)), ((), ())), preferred_element_type=jnp.float32
        )
        blocks.append(gq + former_ref[n] if last else gq)
    gkt_ref[...] = keys_total
    if not last:
        for n in range(PAIR):
            gq_ref[n] = blocks[n]

        @pl.when(i == steps - 1)
        def _():
            gk_ref[...] = gkt_ref[...].T.reshape(gk_ref.shape)

        return

    @pl.when(i < steps // 2)
    def _():
        for n in range(PAIR):
            far_ref[n] = blocks[n]

    @pl.when(i >= steps // 2)
    def _():
        for n in range(PAIR):
            near_ref[n] = blocks[n]

    @pl.when(i == steps - 1)
    def _():
        turned_ref[...] = gkt_ref[...].T.reshape(turned_ref.shape)
        fk_copy.wait()
        rounds, lines = len(gk_refs), turned_ref.shape[1]
        for n, ref in enumerate(gk_refs):
            for y in range(ref.shape[0]):
                owner = y * rounds + (place_ref[1] + n) % rounds
                ref[y, :lines] = fk_ref[owner]
                ref[y, lines:] = turned_ref[owner]


def far_first(i, steps, place):
    half = steps // 2
    return 2 * (i % half) + jnp.where(i < half, 1 - place[0], place[0])


def backward(place, t, s, stats, c, q, k, kt, w, part, owners, former=None):
    rows, width = q.shape
    keys, dim = k.shape
    keys = keys // PARTS
    blocks = width // (dim * GROUP)
    steps = blocks // PAIR
    last = former is not None
    whole = lambda *shape: pl.BlockSpec(shape, lambda i, place: (0,) * len(shape))
    w = jnp.moveaxis(w.reshape(rows, blocks, GROUP), 1, 0)
    block, shape = (PAIR, rows + 8, dim * GROUP), (owners, keys // owners, dim)
    array = lambda *shape: jax.ShapeDtypeStruct(shape, jnp.float32)
    in_specs = [
        whole(*t.shape),
        pl.BlockSpec((rows, keys), lambda i, place: (0, part)),
        whole(*stats.shape),
        whole(1, rows),
        pl.BlockSpec(memory_space=pltpu.HBM),
        pl.BlockSpec((keys, dim), lambda i, place: (part, 0)),
        pl.BlockSpec((dim, keys), lambda i, place: (0, part)),
        whole(*w.shape),
    ]
    args = [t, s, stats, c, q, k, kt, w]
    scratch = [
        pltpu.VMEM((rows, keys), jnp.float32),
        pltpu.VMEM((dim, keys), jnp.float32),
        pltpu.VMEM((rows, width), q.dtype),
        pltpu.SemaphoreType.DMA,
    ]
    if last:
        half = steps // 2
        in_specs += [pl.BlockSpec(block, lambda i, place: (i, 0, 0)), pl.BlockSpec(memory_space=pltpu.HBM)]
        args += former
        scratch += [pltpu.VMEM(shape, jnp.float32), pltpu.VMEM(shape, jnp.float32), pltpu.SemaphoreType.DMA]
        piece = (owners // ROUNDS, PARTS * shape[1], dim)
        out_specs = [
            pl.BlockSpec(block, lambda i, place: (jnp.minimum(i, half - 1), 0, 0)),
            pl.BlockSpec(block, lambda i, place: (jnp.maximum(i - half, 0), 0, 0)),
        ] + [whole(*piece)] * ROUNDS
        out_shape = [array(blocks // 2, *block[1:])] * 2 + [array(*piece)] * ROUNDS
    else:
        out_specs = [pl.BlockSpec(block, lambda i, place: (i, 0, 0)), whole(*shape)]
        out_shape = [array(blocks, *block[1:]), array(*shape)]
    return pl.pallas_call(
        functools.partial(back_kernel, last),
        grid_spec=pltpu.PrefetchScalarGridSpec(
            num_scalar_prefetch=1, grid=(steps,), in_specs=in_specs, out_specs=out_specs, scratch_shapes=scratch
        ),
        out_shape=out_shape,
        compiler_params=pltpu.CompilerParams(vmem_limit_bytes=56 << 20),
        cost_estimate=pl.CostEstimate(
            flops=6 * rows * width * keys, bytes_accessed=4 << 20, transcendentals=rows * keys
        ),
    )(place, *args)


def half_kernel(place_ref, x_ref, own_ref, other_ref):
    mine = place_ref[2]
    total = lambda half: functools.reduce(jnp.add, [x_ref[n, half] for n in range(x_ref.shape[0])])
    own_ref[...] = total(mine)
    other_ref[...] = total(1 - mine)


def halves(place, x):
    vmem = pl.BlockSpec(memory_space=pltpu.VMEM)
    return pl.pallas_call(
        half_kernel,
        in_specs=[pl.BlockSpec(memory_space=pltpu.SMEM), vmem],
        out_specs=[vmem, vmem],
        out_shape=[jax.ShapeDtypeStruct(x.shape[2:], jnp.float32)] * 2,
        compiler_params=pltpu.CompilerParams(vmem_limit_bytes=VMEM),
        name="halves",
    )(place, x)


def end_kernel(x_ref, y_ref, gq_ref, gw_ref):
    rows = gq_ref.shape[0]
    total = x_ref[...] + y_ref[...]
    gq_ref[...] = total[:rows]
    gw_ref[...] = total[rows : rows + GROUP, :rows]


def ended(x, y):
    rows, width = x.shape
    rows -= 8
    return pl.pallas_call(
        end_kernel,
        out_shape=[
            jax.ShapeDtypeStruct((rows, width), jnp.float32),
            jax.ShapeDtypeStruct((GROUP, rows), jnp.float32),
        ],
        compiler_params=pltpu.CompilerParams(vmem_limit_bytes=VMEM),
        name="end",
    )(x, y)


def join_kernel(place_ref, *refs):
    *in_refs, out_ref = refs
    parts, _, rows, _ = out_ref.shape
    rounds = len(in_refs)
    for n, ref in enumerate(in_refs):
        for y in range(ref.shape[0]):
            for p in range(parts):
                owner = y * rounds + (place_ref[1] + rounds - n) % rounds
                out_ref[p, owner] = ref[y, p * rows : (p + 1) * rows]


def joined(place, pieces):
    count, rows, dim = pieces[0].shape
    vmem = pl.BlockSpec(memory_space=pltpu.VMEM)
    return pl.pallas_call(
        join_kernel,
        in_specs=[pl.BlockSpec(memory_space=pltpu.SMEM)] + [vmem] * len(pieces),
        out_specs=vmem,
        out_shape=jax.ShapeDtypeStruct((PARTS, count * len(pieces), rows // PARTS, dim), jnp.float32),
        compiler_params=pltpu.CompilerParams(vmem_limit_bytes=VMEM),
        name="join",
    )(place, *pieces)


def exchanged(x, axis, groups=None):
    return lax.all_to_all(x, axis, 0, 0, axis_index_groups=groups, tiled=True)


def flipped(x, axis, mask):
    return lax.ppermute(x, axis, [(i, i ^ mask) for i in range(lax.axis_size(axis))])


def joined_lse(a, b):
    high = jnp.maximum(a, b)
    return high + jnp.log2(jnp.exp2(a - high) + jnp.exp2(b - high))


def turned(x, k):
    n = lax.axis_size("head")
    return lax.ppermute(x, "head", [(i, i // ROUNDS * ROUNDS + (i + k) % ROUNDS) for i in range(n)])


def shards(q_latent, k_latent, q_index, k_index, head_weight, loss_weight, query_pos, key_start):
    keys = k_latent.shape[0]
    rows = q_index.shape[0]
    owners, peers = lax.axis_size("head"), lax.axis_size("key")
    at_key, at_head = (lax.axis_index(name).astype(jnp.int32) for name in ("key", "head"))
    base, place = (at_key * keys).reshape(1), jnp.stack([at_key % 2, at_head, at_key // 2 % 2])
    own = at_head * rows
    start, pos = key_start.reshape(1, -1), query_pos.reshape(1, -1)
    own_start = lax.dynamic_slice_in_dim(start, own, rows, axis=1)
    own_pos = lax.dynamic_slice_in_dim(pos, own, rows, axis=1)
    kt_index = k_index.T
    count = jnp.sum((key_start < base + keys) & (query_pos >= base), dtype=jnp.int32)
    info = count.reshape(1)
    e, sel, high, lse = main_forward(base, k_latent.T, jnp.swapaxes(q_latent, 1, 2), start, pos, peers)
    stats = exchanged(lse, "key")
    scores, index_lse = index_forward(base, q_index, kt_index, head_weight, own_start, own_pos)
    index_lse = joined_lse(index_lse, flipped(index_lse, "key", 1))
    moved = flipped(index_lse, "key", 2)
    index_lse = joined_lse(index_lse, moved)
    others = [lax.ppermute(index_lse, "key", [(i, (i + 4 * k) % peers) for i in range(peers)]) for k in (1, 2, 3)]
    top = functools.reduce(jnp.maximum, others, index_lse)
    index_stats = top + jnp.log2(sum(jnp.exp2(y - top) for y in [index_lse, *others]))
    targets = []
    for part in range(PARTS):
        partial = weighted_sum(info, e, sel, high, stats, owners, part)
        targets.append(exchanged(partial, "head"))

    def back(part, *former):
        fixed = (scores, index_stats, loss_weight.reshape(1, -1), q_index, k_index, kt_index, head_weight)
        return backward(place, targets[part], *fixed, part, owners, *former)

    former = back(0)
    far, near, *pieces = back(1, former)
    moved = flipped(far, "key", 1)
    groups = [list(range(c, peers, 4)) for c in range(4)]
    gq = near + moved
    gq = exchanged(gq.reshape(peers // 4, 2, *gq.shape[1:]), "key", groups)
    pieces[1:3] = [turned(pieces[k], k) for k in (1, 2)]
    pieces[3] = turned(pieces[3], 3)
    gk = sum(pieces[1:], pieces[0])
    gk = gk + flipped(gk, "head", ROUNDS)
    gk = joined(place, [gk] + [turned(gk, k) for k in range(1, ROUNDS)]).reshape(keys, -1)
    mine, other = halves(place, gq)
    other = flipped(other, "key", 2)
    gq, gw = ended(mine, other)
    return (gq, gk, gw.T)


def solution(mesh):
    return jax.shard_map(
        shards,
        mesh=mesh,
        in_specs=(
            P("head", None, None),
            P("key", None),
            P("head", None),
            P("key", None),
            P("head", None),
            P("head"),
            P(),
            P(),
        ),
        out_specs=(P("head", "key"), P("key", None), P("head", "key")),
        check_vma=False,
    )
```

```python
import functools
import math

import jax
import jax.numpy as jnp
from jax import lax
from jax.experimental import pallas as pl
from jax.experimental.pallas import tpu as pltpu
from jax.sharding import PartitionSpec as P


H = 128
QK_DIM = 192
LOG2E = 1.4426950408889634
LOW = -1e30
FLOOR = -1e29
CHUNK = 256
STRIP = 512
TILE = 256
RUN = 4
GROUP = 4
PAIR = 8
PARTS = 2
ROUNDS = 4
VMEM = 48 << 20


def eye_of(n):
    rows = lax.broadcasted_iota(jnp.int32, (n, n), 0)
    return rows == lax.broadcasted_iota(jnp.int32, (n, n), 1)


def as_column(row):
    n = row.shape[1]
    return jnp.sum(jnp.where(eye_of(n), row, jnp.zeros_like(row)), axis=1, keepdims=True)


def as_row(column):
    n = column.shape[0]
    return jnp.sum(jnp.where(eye_of(n), column, jnp.zeros_like(column)), axis=0, keepdims=True)


def split_dot(x, onehot, dims, pieces):
    total = 0.0
    for _ in range(pieces):
        high = x.astype(jnp.bfloat16)
        x = x - high.astype(jnp.float32)
        total = total + lax.dot_general(*dims(high, onehot), preferred_element_type=jnp.float32)
    return total


def in_use(t, info):
    return (t == 0) | (info[0] > t * TILE)


def main_kernel(base_ref, kt_ref, q0_ref, *refs):
    qt_refs, refs = refs[:RUN], refs[RUN:]
    start_ref, pos_ref, e_ref, sel_ref, m_ref, lse_ref, k_ref, bias_ref, part_ref, picked_ref, count_ref = refs
    step, steps = pl.program_id(0), pl.num_programs(0)
    heads = part_ref.shape[1]
    tiles = bias_ref.shape[0]
    keys, queries = k_ref.shape[0], start_ref.shape[1]
    chunks = keys // CHUNK
    scale = LOG2E / math.sqrt(QK_DIM)
    first = base_ref[0]

    def pick(t, q):
        return jnp.dot(q, sel_ref[t], preferred_element_type=jnp.float32).astype(jnp.bfloat16)

    def any_seen():
        return (start_ref[...] < first + keys) & (pos_ref[...] >= first)

    @pl.when(step == 0)
    def _():
        k_ref[...] = kt_ref[...].T
        count_ref[0] = jnp.sum(any_seen().astype(jnp.int32))

    def prepare(t):
        seen = any_seen()
        rows = lax.broadcasted_iota(jnp.int32, (queries, queries), 0)
        before = rows < lax.broadcasted_iota(jnp.int32, (queries, queries), 1)
        rank = jnp.dot(
            jnp.broadcast_to(seen.astype(jnp.float32), (8, queries)).astype(jnp.bfloat16),
            before.astype(jnp.bfloat16),
            preferred_element_type=jnp.float32,
        )[0:1]
        rank = as_column(jnp.where(seen, rank, -1.0))
        places = t * TILE + lax.broadcasted_iota(jnp.int32, (queries, TILE), 1)
        chosen = rank == places.astype(jnp.float32)
        sel_ref[t] = chosen.astype(jnp.bfloat16)
        left, right = start_ref[...].astype(jnp.float32), pos_ref[...].astype(jnp.float32) + 1.0
        left = jnp.sum(jnp.where(chosen, as_column(left), 0.0), axis=0, keepdims=True)
        right = jnp.sum(jnp.where(chosen, as_column(right), 0.0), axis=0, keepdims=True)
        s = (first + lax.broadcasted_iota(jnp.int32, (keys, TILE), 0)).astype(jnp.float32)
        bias_ref[t] = jnp.where((s >= left) & (s < right), 0.0, LOW)
        picked_ref[t, 0] = pick(t, q0_ref[0])

    def score(t, n):
        h = step * RUN + n
        qt = picked_ref[t, n % 2]
        highs, sums = [], []
        for c in range(chunks):
            here = pl.ds(c * CHUNK, CHUNK)
            s = jnp.dot(k_ref[here, :], qt, preferred_element_type=jnp.float32)
            if c == chunks - 1:
                picked_ref[t, (n + 1) % 2] = pick(t, qt_refs[n][0])
            s = s * scale + bias_ref[t, here, :]
            high = jnp.maximum(jnp.max(s, axis=0, keepdims=True), FLOOR)
            e = jnp.exp2(s - high)
            e_ref[t, n, here, :] = e.astype(jnp.bfloat16)
            highs.append(high)
            sums.append(jnp.sum(e, axis=0, keepdims=True))
            m_ref[pl.ds((t * heads + h) * chunks + c, 1), :] = high
        top = functools.reduce(jnp.maximum, highs)
        total = sum(l * jnp.exp2(m - top) for l, m in zip(sums, highs))
        part_ref[t, pl.ds(h, 1), :] = jnp.where(total > 0.0, top + jnp.log2(total), 0.0)

    def scores(t):
        for n in range(RUN):
            score(t, n)

    def send(t):
        dims = lambda x, y: (x, y, (((1,), (1,)), ((), ())))
        lse = split_dot(part_ref[t], sel_ref[t], dims, 3)
        lse = jnp.where(any_seen(), lse, FLOOR) if t == 0 else lse_ref[0] + lse
        for i in range(lse_ref.shape[0]):
            lse_ref[i] = lse

    for t in range(tiles):
        used = in_use(t, count_ref)
        pl.when(used & (step == 0))(functools.partial(prepare, t))
        pl.when(used)(functools.partial(scores, t)) if t else scores(t)
        pl.when(used & (step == steps - 1))(functools.partial(send, t))


def main_forward(base, kt, qt, start, pos, peers):
    heads, lat, queries = qt.shape
    keys = kt.shape[1]
    chunks, tiles = keys // CHUNK, queries // TILE
    whole = lambda *shape: pl.BlockSpec(shape, lambda i, info: (0,) * len(shape))
    later = lambda n, i, info: (jnp.minimum(i * RUN + n, heads - 1), 0, 0)
    return pl.pallas_call(
        main_kernel,
        grid_spec=pltpu.PrefetchScalarGridSpec(
            num_scalar_prefetch=1,
            grid=(heads // RUN,),
            in_specs=[
                whole(lat, keys),
                whole(1, lat, queries),
                *(pl.BlockSpec((1, lat, queries), functools.partial(later, n)) for n in range(1, RUN + 1)),
                whole(1, queries),
                whole(1, queries),
            ],
            out_specs=[
                pl.BlockSpec((tiles, RUN, keys, TILE), lambda i, info: (0, i, 0, 0)),
                whole(tiles, queries, TILE),
                whole(tiles * heads * chunks, TILE),
                whole(peers, heads, queries),
            ],
            scratch_shapes=[
                pltpu.VMEM((keys, lat), jnp.bfloat16),
                pltpu.VMEM((tiles, keys, TILE), jnp.float32),
                pltpu.VMEM((tiles, heads, TILE), jnp.float32),
                pltpu.VMEM((tiles, 2, lat, TILE), jnp.bfloat16),
                pltpu.SMEM((1,), jnp.int32),
            ],
        ),
        out_shape=[
            jax.ShapeDtypeStruct((tiles, heads, keys, TILE), jnp.bfloat16),
            jax.ShapeDtypeStruct((tiles, queries, TILE), jnp.bfloat16),
            jax.ShapeDtypeStruct((tiles * heads * chunks, TILE), jnp.float32),
            jax.ShapeDtypeStruct((peers, heads, queries), jnp.float32),
        ],
        cost_estimate=pl.CostEstimate(
            flops=2 * heads * keys * queries * lat, bytes_accessed=26 << 20, transcendentals=heads * keys * queries
        ),
        name="main_forward",
    )(base, kt, *([qt] * (RUN + 1)), start, pos)


def index_kernel(base_ref, q_ref, kt_ref, w_ref, start_ref, pos_ref, s_ref, lse_ref):
    c = pl.program_id(0)
    rows, width = s_ref.shape[0], STRIP
    heads = w_ref.shape[1]
    dim = kt_ref.shape[0]
    here = pl.ds(pl.multiple_of(c * width, width), width)
    kt = kt_ref[:, here]
    total = jnp.zeros((rows, width), jnp.float32)
    for j in range(heads):
        d = jnp.dot(q_ref[:, j * dim : (j + 1) * dim], kt, preferred_element_type=jnp.float32)
        total = total + w_ref[:, j : j + 1] * jnp.maximum(d, 0.0)
    s = base_ref[0] + c * width + lax.broadcasted_iota(jnp.int32, (rows, width), 1)
    seen = (s >= as_column(start_ref[...])) & (s <= as_column(pos_ref[...]))
    s_ref[:, here] = jnp.where(seen, total * (LOG2E / math.sqrt(dim)), LOW)

    @pl.when(c == pl.num_programs(0) - 1)
    def _():
        scores = s_ref[...]
        high = jnp.maximum(jnp.max(scores, axis=1, keepdims=True), FLOOR)
        total = jnp.sum(jnp.exp2(scores - high), axis=1, keepdims=True)
        row = as_row(jnp.where(total > 0.0, high + jnp.log2(total), FLOOR))
        lse_ref[...] = row


def index_forward(base, q, kt, w, start, pos):
    rows, width = q.shape
    dim, keys = kt.shape
    heads = w.shape[1]
    whole = lambda *shape: pl.BlockSpec(shape, lambda c: (0,) * len(shape))
    return pl.pallas_call(
        index_kernel,
        grid=(keys // STRIP,),
        in_specs=[
            pl.BlockSpec(memory_space=pltpu.SMEM),
            whole(rows, width),
            whole(dim, keys),
            whole(rows, heads),
            whole(1, rows),
            whole(1, rows),
        ],
        out_specs=[whole(rows, keys), whole(1, rows)],
        out_shape=[
            jax.ShapeDtypeStruct((rows, keys), jnp.float32),
            jax.ShapeDtypeStruct((1, rows), jnp.float32),
        ],
        cost_estimate=pl.CostEstimate(flops=2 * rows * width * keys, bytes_accessed=2 << 20, transcendentals=rows * keys),
        name="index_forward",
    )(base, q, kt, w, start, pos)


def sum_kernel(first, info_ref, e_ref, sel_ref, m_ref, stats_ref, t_ref, lse_ref):
    c, t = pl.program_id(0), pl.program_id(1)
    _, heads, width, _ = e_ref.shape
    owners, rows, _ = t_ref.shape
    chunks = m_ref.shape[0] // heads // pl.num_programs(1)
    lanes = 128

    @pl.when(in_use(t, info_ref) & (c == 0))
    def _():
        stats = [stats_ref[i] for i in range(stats_ref.shape[0])]
        high = functools.reduce(jnp.maximum, stats)
        lse = high + jnp.log2(sum(jnp.exp2(x - high) for x in stats))
        lse_ref[t] = split_dot(lse, sel_ref[0], lambda x, y: (x, y, (((1,), (0,)), ((), ()))), 3)

    @pl.when(in_use(t, info_ref))
    def _():
        lse = lse_ref[t]
        row = t * heads * chunks + first + c
        weights = [jnp.exp2(m_ref[pl.ds(row + h * chunks, 1), :] - lse[h : h + 1]) for h in range(heads)]
        strips = []
        for r in range(width // lanes):
            at = slice(r * lanes, (r + 1) * lanes)
            total = e_ref[0, 0, at, :].astype(jnp.float32) * weights[0]
            for h in range(1, heads):
                total = total + e_ref[0, h, at, :].astype(jnp.float32) * weights[h]
            strips.append(total)
        total = jnp.concatenate(strips, axis=0)
        dense = split_dot(total, sel_ref[0], lambda x, y: (y, x, (((1,), (1,)), ((), ()))), 2)
        dense = dense.reshape(owners, rows, width)

        @pl.when(t == 0)
        def _():
            t_ref[...] = dense

        @pl.when(t > 0)
        def _():
            t_ref[...] += dense


def weighted_sum(info, e, sel, m, stats, owners, part):
    tiles, heads, keys, tile = e.shape
    queries = sel.shape[1]
    rows = queries // owners
    steps = keys // PARTS // CHUNK
    first = part * steps
    used = lambda t, info: jnp.where(in_use(t, info), t, 0)
    return pl.pallas_call(
        functools.partial(sum_kernel, first),
        grid_spec=pltpu.PrefetchScalarGridSpec(
            num_scalar_prefetch=1,
            grid=(steps, tiles),
            in_specs=[
                pl.BlockSpec((1, heads, CHUNK, tile), lambda c, t, info: (used(t, info), 0, first + c, 0)),
                pl.BlockSpec((1, queries, tile), lambda c, t, info: (used(t, info), 0, 0)),
                pl.BlockSpec(m.shape, lambda c, t, info: (0, 0)),
                pl.BlockSpec(stats.shape, lambda c, t, info: (0, 0, 0)),
            ],
            out_specs=pl.BlockSpec((owners, rows, CHUNK), lambda c, t, info: (0, 0, c)),
            scratch_shapes=[pltpu.VMEM((tiles, heads, tile), jnp.float32)],
        ),
        out_shape=jax.ShapeDtypeStruct((owners, rows, keys // PARTS), jnp.float32),
        compiler_params=pltpu.CompilerParams(vmem_limit_bytes=VMEM),
        cost_estimate=pl.CostEstimate(
            flops=2 * heads * keys * queries // PARTS, bytes_accessed=18 << 19, transcendentals=heads * queries
        ),
    )(info, e, sel, m, stats)


def back_kernel(last, place_ref, t_ref, s_ref, stats_ref, c_ref, q_ref, k_ref, kt_ref, w_ref, *refs):
    if last:
        former_ref, fk_ref, far_ref, near_ref, *gk_refs, g_ref, gkt_ref, turned_ref = refs
    else:
        gq_ref, gk_ref, g_ref, gkt_ref = refs
    i, steps = pl.program_id(0), pl.num_programs(0)
    rows, _ = g_ref.shape
    dim = kt_ref.shape[0]
    width = dim * GROUP
    index_scale = 1.0 / math.sqrt(dim)

    @pl.when(i == 0)
    def _():
        target = jnp.sum(t_ref[...], axis=0) * (1.0 / H)
        scores = s_ref[...]
        probs = jnp.exp2(scores - as_column(stats_ref[...]))
        g_ref[...] = jnp.where(scores > FLOOR, as_column(c_ref[...]) * (probs - target), 0.0)
        gkt_ref[...] = jnp.zeros_like(gkt_ref)

    g = g_ref[...]
    blocks, keys_total = [], gkt_ref[...]
    for n in range(PAIR):
        dest = far_first(i * PAIR + n, steps * PAIR, place_ref)
        q = q_ref[:, pl.ds(pl.multiple_of(dest * width, width), width)]
        q = jnp.concatenate([q[:, j * dim : (j + 1) * dim] for j in range(GROUP)], axis=0)
        d = jnp.dot(q, kt_ref[...], preferred_element_type=jnp.float32)
        w = w_ref[dest]
        parts, sums = [], []
        for j in range(GROUP):
            dots = d[j * rows : (j + 1) * rows]
            kept = jnp.where(dots > 0.0, g, 0.0)
            parts.append((kept * (w[:, j : j + 1] * index_scale)).astype(jnp.bfloat16))
            sums.append(as_row(jnp.sum(kept * dots, axis=1, keepdims=True)))
        head_grad = jnp.concatenate(parts, axis=0)
        gq = jnp.dot(head_grad, k_ref[...], preferred_element_type=jnp.float32)
        pad = jnp.zeros((1, width - rows), jnp.float32)
        low = [jnp.concatenate([x * index_scale, pad], axis=1) for x in sums]
        low = jnp.concatenate([*low, jnp.zeros((8 - GROUP, width), jnp.float32)], axis=0)
        gq = jnp.concatenate([gq[j * rows : (j + 1) * rows] for j in range(GROUP)], axis=1)
        gq = jnp.concatenate([gq, low], axis=0)
        keys_total = keys_total + lax.dot_general(
            q, head_grad, (((0,), (0,)), ((), ())), preferred_element_type=jnp.float32
        )
        blocks.append(gq + former_ref[n] if last else gq)
    gkt_ref[...] = keys_total
    if not last:
        for n in range(PAIR):
            gq_ref[n] = blocks[n]

        @pl.when(i == steps - 1)
        def _():
            gk_ref[...] = gkt_ref[...].T.reshape(gk_ref.shape)

        return

    @pl.when(i < steps // 2)
    def _():
        for n in range(PAIR):
            far_ref[n] = blocks[n]

    @pl.when(i >= steps // 2)
    def _():
        for n in range(PAIR):
            near_ref[n] = blocks[n]

    @pl.when(i == steps - 1)
    def _():
        turned_ref[...] = gkt_ref[...].T.reshape(turned_ref.shape)
        rounds, lines = len(gk_refs), turned_ref.shape[1]
        for n, ref in enumerate(gk_refs):
            for y in range(ref.shape[0]):
                owner = y * rounds + (place_ref[1] + n) % rounds
                ref[y, :lines] = fk_ref[owner]
                ref[y, lines:] = turned_ref[owner]


def far_first(i, steps, place):
    half = steps // 2
    return 2 * (i % half) + jnp.where(i < half, 1 - place[0], place[0])


def backward(place, t, s, stats, c, q, k, kt, w, part, owners, former=None):
    rows, width = q.shape
    keys, dim = k.shape
    keys = keys // PARTS
    blocks = width // (dim * GROUP)
    steps = blocks // PAIR
    last = former is not None
    whole = lambda *shape: pl.BlockSpec(shape, lambda i, place: (0,) * len(shape))
    w = jnp.moveaxis(w.reshape(rows, blocks, GROUP), 1, 0)
    block, shape = (PAIR, rows + 8, dim * GROUP), (owners, keys // owners, dim)
    array = lambda *shape: jax.ShapeDtypeStruct(shape, jnp.float32)
    in_specs = [
        whole(*t.shape),
        pl.BlockSpec((rows, keys), lambda i, place: (0, part)),
        whole(*stats.shape),
        whole(1, rows),
        whole(rows, width),
        pl.BlockSpec((keys, dim), lambda i, place: (part, 0)),
        pl.BlockSpec((dim, keys), lambda i, place: (0, part)),
        whole(*w.shape),
    ]
    args = [t, s, stats, c, q, k, kt, w]
    scratch = [pltpu.VMEM((rows, keys), jnp.float32), pltpu.VMEM((dim, keys), jnp.float32)]
    if last:
        half = steps // 2
        in_specs += [pl.BlockSpec(block, lambda i, place: (i, 0, 0)), whole(*shape)]
        args += former
        scratch.append(pltpu.VMEM(shape, jnp.float32))
        piece = (owners // ROUNDS, PARTS * shape[1], dim)
        out_specs = [
            pl.BlockSpec(block, lambda i, place: (jnp.minimum(i, half - 1), 0, 0)),
            pl.BlockSpec(block, lambda i, place: (jnp.maximum(i - half, 0), 0, 0)),
        ] + [whole(*piece)] * ROUNDS
        out_shape = [array(blocks // 2, *block[1:])] * 2 + [array(*piece)] * ROUNDS
    else:
        out_specs = [pl.BlockSpec(block, lambda i, place: (i, 0, 0)), whole(*shape)]
        out_shape = [array(blocks, *block[1:]), array(*shape)]
    return pl.pallas_call(
        functools.partial(back_kernel, last),
        grid_spec=pltpu.PrefetchScalarGridSpec(
            num_scalar_prefetch=1, grid=(steps,), in_specs=in_specs, out_specs=out_specs, scratch_shapes=scratch
        ),
        out_shape=out_shape,
        compiler_params=pltpu.CompilerParams(vmem_limit_bytes=VMEM),
        cost_estimate=pl.CostEstimate(
            flops=6 * rows * width * keys, bytes_accessed=4 << 20, transcendentals=rows * keys
        ),
    )(place, *args)


def half_kernel(place_ref, x_ref, own_ref, other_ref):
    mine = place_ref[2]
    total = lambda half: functools.reduce(jnp.add, [x_ref[n, half] for n in range(x_ref.shape[0])])
    own_ref[...] = total(mine)
    other_ref[...] = total(1 - mine)


def halves(place, x):
    vmem = pl.BlockSpec(memory_space=pltpu.VMEM)
    return pl.pallas_call(
        half_kernel,
        in_specs=[pl.BlockSpec(memory_space=pltpu.SMEM), vmem],
        out_specs=[vmem, vmem],
        out_shape=[jax.ShapeDtypeStruct(x.shape[2:], jnp.float32)] * 2,
        compiler_params=pltpu.CompilerParams(vmem_limit_bytes=VMEM),
        name="halves",
    )(place, x)


def end_kernel(x_ref, y_ref, gq_ref, gw_ref):
    rows = gq_ref.shape[0]
    total = x_ref[...] + y_ref[...]
    gq_ref[...] = total[:rows]
    gw_ref[...] = total[rows : rows + GROUP, :rows]


def ended(x, y):
    rows, width = x.shape
    rows -= 8
    return pl.pallas_call(
        end_kernel,
        out_shape=[
            jax.ShapeDtypeStruct((rows, width), jnp.float32),
            jax.ShapeDtypeStruct((GROUP, rows), jnp.float32),
        ],
        compiler_params=pltpu.CompilerParams(vmem_limit_bytes=VMEM),
        name="end",
    )(x, y)


def join_kernel(place_ref, *refs):
    *in_refs, out_ref = refs
    parts, _, rows, _ = out_ref.shape
    rounds = len(in_refs)
    for n, ref in enumerate(in_refs):
        for y in range(ref.shape[0]):
            for p in range(parts):
                owner = y * rounds + (place_ref[1] + rounds - n) % rounds
                out_ref[p, owner] = ref[y, p * rows : (p + 1) * rows]


def joined(place, pieces):
    count, rows, dim = pieces[0].shape
    vmem = pl.BlockSpec(memory_space=pltpu.VMEM)
    return pl.pallas_call(
        join_kernel,
        in_specs=[pl.BlockSpec(memory_space=pltpu.SMEM)] + [vmem] * len(pieces),
        out_specs=vmem,
        out_shape=jax.ShapeDtypeStruct((PARTS, count * len(pieces), rows // PARTS, dim), jnp.float32),
        compiler_params=pltpu.CompilerParams(vmem_limit_bytes=VMEM),
        name="join",
    )(place, *pieces)


def exchanged(x, axis, groups=None):
    return lax.all_to_all(x, axis, 0, 0, axis_index_groups=groups, tiled=True)


def flipped(x, axis, mask):
    return lax.ppermute(x, axis, [(i, i ^ mask) for i in range(lax.axis_size(axis))])


def joined_lse(a, b):
    high = jnp.maximum(a, b)
    return high + jnp.log2(jnp.exp2(a - high) + jnp.exp2(b - high))


def turned(x, k):
    n = lax.axis_size("head")
    return lax.ppermute(x, "head", [(i, i // ROUNDS * ROUNDS + (i + k) % ROUNDS) for i in range(n)])


def shards(q_latent, k_latent, q_index, k_index, head_weight, loss_weight, query_pos, key_start):
    keys = k_latent.shape[0]
    rows = q_index.shape[0]
    owners, peers = lax.axis_size("head"), lax.axis_size("key")
    at_key, at_head = (lax.axis_index(name).astype(jnp.int32) for name in ("key", "head"))
    base, place = (at_key * keys).reshape(1), jnp.stack([at_key % 2, at_head, at_key // 2 % 2])
    own = at_head * rows
    start, pos = key_start.reshape(1, -1), query_pos.reshape(1, -1)
    own_start = lax.dynamic_slice_in_dim(start, own, rows, axis=1)
    own_pos = lax.dynamic_slice_in_dim(pos, own, rows, axis=1)
    kt_index = k_index.T
    count = jnp.sum((key_start < base + keys) & (query_pos >= base), dtype=jnp.int32)
    info = count.reshape(1)
    e, sel, high, lse = main_forward(base, k_latent.T, jnp.swapaxes(q_latent, 1, 2), start, pos, peers)
    stats = exchanged(lse, "key")
    scores, index_lse = index_forward(base, q_index, kt_index, head_weight, own_start, own_pos)
    index_lse = joined_lse(index_lse, flipped(index_lse, "key", 1))
    moved = flipped(index_lse, "key", 2)
    index_lse = joined_lse(index_lse, moved)
    others = [lax.ppermute(index_lse, "key", [(i, (i + 4 * k) % peers) for i in range(peers)]) for k in (1, 2, 3)]
    top = functools.reduce(jnp.maximum, others, index_lse)
    index_stats = top + jnp.log2(sum(jnp.exp2(y - top) for y in [index_lse, *others]))
    targets = []
    for part in range(PARTS):
        partial = weighted_sum(info, e, sel, high, stats, owners, part)
        targets.append(exchanged(partial, "head"))

    def back(part, *former):
        fixed = (scores, index_stats, loss_weight.reshape(1, -1), q_index, k_index, kt_index, head_weight)
        return backward(place, targets[part], *fixed, part, owners, *former)

    former = back(0)
    far, near, *pieces = back(1, former)
    moved = flipped(far, "key", 1)
    groups = [list(range(c, peers, 4)) for c in range(4)]
    gq = near + moved
    gq = exchanged(gq.reshape(peers // 4, 2, *gq.shape[1:]), "key", groups)
    pieces[1:3] = [turned(pieces[k], k) for k in (1, 2)]
    pieces[3] = turned(pieces[3], 3)
    gk = sum(pieces[1:], pieces[0])
    gk = gk + flipped(gk, "head", ROUNDS)
    gk = joined(place, [gk] + [turned(gk, k) for k in range(1, ROUNDS)]).reshape(keys, -1)
    mine, other = halves(place, gq)
    other = flipped(other, "key", 2)
    gq, gw = ended(mine, other)
    return (gq, gk, gw.T)


def solution(mesh):
    return jax.shard_map(
        shards,
        mesh=mesh,
        in_specs=(
            P("head", None, None),
            P("key", None),
            P("head", None),
            P("key", None),
            P("head", None),
            P("head"),
            P(),
            P(),
        ),
        out_specs=(P("head", "key"), P("key", None), P("head", "key")),
        check_vma=False,
    )
```
